256 devices in a mesh: seq: 32 (over x, z), head: 8 (over y, core).
Axes of the slice: x: 4, y: 4, z: 8, core: 2. Of those that a mesh axis runs over, the one named last changes fastest.
Arguments:
- query_in: bfloat16 [8192, 8192], P('seq', 'head'), may hold values from -1.796875 to 1.796875
- key_in: bfloat16 [8192, 8192], P('seq', 'head'), may hold values from -1.796875 to 1.796875
- value_in: bfloat16 [8192, 8192], P('seq', 'head'), may hold values from -11 to 11
- log_decay: float32 [8192, 64], P('seq', 'head'), may hold values from -1 to 0, as said below
- norm_gain: float32 [8192], P('head'), may hold values from 0.5 to 1.5
- prompt_lengths: int32 [4], replicated, may hold values from 1 to 6144, 8192 in all
- step_query: bfloat16 [4, 512, 8192], P(None, 'seq', 'head'), may hold values from -1.796875 to 1.796875
- step_key: bfloat16 [4, 512, 8192], P(None, 'seq', 'head'), may hold values from -1.796875 to 1.796875
- step_value: bfloat16 [4, 512, 8192], P(None, 'seq', 'head'), may hold values from -6 to 6
- step_decay: float32 [4, 512, 64], P(None, 'seq', 'head'), may hold values from -0.3 to -0.01
- row_prompt: int32 [512], P('seq'), may hold values from 0 to 3
Outputs:
- attn_out: bfloat16 [8192, 8192], P('seq', 'head')
- decode_out: bfloat16 [4, 512, 8192], P(None, 'seq', 'head')
The draws below stay inside these ranges and needn't reach their ends.
Inputs may be any that keep to these rules, and one draw needn't show every extreme that they name: `log_decay`: Negative; per head and token.
All inputs are finite; a program needn't handle non-finite values.
Results may differ from the reference program's by a relative error of at most 0.0056.
Values sent between devices are 32-bit elements; how exact they have to be, the bound alone decides.
No kernel may reach another device: no remote copies, remote signals or barrier semaphores. Data moves between devices by JAX's collectives and lax.ppermute only.
A program may use at most 64 MiB of HBM per device.

```python
import math
import jax
import jax.numpy as jnp
import numpy as np
from jax import lax

HEAD_COUNT = 64
HDIM = 128
TOK_DEV = 256
BLOCK = 256
PROMPTS = 4
STEPS = 4
PROMPT_TOKENS = 8192
ROWS = 512


def draw_log_decay(key, part):
    fragments = jax.random.split(jax.random.fold_in(key, 11), 7)
    order = jax.random.permutation(fragments[0], HEAD_COUNT)
    fast = order < HEAD_COUNT // 2
    slow_rate = jnp.exp(jax.random.uniform(fragments[1], (HEAD_COUNT,), jnp.float32, jnp.log(0.2), jnp.log(1.0))) / PROMPT_TOKENS
    fast_rate = jnp.exp(jax.random.uniform(fragments[2], (HEAD_COUNT,), jnp.float32, jnp.log(1.0 / 50.0), jnp.log(1.0 / 30.0)))
    decay_rate = jnp.where(fast, fast_rate, slow_rate)
    spans = PROMPT_TOKENS // TOK_DEV
    device_multiplier = jnp.exp(jax.random.uniform(fragments[3], (spans, HEAD_COUNT), jnp.float32, -0.7, 0.7))
    device_multiplier = jnp.repeat(device_multiplier, TOK_DEV, axis=0)
    coarse_estimate = jax.random.uniform(fragments[4], (PROMPT_TOKENS, HEAD_COUNT), jnp.float32, 0.5, 1.5)
    spike_positions = jax.random.randint(fragments[5], (4,), 0, PROMPT_TOKENS)
    marked_rows = jnp.any(jnp.arange(PROMPT_TOKENS)[:, None] == spike_positions[None, :], axis=1)
    spike_group = jnp.log(jax.random.uniform(fragments[6], (PROMPT_TOKENS, HEAD_COUNT), jnp.float32, 0.5, 0.8))
    return (-decay_rate[None, :] * device_multiplier * coarse_estimate + jnp.where(marked_rows[:, None], spike_group, 0.0)).astype(jnp.float32)


def draw_value_in(key, part):
    fragments = jax.random.split(jax.random.fold_in(key, 23), 1)
    head_of = (jnp.arange(HEAD_COUNT * HDIM) // HDIM).astype(jnp.float32)
    scale = 0.5 * 3.0 ** (head_of / max(HEAD_COUNT - 1, 1))
    base = jnp.clip(jax.random.normal(fragments[0], (PROMPT_TOKENS, HEAD_COUNT * HDIM), jnp.float32), -4.0, 4.0)
    return (base * scale[None, :]).astype(jnp.bfloat16)


def place_ends(result, own_key, least, top_value):
    longest = result.shape.index(max(result.shape))
    spots = []
    for shift in (0, 1):
        where = [jax.random.randint(jax.random.fold_in(own_key, axis), (), 0, length) for axis, length in enumerate(result.shape)]
        where[longest] = (where[longest] + shift) % result.shape[longest]
        spots.append(tuple(where))
    return result.at[spots[0]].set(least).at[spots[1]].set(top_value)


def shard_levels(stream_key, dims, pieces, low, top_value):
    level = 1.0
    for position, parts in pieces:
        heights = jax.random.uniform(jax.random.fold_in(jax.random.fold_in(stream_key, 6), position), (parts,), jnp.float32, low / len(pieces), top_value / len(pieces))
        level = level * jnp.repeat(jnp.exp(heights), dims[position] // parts).reshape((-1,) + (1,) * (len(dims) - 1 - position))
    return level


def split_up(count, total, limit, lean):
    portions = [(1 << 20) // math.isqrt(grade ** lean) + 1 for grade in range(2, count + 1)]
    spare, counts = total - limit - (count - 1), [1] * (count - 1)
    while spare > 0:
        candidates = [i for i in range(count - 1) if counts[i] < limit]
        mass, remaining = sum([portions[i] for i in candidates]), spare
        for i in candidates:
            more = min(limit - counts[i], max(1, remaining * portions[i] // mass), spare)
            counts[i] = counts[i] + more
            spare = spare - more
    return np.array([limit] + counts)


def ragged_sizes(own_key, count, total, bound, lean):
    if count == 2:
        one = jax.random.randint(own_key, (), max(1, total - bound), min(bound, total - 1) + 1)
        return jnp.stack([one, total - one])
    sizes = jnp.asarray(split_up(count, total, bound, lean), jnp.int32)
    pairs = (count - 1) // 2
    giver, sink = sizes[1:1 + 2 * pairs:2], sizes[2:2 + 2 * pairs:2]
    margin = jnp.minimum(giver - 1, bound - sink)
    moved = jax.random.randint(jax.random.fold_in(own_key, 1), (pairs,), 0, 1 << 20) % (margin + 1)
    sizes = sizes.at[1:1 + 2 * pairs:2].set(giver - moved).at[2:2 + 2 * pairs:2].set(sink + moved)
    return sizes[jax.random.permutation(jax.random.fold_in(own_key, 2), count)]


def gaussian(rng, dims, scale, most, pieces=(), kind=jnp.bfloat16):
    values = scale * jax.random.normal(rng, dims, jnp.float32)
    if pieces:
        values = values * shard_levels(rng, dims, pieces, -0.22, 0.18)
    return jnp.clip(values, -most, most).astype(kind)


def setup_inputs(seed: int = 0) -> dict:
    streams_of = jax.random.split(jax.random.key(seed), 12)
    return {
        "query_in": gaussian(streams_of[0], (PROMPT_TOKENS, HEAD_COUNT * HDIM), 0.3, 1.796875, ((0, 32), (1, 8))),
        "key_in": gaussian(streams_of[1], (PROMPT_TOKENS, HEAD_COUNT * HDIM), 0.3, 1.796875, ((0, 32), (1, 8))),
        "value_in": draw_value_in(jax.random.fold_in(streams_of[11], 71), 0),
        "log_decay": draw_log_decay(jax.random.fold_in(streams_of[11], 71), 0),
        "norm_gain": jnp.clip(1.0 + 0.1 * jax.random.normal(streams_of[4], (HEAD_COUNT * HDIM,), jnp.float32), 0.5, 1.5),
        "prompt_lengths": ragged_sizes(streams_of[5], PROMPTS, PROMPT_TOKENS, PROMPT_TOKENS * 3 // 4, 2).astype(jnp.int32),
        "step_query": gaussian(streams_of[6], (STEPS, ROWS, HEAD_COUNT * HDIM), 0.3, 1.796875, ((1, 32), (2, 8))),
        "step_key": gaussian(streams_of[7], (STEPS, ROWS, HEAD_COUNT * HDIM), 0.3, 1.796875, ((1, 32), (2, 8))),
        "step_value": gaussian(streams_of[8], (STEPS, ROWS, HEAD_COUNT * HDIM), 1.0, 6.0, ((1, 32), (2, 8))),
        "step_decay": jnp.clip(-0.3 + 0.29000001 * jax.random.uniform(streams_of[9], (STEPS, ROWS, HEAD_COUNT), jnp.float32) ** shard_levels(streams_of[9], (STEPS, ROWS, HEAD_COUNT), ((1, 32), (2, 8)), -0.2, 0.2), -0.3, -0.01),
        "row_prompt": place_ends(jax.random.randint(streams_of[10], (ROWS,), 0, PROMPTS), jax.random.fold_in(streams_of[10], 1), 0, PROMPTS - 1).astype(jnp.int32),
    }


EPSILON = 1e-06

def segment_ids(prompt_lengths, positions):
    boundary = jnp.cumsum(prompt_lengths).astype(jnp.int32)
    return lax.optimization_barrier(jnp.sum((positions[:, None] >= boundary[None, :]).astype(jnp.int32), axis=1)).astype(jnp.int32)

def half_round(array):
    return lax.optimization_barrier(array.astype(jnp.bfloat16)).astype(jnp.float32)

def block_pass(query_blk, key_blk, value_blk, decay_blk, seg_blk, seg_front, state):
    cumul = jnp.cumsum(decay_blk, axis=0)
    length = seg_blk.shape[0]
    causal = jnp.arange(length)[:, None] >= jnp.arange(length)[None, :]
    linked = causal & (seg_blk[:, None] == seg_blk[None, :])
    spread = cumul[:, None, :] - cumul[None, :, :]
    factor = jnp.where(linked[:, :, None], jnp.exp(jnp.where(linked[:, :, None], spread, 0.0)), 0.0)
    query_f = query_blk.astype(jnp.float32)
    key_f = key_blk.astype(jnp.float32)
    value_f = value_blk.astype(jnp.float32)
    scores = jnp.einsum('thd,shd->hts', query_f, key_f)
    weights = half_round(scores * jnp.transpose(factor, (2, 0, 1)))
    inner = jnp.einsum('hts,shd->thd', weights, value_f)
    carried = jnp.exp(cumul) * (seg_blk == seg_front).astype(jnp.float32)[:, None]
    state_half = half_round(state)
    outer = jnp.einsum('thd,hde->the', query_f, state_half) * carried[:, :, None]
    keep = jnp.exp(cumul[-1:] - cumul) * (seg_blk == seg_blk[-1]).astype(jnp.float32)[:, None]
    keyed = half_round(key_f * keep[:, :, None])
    update = jnp.einsum('shd,she->hde', keyed, value_f)
    onward = jnp.exp(cumul[-1]) * (seg_blk[-1] == seg_front).astype(jnp.float32)
    new_state = onward[:, None, None] * state + update
    return (inner + outer, new_state)

def reference(query_in, key_in, value_in, log_decay, norm_gain, prompt_lengths, step_query, step_key, step_value, step_decay, row_prompt):
    nblocks = PROMPT_TOKENS // BLOCK
    positions = jnp.arange(PROMPT_TOKENS, dtype=jnp.int32)
    segs = segment_ids(prompt_lengths, positions)
    seg_prior = jnp.concatenate([jnp.full((1,), -1, jnp.int32), segs[:-1]]).astype(jnp.int32)
    shape4 = (nblocks, BLOCK, HEAD_COUNT, HDIM)
    inputs = (query_in.reshape(shape4), key_in.reshape(shape4), value_in.reshape(shape4), log_decay.reshape(nblocks, BLOCK, HEAD_COUNT), segs.reshape(nblocks, BLOCK), seg_prior.reshape(nblocks, BLOCK)[:, 0])

    def stepper(state, fragments):
        mixed_blk, new_state = block_pass(fragments[0], fragments[1], fragments[2], fragments[3], fragments[4], fragments[5], state)
        return (new_state, (mixed_blk, state))
    initial = jnp.zeros((HEAD_COUNT, HDIM, HDIM), jnp.float32)
    final_state, (mixed_all, starts) = lax.scan(stepper, initial, inputs)
    mixed = mixed_all.reshape(PROMPT_TOKENS, HEAD_COUNT * HDIM)
    scale = lax.rsqrt(lax.optimization_barrier(jnp.sum(mixed * mixed, axis=1)) / (HEAD_COUNT * HDIM) + EPSILON)
    attn_out = (mixed * scale[:, None] * norm_gain[None, :]).astype(jnp.bfloat16)
    boundary = jnp.cumsum(prompt_lengths).astype(jnp.int32)

    def prompt_end(prompt):
        last_tok = (boundary[prompt] - 1).astype(jnp.int32)
        blk_index = (last_tok // BLOCK).astype(jnp.int32)
        offset = (last_tok - blk_index * BLOCK).astype(jnp.int32)
        begin = (blk_index * BLOCK).astype(jnp.int32)
        key_blk = lax.dynamic_slice_in_dim(key_in, begin, BLOCK, 0).reshape(BLOCK, HEAD_COUNT, HDIM).astype(jnp.float32)
        value_blk = lax.dynamic_slice_in_dim(value_in, begin, BLOCK, 0).reshape(BLOCK, HEAD_COUNT, HDIM).astype(jnp.float32)
        decay_blk = lax.dynamic_slice_in_dim(log_decay, begin, BLOCK, 0)
        seg_blk = lax.dynamic_slice_in_dim(segs, begin, BLOCK, 0)
        seg_front = seg_prior[begin]
        cumul = jnp.cumsum(decay_blk, axis=0)
        reached = cumul[offset]
        taken = (jnp.arange(BLOCK) <= offset) & (seg_blk == prompt)
        keep_end = jnp.exp(jnp.where(taken[:, None], reached[None, :] - cumul, 0.0)) * taken.astype(jnp.float32)[:, None]
        tailed = half_round(key_blk * keep_end[:, :, None])
        part = jnp.einsum('shd,she->hde', tailed, value_blk)
        lead = jnp.exp(reached) * (seg_front == prompt).astype(jnp.float32)
        return lead[:, None, None] * starts[blk_index] + part
    prompt_state = lax.map(prompt_end, jnp.arange(PROMPTS, dtype=jnp.int32))

    def decode_row(fragments):
        prompt, queries, keyset, valueset, decays = fragments
        row_state = prompt_state[prompt]
        results = []
        for section in range(STEPS):
            query_now = queries[section].astype(jnp.float32).reshape(HEAD_COUNT, HDIM)
            key_now = keyset[section].astype(jnp.float32).reshape(HEAD_COUNT, HDIM)
            value_now = valueset[section].astype(jnp.float32).reshape(HEAD_COUNT, HDIM)
            row_state = jnp.exp(decays[section])[:, None, None] * row_state + key_now[:, :, None] * value_now[:, None, :]
            results.append(jnp.einsum('hd,hde->he', query_now, row_state, precision=lax.Precision.HIGHEST).reshape(HEAD_COUNT * HDIM))
        return jnp.stack(results)
    decoded = lax.map(decode_row, (row_prompt, jnp.transpose(step_query, (1, 0, 2)), jnp.transpose(step_key, (1, 0, 2)), jnp.transpose(step_value, (1, 0, 2)), jnp.transpose(step_decay, (1, 0, 2))))
    decoded = jnp.transpose(decoded, (1, 0, 2))
    step_scale = lax.rsqrt(lax.optimization_barrier(jnp.sum(decoded * decoded, axis=2)) / (HEAD_COUNT * HDIM) + EPSILON)
    decode_out = (decoded * step_scale[:, :, None] * norm_gain[None, None, :]).astype(jnp.bfloat16)
    return (attn_out, decode_out)
```

```python
import functools

import jax
import jax.numpy as jnp
from jax import lax
from jax.experimental import pallas as pl
from jax.experimental.pallas import tpu as pltpu
from jax.sharding import Mesh
from jax.sharding import PartitionSpec as P

HEAD_COUNT = 64
HDIM = 128
BLOCK = 256
PROMPTS = 4
STEPS = 4
SEQ = ("seq_0", "seq_1")
EPSILON = 1e-06

NX = 4
HEADS = 8
NDEV = NX * HEADS
QUART = HDIM // NX
ROWS_DEV = 16

U0, T0, Q0, S0, MSG = 0, 32, 64, 80, 88

BF = jnp.bfloat16
F32 = jnp.float32
HI = lax.Precision.HIGHEST

SMEM = pl.BlockSpec(memory_space=pltpu.SMEM)
VMEM = pl.BlockSpec(memory_space=pltpu.VMEM)


def params(mib=48):
    return pltpu.CompilerParams(vmem_limit_bytes=mib << 20)


def cost(us):
    return pl.CostEstimate(flops=int(us * 1e9), bytes_accessed=int(us * 3e6), transcendentals=0)


def bounds(lens):
    ends = []
    total = lens[0]
    for p in range(PROMPTS):
        if p:
            total = total + lens[p]
        ends.append(total)
    return ends


def seg_of(pos, ends):
    out = (pos >= ends[0]).astype(jnp.int32)
    for p in range(1, PROMPTS):
        out = out + (pos >= ends[p]).astype(jnp.int32)
    return out


def entry_seg(first, ends):
    return jnp.where(first > 0, seg_of(first - 1, ends), -1)


def cum_columns(logd):
    t = lax.broadcasted_iota(jnp.int32, (BLOCK, BLOCK), 0)
    s = lax.broadcasted_iota(jnp.int32, (BLOCK, BLOCK), 1)
    tri = (s <= t).astype(F32)
    return jnp.dot(tri, logd, precision=HI, preferred_element_type=F32)


def contract_rows(a, b):
    return lax.dot_general(a, b, (((0,), (0,)), ((), ())), preferred_element_type=F32)


def contract_cols(a, b):
    return lax.dot_general(a, b, (((1,), (1,)), ((), ())), preferred_element_type=F32)


def send_kernel(lens, here, rows, key_ref, value_ref, logd_ref, query_ref, out_ref, cum_ref):
    first = here[0] * BLOCK
    ends = bounds(lens)
    front = entry_seg(first, ends)
    seg_last = seg_of(first + (BLOCK - 1), ends)
    cum = cum_columns(logd_ref[...])
    cum_ref[...] = cum
    tok = lax.broadcasted_iota(jnp.int32, (BLOCK, HEADS), 0)
    seg = seg_of(tok + first, ends)
    last = cum[BLOCK - 1 : BLOCK, :]
    keep = jnp.where(seg == seg_last, jnp.exp(last - cum), 0.0)
    growth = jnp.exp(last) * (seg_last == front).astype(F32)
    leads = []
    found = jnp.int32(-1)
    spot = jnp.int32(0)
    for p in range(PROMPTS):
        local = ends[p] - 1 - first
        inside = (local >= 0) & (local < BLOCK)
        safe = jnp.clip(local, 0, BLOCK - 1)
        reached = cum_ref[pl.ds(safe, 1), :]
        leads.append(jnp.exp(reached) * (inside & (front == p)).astype(F32))
        interior = (local >= 0) & (local < BLOCK - 1)
        take = interior & (found < 0)
        found = jnp.where(take, p, found)
        spot = jnp.where(take, local, spot)
    lane = lax.broadcasted_iota(jnp.int32, (1, HDIM), 1)
    ids = jnp.zeros((1, HDIM), F32)
    for r in range(ROWS_DEV):
        ids = jnp.where(lane == r, rows[r].astype(F32), ids)

    for h in range(HEADS):
        cols = slice(h * HDIM, (h + 1) * HDIM)
        keyed = (key_ref[:, cols].astype(F32) * keep[:, h : h + 1]).astype(BF)
        update = contract_rows(keyed, value_ref[:, cols])
        scal = jnp.concatenate(
            [jnp.broadcast_to(growth[:, h : h + 1], (1, HDIM))]
            + [jnp.broadcast_to(leads[p][:, h : h + 1], (1, HDIM)) for p in range(PROMPTS)]
            + [ids, ids, ids],
            axis=0,
        )
        for x in range(NX):
            out_ref[x * HEADS + h, U0:T0, :] = update[x * QUART : (x + 1) * QUART, :]
            out_ref[x * HEADS + h, Q0:S0, :] = query_ref[x, :, cols].astype(F32)
            out_ref[x * HEADS + h, S0:MSG, :] = scal

    @pl.when(found < 0)
    def _():
        out_ref[:, T0:Q0, :] = jnp.zeros((NDEV, QUART, HDIM), F32)

    @pl.when(found >= 0)
    def _():
        reached = cum_ref[pl.ds(spot, 1), :]
        taken = (tok <= spot) & (seg == found)
        tail = jnp.where(taken, jnp.exp(jnp.where(taken, reached - cum, 0.0)), 0.0)
        for h in range(HEADS):
            cols = slice(h * HDIM, (h + 1) * HDIM)
            tailed = (key_ref[:, cols].astype(F32) * tail[:, h : h + 1]).astype(BF)
            part = contract_rows(tailed, value_ref[:, cols])
            for x in range(NX):
                out_ref[x * HEADS + h, T0:Q0, :] = part[x * QUART : (x + 1) * QUART, :]


def intra_kernel(
    lens, here, query_ref, key_ref, value_ref, logd_ref, sq_ref, sk_ref, sv_ref, sd_ref,
    intra_ref, carried_ref, local_ref, scarried_ref,
):
    first = here[0] * BLOCK
    ends = bounds(lens)
    front = entry_seg(first, ends)
    logd = logd_ref[...]
    t = lax.broadcasted_iota(jnp.int32, (BLOCK, BLOCK), 0)
    s = lax.broadcasted_iota(jnp.int32, (BLOCK, BLOCK), 1)
    cum = jnp.dot((s <= t).astype(F32), logd, precision=HI, preferred_element_type=F32)
    cum_rows = lax.dot_general(
        logd, (t <= s).astype(F32), (((0,), (0,)), ((), ())), precision=HI, preferred_element_type=F32
    )
    linked = (s <= t) & (seg_of(t + first, ends) == seg_of(s + first, ends))
    tok = lax.broadcasted_iota(jnp.int32, (BLOCK, HEADS), 0)
    carried_ref[...] = jnp.where(seg_of(tok + first, ends) == front, jnp.exp(cum), 0.0)
    for h in range(HEADS):
        cols = slice(h * HDIM, (h + 1) * HDIM)
        scores = contract_cols(query_ref[:, cols], key_ref[:, cols])
        spread = cum[:, h : h + 1] - cum_rows[h : h + 1, :]
        factor = jnp.exp(jnp.where(linked, spread, -1e30))
        weights = (scores * factor).astype(BF)
        intra_ref[:, cols] = jnp.dot(weights, value_ref[:, cols], preferred_element_type=F32)

    n = STEPS * ROWS_DEV
    a = lax.broadcasted_iota(jnp.int32, (n, n), 0)
    b = lax.broadcasted_iota(jnp.int32, (n, n), 1)
    same = (b <= a) & ((a - b) % ROWS_DEV == 0)
    sd = sd_ref[...].reshape(n, HEADS)
    scum = jnp.dot(same.astype(F32), sd, precision=HI, preferred_element_type=F32)
    scum_rows = lax.dot_general(
        sd, ((a <= b) & ((b - a) % ROWS_DEV == 0)).astype(F32), (((0,), (0,)), ((), ())),
        precision=HI, preferred_element_type=F32,
    )
    scarried_ref[...] = jnp.exp(scum)
    for h in range(HEADS):
        cols = slice(h * HDIM, (h + 1) * HDIM)
        q = sq_ref[:, :, cols].reshape(n, HDIM)
        k = sk_ref[:, :, cols].reshape(n, HDIM)
        v = sv_ref[:, :, cols].reshape(n, HDIM)
        spread = scum[:, h : h + 1] - scum_rows[h : h + 1, :]
        weights = contract_cols(q, k) * jnp.exp(jnp.where(same, spread, -1e30))
        high = weights.astype(BF)
        low = (weights - high.astype(F32)).astype(BF)
        local_ref[:, cols] = jnp.dot(high, v, preferred_element_type=F32) + jnp.dot(
            low, v, preferred_element_type=F32
        )


def scan_kernel(lens, got_ref, extra_ref, entry_ref, slice_ref):
    ends = bounds(lens)
    state = jnp.zeros((QUART, HDIM), F32)
    for k in range(NDEV):
        entry_ref[k] = state
        state = got_ref[k, S0 : S0 + 1, :] * state + got_ref[k, U0:T0, :]
    earlier = []
    for p in range(PROMPTS):
        e = ends[p] - 1
        b = e // BLOCK
        slot = jnp.int32(0)
        for other in earlier:
            slot = slot + (other == b).astype(jnp.int32)
        earlier.append(b)
        whole = e % BLOCK == BLOCK - 1
        lead = got_ref[b, S0 + 1 + p : S0 + 2 + p, :]
        tail = jnp.where(slot == 0, got_ref[b, T0:Q0, :], extra_ref[p])
        tail = jnp.where(whole, got_ref[b, U0:T0, :], tail)
        slice_ref[p] = lead * entry_ref[b] + tail


def project_kernel(here, got_ref, own_ref, s1_ref, s2_ref, s3_ref, out_ref, st_ref):
    x = here[0] // HEADS
    for shift, ref in enumerate((own_ref, s1_ref, s2_ref, s3_ref)):
        origin = lax.rem(x - shift + NX, NX)
        for p in range(PROMPTS):
            at = pl.multiple_of(p * HDIM + origin * QUART, QUART)
            st_ref[pl.ds(at, QUART), :] = ref[p]
    n = NDEV * ROWS_DEV
    q = got_ref[:, Q0:S0, :].reshape(n, HDIM).astype(BF)
    ids = jnp.broadcast_to(got_ref[:, S0 + 5 : S0 + 6, :], (NDEV, ROWS_DEV, HDIM))
    r = lax.broadcasted_iota(jnp.int32, (NDEV, ROWS_DEV, HDIM), 1)
    c = lax.broadcasted_iota(jnp.int32, (NDEV, ROWS_DEV, HDIM), 2)
    prompt = jnp.sum(jnp.where(r == c, ids, 0.0), axis=2, keepdims=True).reshape(n, 1)
    parts = [jnp.where(prompt == float(p), q, jnp.zeros_like(q)) for p in range(PROMPTS)]
    wide = jnp.concatenate(parts, axis=1)
    st = st_ref[...]
    high = st.astype(BF)
    low = (st - high.astype(F32)).astype(BF)
    res = jnp.dot(wide, high, preferred_element_type=F32) + jnp.dot(
        wide, low, preferred_element_type=F32
    )
    out_ref[...] = res.reshape(NDEV, ROWS_DEV, HDIM)


def mixed_kernel(query_ref, back_ref, intra_ref, carried_ref, mixed_ref, sums_ref):
    acc = jnp.zeros((BLOCK, HDIM), F32)
    for h in range(HEADS):
        cols = slice(h * HDIM, (h + 1) * HDIM)
        state = jnp.concatenate([back_ref[x * HEADS + h] for x in range(NX)], axis=0).astype(BF)
        outer = jnp.dot(query_ref[:, cols], state, preferred_element_type=F32)
        mixed = intra_ref[:, cols] + outer * carried_ref[:, h : h + 1]
        mixed_ref[:, cols] = mixed
        acc = acc + mixed * mixed
    flat = jnp.sum(acc.T, axis=0, keepdims=True)
    sums_ref[...] = jnp.concatenate(
        [flat[:, :HDIM], flat[:, HDIM:], jnp.zeros((6, HDIM), F32)], axis=0
    )


def decode_kernel(back_ref, local_ref, scarried_ref, sums_ref, dec_ref, send_ref):
    n = STEPS * ROWS_DEV
    acc = jnp.zeros((n, HDIM), F32)
    for h in range(HEADS):
        cols = slice(h * HDIM, (h + 1) * HDIM)
        carry = jnp.concatenate([back_ref[x * HEADS + h] for x in range(STEPS)], axis=0)
        dec = local_ref[:, cols] + carry * scarried_ref[:, h : h + 1]
        dec_ref[:, cols] = dec
        acc = acc + dec * dec
    full = jnp.concatenate([acc, jnp.zeros((HDIM - n, HDIM), F32)], axis=0)
    flat = jnp.sum(full.T, axis=0, keepdims=True)
    both = jnp.concatenate([sums_ref[0:2, :], flat, jnp.zeros((5, HDIM), F32)], axis=0)
    for k in range(HEADS):
        send_ref[k] = both


def final_kernel(sums_ref, mixed_ref, dec_ref, gain_ref, attn_ref, out_ref):
    total = sums_ref[0]
    for k in range(1, HEADS):
        total = total + sums_ref[k]
    scale = lax.rsqrt(total / (HEAD_COUNT * HDIM) + EPSILON)
    gain = gain_ref[...]

    def column(row):
        return jnp.broadcast_to(scale[row : row + 1, :], (HDIM, HDIM)).T

    for half in range(2):
        part = slice(half * HDIM, (half + 1) * HDIM)
        col = column(half)
        for h in range(HEADS):
            cols = slice(h * HDIM, (h + 1) * HDIM)
            attn_ref[part, cols] = (mixed_ref[part, cols] * col * gain[:, cols]).astype(BF)
    col = column(2)
    for h in range(HEADS):
        cols = slice(h * HDIM, (h + 1) * HDIM)
        res = (dec_ref[:, cols] * col[: STEPS * ROWS_DEV, :] * gain[:, cols]).astype(BF)
        for step in range(STEPS):
            out_ref[step, :, cols] = res[step * ROWS_DEV : (step + 1) * ROWS_DEV, :]


def shape(*dims, dtype=F32):
    return jax.ShapeDtypeStruct(dims, dtype)


def exchange(x, axis):
    return lax.all_to_all(x, axis, split_axis=0, concat_axis=0, tiled=True)


def more_tails(key_in, value_in, log_decay, prompt_lengths, first):
    ends = jnp.cumsum(prompt_lengths)
    positions = first + jnp.arange(BLOCK, dtype=jnp.int32)
    segs = jnp.sum((positions[:, None] >= ends[None, :]).astype(jnp.int32), axis=1)
    cum = jnp.cumsum(log_decay, axis=0)
    keys = key_in.reshape(BLOCK, HEADS, HDIM)
    values = value_in.reshape(BLOCK, HEADS, HDIM)
    parts = []
    for p in (1, 2):
        local = ends[p] - 1 - first
        owned = (local >= 0) & (local < BLOCK) & (ends[p - 1] - 1 >= first)
        safe = jnp.clip(local, 0, BLOCK - 1)
        taken = (jnp.arange(BLOCK) <= safe) & (segs == p) & owned
        spread = jnp.where(taken[:, None], cum[safe][None, :] - cum, 0.0)
        keep = jnp.where(taken[:, None], jnp.exp(spread), 0.0)
        tailed = (keys.astype(F32) * keep[:, :, None]).astype(BF)
        part = jnp.einsum("shd,she->hde", tailed, values, preferred_element_type=F32)
        part = part.reshape(HEADS, NX, QUART, HDIM).transpose(1, 0, 2, 3)
        parts.append(part.reshape(NDEV, QUART, HDIM))
    got = exchange(jnp.concatenate(parts, axis=1), SEQ)
    both = jnp.sum(got, axis=0)
    blank = jnp.zeros((QUART, HDIM), F32)
    return jnp.stack([blank, both[:QUART], both[QUART:], blank])


def local(
    query_in,
    key_in,
    value_in,
    log_decay,
    norm_gain,
    prompt_lengths,
    step_query,
    step_key,
    step_value,
    step_decay,
    row_prompt,
):
    me = lax.axis_index(SEQ).astype(jnp.int32)
    here = me[None]
    width = HEADS * HDIM
    n = STEPS * ROWS_DEV

    send = pl.pallas_call(
        send_kernel,
        out_shape=shape(NDEV, MSG, HDIM),
        in_specs=[SMEM] * 3 + [VMEM] * 4,
        out_specs=VMEM,
        scratch_shapes=[pltpu.VMEM((BLOCK, HEADS), F32)],
        compiler_params=params(),
        cost_estimate=cost(5),
        name="send",
    )(prompt_lengths, here, row_prompt, key_in, value_in, log_decay, step_query)
    got = exchange(send, SEQ)

    intra, carried, local_dec, scarried = pl.pallas_call(
        intra_kernel,
        out_shape=(shape(BLOCK, width), shape(BLOCK, HEADS), shape(n, width), shape(n, HEADS)),
        in_specs=[SMEM] * 2 + [VMEM] * 8,
        out_specs=(VMEM,) * 4,
        compiler_params=params(),
        cost_estimate=cost(6),
        name="intra",
    )(
        prompt_lengths, here, query_in, key_in, value_in, log_decay,
        step_query, step_key, step_value, step_decay,
    )

    ends = jnp.cumsum(prompt_lengths)
    blocks = (ends - 1) // BLOCK
    inner = (ends % BLOCK) != 0
    crowded = jnp.any((blocks[1:] == blocks[:-1]) & inner[1:])
    extra = lax.cond(
        crowded,
        lambda: more_tails(key_in, value_in, log_decay, prompt_lengths, me * BLOCK),
        lambda: jnp.zeros((PROMPTS, QUART, HDIM), F32),
    )

    entry, own = pl.pallas_call(
        scan_kernel,
        out_shape=(shape(NDEV, QUART, HDIM), shape(PROMPTS, QUART, HDIM)),
        in_specs=[SMEM] + [VMEM] * 2,
        out_specs=(VMEM,) * 2,
        compiler_params=params(),
        cost_estimate=cost(2),
        name="scan",
    )(prompt_lengths, got, extra)
    back = exchange(entry, SEQ)

    shifted = [
        lax.ppermute(own, "seq_0", [(i, (i + d) % NX) for i in range(NX)]) for d in range(1, NX)
    ]
    proj = pl.pallas_call(
        project_kernel,
        out_shape=shape(NDEV, ROWS_DEV, HDIM),
        in_specs=[SMEM] + [VMEM] * 5,
        out_specs=VMEM,
        scratch_shapes=[pltpu.VMEM((PROMPTS * HDIM, HDIM), F32)],
        compiler_params=params(),
        cost_estimate=cost(2),
        name="project",
    )(here, got, own, *shifted)
    proj_back = exchange(proj, SEQ)

    mixed, sums = pl.pallas_call(
        mixed_kernel,
        out_shape=(shape(BLOCK, width), shape(8, HDIM)),
        in_specs=[VMEM] * 4,
        out_specs=(VMEM,) * 2,
        compiler_params=params(),
        cost_estimate=cost(4),
        name="mixed",
    )(query_in, back, intra, carried)

    dec, sums_send = pl.pallas_call(
        decode_kernel,
        out_shape=(shape(n, width), shape(HEADS, 8, HDIM)),
        in_specs=[VMEM] * 4,
        out_specs=(VMEM,) * 2,
        compiler_params=params(),
        cost_estimate=cost(1),
        name="decode",
    )(proj_back, local_dec, scarried, sums)
    sums_all = exchange(sums_send, "head")

    return pl.pallas_call(
        final_kernel,
        out_shape=(shape(BLOCK, width, dtype=BF), shape(STEPS, ROWS_DEV, width, dtype=BF)),
        in_specs=[VMEM] * 4,
        out_specs=(VMEM,) * 2,
        compiler_params=params(),
        cost_estimate=cost(2),
        name="final",
    )(sums_all, mixed, dec, norm_gain.reshape(1, width))


def solution(mesh):
    split = Mesh(mesh.devices.reshape(NX, HEADS, mesh.shape["head"]), ("seq_0", "seq_1", "head"))
    placed = (
        P(SEQ, "head"),
        P(SEQ, "head"),
        P(SEQ, "head"),
        P(SEQ, "head"),
        P("head"),
        P(),
        P(None, SEQ, "head"),
        P(None, SEQ, "head"),
        P(None, SEQ, "head"),
        P(None, SEQ, "head"),
        P(SEQ),
    )
    return jax.shard_map(
        local,
        mesh=split,
        in_specs=placed,
        out_specs=(P(SEQ, "head"), P(None, SEQ, "head")),
        check_vma=False,
    )
```

```python
import functools

import jax
import jax.numpy as jnp
from jax import lax
from jax.experimental import pallas as pl
from jax.experimental.pallas import tpu as pltpu
from jax.sharding import Mesh
from jax.sharding import PartitionSpec as P

HEAD_COUNT = 64
HDIM = 128
BLOCK = 256
PROMPTS = 4
STEPS = 4
SEQ = ("seq_0", "seq_1")
EPSILON = 1e-06

NX = 4
HEADS = 8
NDEV = NX * HEADS
QUART = HDIM // NX
ROWS_DEV = 16

U0, Q0, S0, MSG = 0, 32, 48, 56
TAILS = PROMPTS - 1

BF = jnp.bfloat16
F32 = jnp.float32
HI = lax.Precision.HIGHEST

SMEM = pl.BlockSpec(memory_space=pltpu.SMEM)
VMEM = pl.BlockSpec(memory_space=pltpu.VMEM)


def params(mib=48):
    return pltpu.CompilerParams(vmem_limit_bytes=mib << 20)


def cost(us):
    return pl.CostEstimate(flops=int(us * 1e9), bytes_accessed=int(us * 3e6), transcendentals=0)


def bounds(lens):
    ends = []
    total = lens[0]
    for p in range(PROMPTS):
        if p:
            total = total + lens[p]
        ends.append(total)
    return ends


def seg_of(pos, ends):
    out = (pos >= ends[0]).astype(jnp.int32)
    for p in range(1, PROMPTS):
        out = out + (pos >= ends[p]).astype(jnp.int32)
    return out


def entry_seg(first, ends):
    return jnp.where(first > 0, seg_of(first - 1, ends), -1)


def cum_columns(logd):
    t = lax.broadcasted_iota(jnp.int32, (BLOCK, BLOCK), 0)
    s = lax.broadcasted_iota(jnp.int32, (BLOCK, BLOCK), 1)
    return lax.dot_general(
        (s <= t).astype(F32), logd, (((1,), (1,)), ((), ())), precision=HI, preferred_element_type=F32
    )


def contract_rows(a, b):
    return lax.dot_general(a, b, (((0,), (0,)), ((), ())), preferred_element_type=F32)


def contract_cols(a, b):
    return lax.dot_general(a, b, (((1,), (1,)), ((), ())), preferred_element_type=F32)


def send_kernel(
    lens, here, rows, key_ref, value_ref, logd_ref, query_ref, out_ref, tail_ref, cum_ref
):
    first = here[0] * BLOCK
    ends = bounds(lens)
    front = entry_seg(first, ends)
    seg_last = seg_of(first + (BLOCK - 1), ends)
    cum = cum_columns(logd_ref[...])
    cum_ref[...] = cum
    tok = lax.broadcasted_iota(jnp.int32, (BLOCK, HEADS), 0)
    seg = seg_of(tok + first, ends)

    leads = []
    for p in range(TAILS):
        at = ends[p] - 1 - first
        inside = (at >= 0) & (at < BLOCK)
        reached = cum_ref[pl.ds(jnp.clip(at, 0, BLOCK - 1), 1), :]
        leads.append(jnp.exp(reached) * (inside & (front == p)).astype(F32))
        rows_p = slice(p * QUART, (p + 1) * QUART)

        @pl.when(jnp.logical_not(inside))
        def _(rows_p=rows_p):
            tail_ref[:, rows_p, :] = jnp.zeros((NDEV, QUART, HDIM), F32)

        @pl.when(inside)
        def _(p=p, at=at, reached=reached, rows_p=rows_p):
            taken = (tok <= at) & (seg == p)
            tail = jnp.where(taken, jnp.exp(jnp.where(taken, reached - cum, 0.0)), 0.0)
            for h in range(HEADS):
                cols = slice(h * HDIM, (h + 1) * HDIM)
                tailed = (key_ref[:, cols].astype(F32) * tail[:, h : h + 1]).astype(BF)
                part = contract_rows(tailed, value_ref[:, cols])
                for x in range(NX):
                    tail_ref[x * HEADS + h, rows_p, :] = part[x * QUART : (x + 1) * QUART, :]

    last = cum[BLOCK - 1 : BLOCK, :]
    keep = jnp.where(seg == seg_last, jnp.exp(last - cum), 0.0)
    growth = jnp.exp(last) * (seg_last == front).astype(F32)
    lane = lax.broadcasted_iota(jnp.int32, (1, HDIM), 1)
    ids = jnp.zeros((1, HDIM), F32)
    for r in range(ROWS_DEV):
        ids = jnp.where(lane == r, rows[r].astype(F32), ids)
    for h in range(HEADS):
        cols = slice(h * HDIM, (h + 1) * HDIM)
        keyed = (key_ref[:, cols].astype(F32) * keep[:, h : h + 1]).astype(BF)
        update = contract_rows(keyed, value_ref[:, cols])
        scal = jnp.concatenate(
            [jnp.broadcast_to(growth[:, h : h + 1], (1, HDIM))]
            + [jnp.broadcast_to(leads[p][:, h : h + 1], (1, HDIM)) for p in range(TAILS)]
            + [ids, ids, ids, ids],
            axis=0,
        )
        for x in range(NX):
            out_ref[x * HEADS + h, U0:Q0, :] = update[x * QUART : (x + 1) * QUART, :]
            out_ref[x * HEADS + h, Q0:S0, :] = query_ref[x, :, cols].astype(F32)
            out_ref[x * HEADS + h, S0:MSG, :] = scal


def intra_kernel(
    lens, here, query_ref, key_ref, value_ref, logd_ref, sq_ref, sk_ref, sv_ref, sd_ref,
    intra_ref, carried_ref, local_ref, scarried_ref,
):
    first = here[0] * BLOCK
    ends = bounds(lens)
    front = entry_seg(first, ends)
    logd = logd_ref[...]
    t = lax.broadcasted_iota(jnp.int32, (BLOCK, BLOCK), 0)
    s = lax.broadcasted_iota(jnp.int32, (BLOCK, BLOCK), 1)
    cum = cum_columns(logd)
    cum_rows = jnp.dot(logd, (t <= s).astype(F32), precision=HI, preferred_element_type=F32)
    linked = (s <= t) & (seg_of(t + first, ends) == seg_of(s + first, ends))
    tok = lax.broadcasted_iota(jnp.int32, (BLOCK, HEADS), 0)
    carried_ref[...] = jnp.where(seg_of(tok + first, ends) == front, jnp.exp(cum), 0.0)
    for h in range(HEADS):
        cols = slice(h * HDIM, (h + 1) * HDIM)
        scores = contract_cols(query_ref[:, cols], key_ref[:, cols])
        spread = cum[:, h : h + 1] - cum_rows[h : h + 1, :]
        factor = jnp.exp(jnp.where(linked, spread, -1e30))
        weights = (scores * factor).astype(BF)
        intra_ref[:, cols] = jnp.dot(weights, value_ref[:, cols], preferred_element_type=F32)

    n = STEPS * ROWS_DEV
    a = lax.broadcasted_iota(jnp.int32, (n, n), 0)
    b = lax.broadcasted_iota(jnp.int32, (n, n), 1)
    same = (b <= a) & ((a - b) % ROWS_DEV == 0)
    total = sd_ref[0]
    pieces = [total]
    for step in range(1, STEPS):
        total = total + sd_ref[step]
        pieces.append(total)
    scum_rows = jnp.concatenate(pieces, axis=1)
    scum = lax.dot_general(
        (a == b).astype(F32), scum_rows, (((1,), (1,)), ((), ())), precision=HI,
        preferred_element_type=F32,
    )
    scarried_ref[...] = jnp.exp(scum)
    for h in range(HEADS):
        cols = slice(h * HDIM, (h + 1) * HDIM)
        q = sq_ref[:, :, cols].reshape(n, HDIM)
        k = sk_ref[:, :, cols].reshape(n, HDIM)
        v = sv_ref[:, :, cols].reshape(n, HDIM)
        spread = scum[:, h : h + 1] - scum_rows[h : h + 1, :]
        weights = contract_cols(q, k) * jnp.exp(jnp.where(same, spread, -1e30))
        high = weights.astype(BF)
        low = (weights - high.astype(F32)).astype(BF)
        local_ref[:, cols] = jnp.dot(high, v, preferred_element_type=F32) + jnp.dot(
            low, v, preferred_element_type=F32
        )


def scan_kernel(lens, got_ref, entry_ref, slice_ref):
    ends = bounds(lens)
    state = jnp.zeros((QUART, HDIM), F32)
    for k in range(NDEV):
        entry_ref[k] = state
        state = got_ref[k, S0 : S0 + 1, :] * state + got_ref[k, U0:Q0, :]
    slice_ref[TAILS] = state
    for p in range(TAILS):
        b = (ends[p] - 1) // BLOCK
        slice_ref[p] = got_ref[b, S0 + 1 + p : S0 + 2 + p, :] * entry_ref[b]


def join_kernel(slice_ref, tail_ref, out_ref):
    for p in range(TAILS):
        out_ref[p] = slice_ref[p] + tail_ref[0, p * QUART : (p + 1) * QUART, :]
    out_ref[TAILS] = slice_ref[TAILS]


def project_kernel(here, got_ref, own_ref, s1_ref, s2_ref, s3_ref, out_ref, st_ref):
    x = here[0] // HEADS
    for shift, ref in enumerate((own_ref, s1_ref, s2_ref, s3_ref)):
        origin = lax.rem(x - shift + NX, NX)
        for p in range(PROMPTS):
            at = pl.multiple_of(p * HDIM + origin * QUART, QUART)
            st_ref[pl.ds(at, QUART), :] = ref[p]
    n = NDEV * ROWS_DEV
    q = got_ref[:, Q0:S0, :].reshape(n, HDIM).astype(BF)
    ids = jnp.broadcast_to(got_ref[:, S0 + 4 : S0 + 5, :], (NDEV, ROWS_DEV, HDIM))
    r = lax.broadcasted_iota(jnp.int32, (NDEV, ROWS_DEV, HDIM), 1)
    c = lax.broadcasted_iota(jnp.int32, (NDEV, ROWS_DEV, HDIM), 2)
    prompt = jnp.sum(jnp.where(r == c, ids, 0.0), axis=2, keepdims=True).reshape(n, 1)
    parts = [jnp.where(prompt == float(p), q, jnp.zeros_like(q)) for p in range(PROMPTS)]
    wide = jnp.concatenate(parts, axis=1)
    st = st_ref[...]
    high = st.astype(BF)
    low = (st - high.astype(F32)).astype(BF)
    res = jnp.dot(wide, high, preferred_element_type=F32) + jnp.dot(
        wide, low, preferred_element_type=F32
    )
    out_ref[...] = res.reshape(NDEV, ROWS_DEV, HDIM)


def mixed_kernel(query_ref, back_ref, intra_ref, carried_ref, mixed_ref, sums_ref):
    acc = jnp.zeros((BLOCK, HDIM), F32)
    for h in range(HEADS):
        cols = slice(h * HDIM, (h + 1) * HDIM)
        state = jnp.concatenate([back_ref[x * HEADS + h] for x in range(NX)], axis=0).astype(BF)
        outer = jnp.dot(query_ref[:, cols], state, preferred_element_type=F32)
        mixed = intra_ref[:, cols] + outer * carried_ref[:, h : h + 1]
        mixed_ref[:, cols] = mixed
        acc = acc + mixed * mixed
    flat = jnp.sum(acc.T, axis=0, keepdims=True)
    sums_ref[...] = jnp.concatenate(
        [flat[:, :HDIM], flat[:, HDIM:], jnp.zeros((6, HDIM), F32)], axis=0
    )


def decode_kernel(back_ref, local_ref, scarried_ref, sums_ref, dec_ref, send_ref):
    n = STEPS * ROWS_DEV
    acc = jnp.zeros((n, HDIM), F32)
    for h in range(HEADS):
        cols = slice(h * HDIM, (h + 1) * HDIM)
        carry = jnp.concatenate([back_ref[x * HEADS + h] for x in range(STEPS)], axis=0)
        dec = local_ref[:, cols] + carry * scarried_ref[:, h : h + 1]
        dec_ref[:, cols] = dec
        acc = acc + dec * dec
    full = jnp.concatenate([acc, jnp.zeros((HDIM - n, HDIM), F32)], axis=0)
    flat = jnp.sum(full.T, axis=0, keepdims=True)
    both = jnp.concatenate([sums_ref[0:2, :], flat, jnp.zeros((5, HDIM), F32)], axis=0)
    for k in range(HEADS):
        send_ref[k] = both


def final_kernel(sums_ref, mixed_ref, dec_ref, gain_ref, attn_ref, out_ref):
    total = sums_ref[0]
    for k in range(1, HEADS):
        total = total + sums_ref[k]
    scale = lax.rsqrt(total / (HEAD_COUNT * HDIM) + EPSILON)
    gain = gain_ref[...]

    def column(row):
        return jnp.broadcast_to(scale[row : row + 1, :], (HDIM, HDIM)).T

    for half in range(2):
        part = slice(half * HDIM, (half + 1) * HDIM)
        col = column(half)
        for h in range(HEADS):
            cols = slice(h * HDIM, (h + 1) * HDIM)
            attn_ref[part, cols] = (mixed_ref[part, cols] * col * gain[:, cols]).astype(BF)
    col = column(2)
    for h in range(HEADS):
        cols = slice(h * HDIM, (h + 1) * HDIM)
        res = (dec_ref[:, cols] * col[: STEPS * ROWS_DEV, :] * gain[:, cols]).astype(BF)
        for step in range(STEPS):
            out_ref[step, :, cols] = res[step * ROWS_DEV : (step + 1) * ROWS_DEV, :]


def shape(*dims, dtype=F32):
    return jax.ShapeDtypeStruct(dims, dtype)


def exchange(x, axis):
    return lax.all_to_all(x, axis, split_axis=0, concat_axis=0, tiled=True)


def local(
    query_in,
    key_in,
    value_in,
    log_decay,
    norm_gain,
    prompt_lengths,
    step_query,
    step_key,
    step_value,
    step_decay,
    row_prompt,
):
    me = lax.axis_index(SEQ).astype(jnp.int32)
    here = me[None]
    width = HEADS * HDIM
    n = STEPS * ROWS_DEV

    logd = log_decay.T
    send, tails = pl.pallas_call(
        send_kernel,
        out_shape=(shape(NDEV, MSG, HDIM), shape(NDEV, TAILS * QUART, HDIM)),
        in_specs=[SMEM] * 3 + [VMEM] * 4,
        out_specs=(VMEM,) * 2,
        scratch_shapes=[pltpu.VMEM((BLOCK, HEADS), F32)],
        compiler_params=params(),
        cost_estimate=cost(5),
        name="send",
    )(prompt_lengths, here, row_prompt, key_in, value_in, logd, step_query)
    tails = lax.psum_scatter(tails, "seq_0", scatter_dimension=0, tiled=True)
    tails = lax.psum_scatter(tails, "seq_1", scatter_dimension=0, tiled=True)
    got = exchange(send, SEQ)

    intra, carried, local_dec, scarried = pl.pallas_call(
        intra_kernel,
        out_shape=(shape(BLOCK, width), shape(BLOCK, HEADS), shape(n, width), shape(n, HEADS)),
        in_specs=[SMEM] * 2 + [VMEM] * 8,
        out_specs=(VMEM,) * 4,
        compiler_params=params(),
        cost_estimate=cost(6),
        name="intra",
    )(
        prompt_lengths, here, query_in, key_in, value_in, logd,
        step_query, step_key, step_value, step_decay.transpose(0, 2, 1),
    )

    got, intra, carried, local_dec, scarried = lax.optimization_barrier(
        (got, intra, carried, local_dec, scarried)
    )
    entry, own = pl.pallas_call(
        scan_kernel,
        out_shape=(shape(NDEV, QUART, HDIM), shape(PROMPTS, QUART, HDIM)),
        in_specs=[SMEM, VMEM],
        out_specs=(VMEM,) * 2,
        compiler_params=params(),
        cost_estimate=cost(2),
        name="scan",
    )(prompt_lengths, got)
    own = pl.pallas_call(
        join_kernel,
        out_shape=shape(PROMPTS, QUART, HDIM),
        in_specs=[VMEM] * 2,
        out_specs=VMEM,
        compiler_params=params(),
        cost_estimate=cost(1),
        name="join",
    )(own, tails)
    back = exchange(entry, SEQ)

    shifted = [
        lax.ppermute(own, "seq_0", [(i, (i + d) % NX) for i in range(NX)]) for d in range(1, NX)
    ]
    proj = pl.pallas_call(
        project_kernel,
        out_shape=shape(NDEV, ROWS_DEV, HDIM),
        in_specs=[SMEM] + [VMEM] * 5,
        out_specs=VMEM,
        scratch_shapes=[pltpu.VMEM((PROMPTS * HDIM, HDIM), F32)],
        compiler_params=params(),
        cost_estimate=cost(2),
        name="project",
    )(here, got, own, *shifted)
    proj_back = exchange(proj, SEQ)

    mixed, sums = pl.pallas_call(
        mixed_kernel,
        out_shape=(shape(BLOCK, width), shape(8, HDIM)),
        in_specs=[VMEM] * 4,
        out_specs=(VMEM,) * 2,
        compiler_params=params(),
        cost_estimate=cost(4),
        name="mixed",
    )(query_in, back, intra, carried)

    dec, sums_send = pl.pallas_call(
        decode_kernel,
        out_shape=(shape(n, width), shape(HEADS, 8, HDIM)),
        in_specs=[VMEM] * 4,
        out_specs=(VMEM,) * 2,
        compiler_params=params(),
        cost_estimate=cost(1),
        name="decode",
    )(proj_back, local_dec, scarried, sums)
    sums_all = exchange(sums_send, "head")

    return pl.pallas_call(
        final_kernel,
        out_shape=(shape(BLOCK, width, dtype=BF), shape(STEPS, ROWS_DEV, width, dtype=BF)),
        in_specs=[VMEM] * 4,
        out_specs=(VMEM,) * 2,
        compiler_params=params(),
        cost_estimate=cost(2),
        name="final",
    )(sums_all, mixed, dec, norm_gain.reshape(1, width))


def solution(mesh):
    split = Mesh(mesh.devices.reshape(NX, HEADS, mesh.shape["head"]), ("seq_0", "seq_1", "head"))
    placed = (
        P(SEQ, "head"),
        P(SEQ, "head"),
        P(SEQ, "head"),
        P(SEQ, "head"),
        P("head"),
        P(),
        P(None, SEQ, "head"),
        P(None, SEQ, "head"),
        P(None, SEQ, "head"),
        P(None, SEQ, "head"),
        P(SEQ),
    )
    return jax.shard_map(
        local,
        mesh=split,
        in_specs=placed,
        out_specs=(P(SEQ, "head"), P(None, SEQ, "head")),
        check_vma=False,
    )
```

```python
import functools

import jax
import jax.numpy as jnp
from jax import lax
from jax.experimental import pallas as pl
from jax.experimental.pallas import tpu as pltpu
from jax.sharding import Mesh
from jax.sharding import PartitionSpec as P

HEAD_COUNT = 64
HDIM = 128
BLOCK = 256
PROMPTS = 4
STEPS = 4
SEQ = ("seq_0", "seq_1")
EPSILON = 1e-06

NX = 4
HEADS = 8
NDEV = NX * HEADS
QUART = HDIM // NX
ROWS_DEV = 16

S0, ASK = 16, 24
IDS = S0 + 1 + PROMPTS
T0, GIVE = 32, 64
O0, BACK = 32, 48

BF = jnp.bfloat16
F32 = jnp.float32
HI = lax.Precision.HIGHEST

SMEM = pl.BlockSpec(memory_space=pltpu.SMEM)
VMEM = pl.BlockSpec(memory_space=pltpu.VMEM)


def params(mib=24):
    return pltpu.CompilerParams(vmem_limit_bytes=mib << 20)


def cost(us):
    return pl.CostEstimate(flops=int(us * 1e9), bytes_accessed=int(us * 3e6), transcendentals=0)


def bounds(lens):
    ends = []
    total = lens[0]
    for p in range(PROMPTS):
        if p:
            total = total + lens[p]
        ends.append(total)
    return ends


def seg_of(pos, ends):
    out = (pos >= ends[0]).astype(jnp.int32)
    for p in range(1, PROMPTS):
        out = out + (pos >= ends[p]).astype(jnp.int32)
    return out


def entry_seg(first, ends):
    return jnp.where(first > 0, seg_of(first - 1, ends), -1)


def cum_columns(logd):
    t = lax.broadcasted_iota(jnp.int32, (BLOCK, BLOCK), 0)
    s = lax.broadcasted_iota(jnp.int32, (BLOCK, BLOCK), 1)
    return lax.dot_general(
        (s <= t).astype(F32), logd, (((1,), (1,)), ((), ())), precision=HI, preferred_element_type=F32
    )


def contract_rows(a, b):
    return lax.dot_general(a, b, (((0,), (0,)), ((), ())), preferred_element_type=F32)


def contract_cols(a, b):
    return lax.dot_general(a, b, (((1,), (1,)), ((), ())), preferred_element_type=F32)


def ask_kernel(lens, here, rows, logd_ref, query_ref, out_ref, flag_ref, cum_ref):
    first = here[0] * BLOCK
    ends = bounds(lens)
    front = entry_seg(first, ends)
    seg_last = seg_of(first + (BLOCK - 1), ends)
    cum_ref[...] = cum_columns(logd_ref[...])
    growth = jnp.exp(cum_ref[BLOCK - 1 : BLOCK, :]) * (seg_last == front).astype(F32)
    leads = []
    crowded = jnp.int32(0)
    for p in range(PROMPTS):
        at = ends[p] - 1 - first
        inside = (at >= 0) & (at < BLOCK)
        reached = cum_ref[pl.ds(jnp.clip(at, 0, BLOCK - 1), 1), :]
        leads.append(jnp.exp(reached) * (inside & (front == p)).astype(F32))
        if p:
            same = (ends[p] - 1) // BLOCK == (ends[p - 1] - 1) // BLOCK
            crowded = crowded | (same & (ends[p] % BLOCK != 0)).astype(jnp.int32)
    flag_ref[0] = crowded
    lane = lax.broadcasted_iota(jnp.int32, (1, HDIM), 1)
    ids = jnp.zeros((1, HDIM), F32)
    for r in range(ROWS_DEV):
        ids = jnp.where(lane == r, rows[r].astype(F32), ids)
    for h in range(HEADS):
        cols = slice(h * HDIM, (h + 1) * HDIM)
        scal = jnp.concatenate(
            [jnp.broadcast_to(growth[:, h : h + 1], (1, HDIM))]
            + [jnp.broadcast_to(leads[p][:, h : h + 1], (1, HDIM)) for p in range(PROMPTS)]
            + [ids, ids, ids],
            axis=0,
        )
        for x in range(NX):
            out_ref[x * HEADS + h, 0:S0, :] = query_ref[x, :, cols].astype(F32)
            out_ref[x * HEADS + h, S0:ASK, :] = scal


def update_kernel(lens, here, key_ref, value_ref, logd_ref, out_ref, cum_ref):
    first = here[0] * BLOCK
    ends = bounds(lens)
    seg_last = seg_of(first + (BLOCK - 1), ends)
    cum = cum_columns(logd_ref[...])
    cum_ref[...] = cum
    tok = lax.broadcasted_iota(jnp.int32, (BLOCK, HEADS), 0)
    seg = seg_of(tok + first, ends)
    keep = jnp.where(seg == seg_last, jnp.exp(cum[BLOCK - 1 : BLOCK, :] - cum), 0.0)
    found = jnp.int32(-1)
    spot = jnp.int32(0)
    for p in range(PROMPTS):
        at = ends[p] - 1 - first
        take = (at >= 0) & (at < BLOCK - 1) & (found < 0)
        found = jnp.where(take, p, found)
        spot = jnp.where(take, at, spot)

    def emit(factor, row):
        for h in range(HEADS):
            cols = slice(h * HDIM, (h + 1) * HDIM)
            keyed = (key_ref[:, cols].astype(F32) * factor[:, h : h + 1]).astype(BF)
            total = contract_rows(value_ref[:, cols], keyed)
            for x in range(NX):
                out_ref[x * HEADS + h, row : row + QUART, :] = total[x * QUART : (x + 1) * QUART, :]

    emit(keep, 0)

    @pl.when(found < 0)
    def _():
        out_ref[:, T0:GIVE, :] = jnp.zeros((NDEV, QUART, HDIM), F32)

    @pl.when(found >= 0)
    def _():
        reached = cum_ref[pl.ds(spot, 1), :]
        taken = (tok <= spot) & (seg == found)
        emit(jnp.where(taken, jnp.exp(jnp.where(taken, reached - cum, 0.0)), 0.0), T0)


def intra_kernel(
    lens, here, query_ref, key_ref, value_ref, logd_ref, sq_ref, sk_ref, sv_ref, sd_ref,
    intra_ref, carried_ref, local_ref, scarried_ref,
):
    first = here[0] * BLOCK
    ends = bounds(lens)
    front = entry_seg(first, ends)
    logd = logd_ref[...]
    t = lax.broadcasted_iota(jnp.int32, (BLOCK, BLOCK), 0)
    s = lax.broadcasted_iota(jnp.int32, (BLOCK, BLOCK), 1)
    cum = cum_columns(logd)
    cum_rows = jnp.dot(logd, (t <= s).astype(F32), precision=HI, preferred_element_type=F32)
    linked = (s <= t) & (seg_of(t + first, ends) == seg_of(s + first, ends))
    tok = lax.broadcasted_iota(jnp.int32, (BLOCK, HEADS), 0)
    carried_ref[...] = jnp.where(seg_of(tok + first, ends) == front, jnp.exp(cum), 0.0)
    for h in range(HEADS):
        cols = slice(h * HDIM, (h + 1) * HDIM)
        scores = contract_cols(query_ref[:, cols], key_ref[:, cols])
        spread = cum[:, h : h + 1] - cum_rows[h : h + 1, :]
        factor = jnp.exp(jnp.where(linked, spread, -1e30))
        weights = (scores * factor).astype(BF)
        intra_ref[:, cols] = jnp.dot(weights, value_ref[:, cols], preferred_element_type=F32)

    n = STEPS * ROWS_DEV
    a = lax.broadcasted_iota(jnp.int32, (n, n), 0)
    b = lax.broadcasted_iota(jnp.int32, (n, n), 1)
    same = (b <= a) & ((a - b) % ROWS_DEV == 0)
    total = sd_ref[0]
    pieces = [total]
    for step in range(1, STEPS):
        total = total + sd_ref[step]
        pieces.append(total)
    scum_rows = jnp.concatenate(pieces, axis=1)
    scum = lax.dot_general(
        (a == b).astype(F32), scum_rows, (((1,), (1,)), ((), ())), precision=HI,
        preferred_element_type=F32,
    )
    scarried_ref[...] = jnp.exp(scum)
    for h in range(HEADS):
        cols = slice(h * HDIM, (h + 1) * HDIM)
        q = sq_ref[:, :, cols].reshape(n, HDIM)
        k = sk_ref[:, :, cols].reshape(n, HDIM)
        v = sv_ref[:, :, cols].reshape(n, HDIM)
        spread = scum[:, h : h + 1] - scum_rows[h : h + 1, :]
        weights = contract_cols(q, k) * jnp.exp(jnp.where(same, spread, -1e30))
        high = weights.astype(BF)
        low = (weights - high.astype(F32)).astype(BF)
        local_ref[:, cols] = jnp.dot(high, v, preferred_element_type=F32) + jnp.dot(
            low, v, preferred_element_type=F32
        )


def scan_kernel(lens, here, ask_ref, q1_ref, q2_ref, q3_ref, give_ref, extra_ref, out_ref, st_ref):
    ends = bounds(lens)
    state = jnp.zeros((QUART, HDIM), F32)
    for k in range(NDEV):
        out_ref[k, 0:O0, :] = state
        state = ask_ref[k, S0 : S0 + 1, :] * state + give_ref[k, 0:T0, :]
    finals = []
    earlier = []
    for p in range(PROMPTS):
        e = ends[p] - 1
        b = e // BLOCK
        slot = jnp.int32(0)
        for other in earlier:
            slot = slot + (other == b).astype(jnp.int32)
        earlier.append(b)
        whole = e % BLOCK == BLOCK - 1
        lead = ask_ref[b, S0 + 1 + p : S0 + 2 + p, :]
        tail = jnp.where(slot == 0, give_ref[b, T0:GIVE, :], extra_ref[p])
        tail = jnp.where(whole, give_ref[b, 0:T0, :], tail)
        finals.append(lead * out_ref[b, 0:O0, :] + tail)

    n = NDEV * ROWS_DEV
    x = here[0] // HEADS
    st_ref[...] = jnp.zeros_like(st_ref)
    ids = jnp.broadcast_to(ask_ref[:, IDS : IDS + 1, :], (NDEV, ROWS_DEV, HDIM))
    r = lax.broadcasted_iota(jnp.int32, (NDEV, ROWS_DEV, HDIM), 1)
    c = lax.broadcasted_iota(jnp.int32, (NDEV, ROWS_DEV, HDIM), 2)
    prompt = jnp.sum(jnp.where(r == c, ids, 0.0), axis=2, keepdims=True).reshape(n, 1)
    res = jnp.zeros((n, HDIM), F32)
    for shift in range(NX):
        step = lax.rem(x - shift + NX, NX)
        at = pl.multiple_of(step * QUART, QUART)
        if shift:
            q = (q1_ref, q2_ref, q3_ref)[shift - 1][...]
        else:
            q = ask_ref[:, 0:S0, :]
        q = q.reshape(n, HDIM)
        for p in range(PROMPTS):
            st_ref[shift, pl.ds(at, QUART), p * HDIM : (p + 1) * HDIM] = finals[p]
        wide = jnp.concatenate(
            [jnp.where(prompt == float(p), q, 0.0).astype(BF) for p in range(PROMPTS)], axis=1
        )
        st = st_ref[shift]
        high = st.astype(BF)
        low = (st - high.astype(F32)).astype(BF)
        res = res + contract_cols(wide, high) + contract_cols(wide, low)
    out_ref[:, O0:BACK, :] = res.reshape(NDEV, ROWS_DEV, HDIM)


def mixed_kernel(
    query_ref, back_ref, intra_ref, carried_ref, local_ref, scarried_ref,
    mixed_ref, dec_ref, send_ref,
):
    acc = jnp.zeros((BLOCK, HDIM), F32)
    for h in range(HEADS):
        cols = slice(h * HDIM, (h + 1) * HDIM)
        state = jnp.concatenate(
            [back_ref[x * HEADS + h, 0:O0, :] for x in range(NX)], axis=0
        ).astype(BF)
        outer = contract_cols(query_ref[:, cols], state)
        mixed = intra_ref[:, cols] + outer * carried_ref[:, h : h + 1]
        mixed_ref[:, cols] = mixed
        acc = acc + mixed * mixed
    flat = jnp.sum(acc.T, axis=0, keepdims=True)

    n = STEPS * ROWS_DEV
    acc = jnp.zeros((n, HDIM), F32)
    for h in range(HEADS):
        cols = slice(h * HDIM, (h + 1) * HDIM)
        got = [back_ref[x * HEADS + h, O0:BACK, :] for x in range(NX)]
        carry = jnp.concatenate(
            [
                jnp.concatenate([g[:, i * QUART : (i + 1) * QUART] for g in got], axis=1)
                for i in range(STEPS)
            ],
            axis=0,
        )
        dec = local_ref[:, cols] + carry * scarried_ref[:, h : h + 1]
        dec_ref[:, cols] = dec
        acc = acc + dec * dec
    full = jnp.concatenate([acc, jnp.zeros((HDIM - n, HDIM), F32)], axis=0)
    dflat = jnp.sum(full.T, axis=0, keepdims=True)
    both = jnp.concatenate(
        [flat[:, :HDIM], flat[:, HDIM:], dflat, jnp.zeros((5, HDIM), F32)], axis=0
    )
    for k in range(HEADS):
        send_ref[k] = both


def final_kernel(sums_ref, mixed_ref, dec_ref, gain_ref, attn_ref, out_ref):
    total = sums_ref[0]
    for k in range(1, HEADS):
        total = total + sums_ref[k]
    scale = lax.rsqrt(total / (HEAD_COUNT * HDIM) + EPSILON)
    gain = gain_ref[...]

    def column(row):
        return jnp.broadcast_to(scale[row : row + 1, :], (HDIM, HDIM)).T

    for half in range(2):
        part = slice(half * HDIM, (half + 1) * HDIM)
        col = column(half)
        for h in range(HEADS):
            cols = slice(h * HDIM, (h + 1) * HDIM)
            attn_ref[part, cols] = (mixed_ref[part, cols] * col * gain[:, cols]).astype(BF)
    col = column(2)
    for h in range(HEADS):
        cols = slice(h * HDIM, (h + 1) * HDIM)
        res = (dec_ref[:, cols] * col[: STEPS * ROWS_DEV, :] * gain[:, cols]).astype(BF)
        for step in range(STEPS):
            out_ref[step, :, cols] = res[step * ROWS_DEV : (step + 1) * ROWS_DEV, :]


def shape(*dims, dtype=F32):
    return jax.ShapeDtypeStruct(dims, dtype)


def exchange(x, axis):
    return lax.all_to_all(x, axis, split_axis=0, concat_axis=0, tiled=True)


def more_tails(key_in, value_in, log_decay, prompt_lengths, first):
    ends = jnp.cumsum(prompt_lengths)
    positions = first + jnp.arange(BLOCK, dtype=jnp.int32)
    segs = jnp.sum((positions[:, None] >= ends[None, :]).astype(jnp.int32), axis=1)
    cum = jnp.cumsum(log_decay, axis=0)
    keys = key_in.reshape(BLOCK, HEADS, HDIM)
    values = value_in.reshape(BLOCK, HEADS, HDIM)
    parts = []
    for p in (1, 2):
        local = ends[p] - 1 - first
        owned = (local >= 0) & (local < BLOCK) & (ends[p - 1] - 1 >= first)
        safe = jnp.clip(local, 0, BLOCK - 1)
        taken = (jnp.arange(BLOCK) <= safe) & (segs == p) & owned
        spread = jnp.where(taken[:, None], cum[safe][None, :] - cum, 0.0)
        keep = jnp.where(taken[:, None], jnp.exp(spread), 0.0)
        tailed = (keys.astype(F32) * keep[:, :, None]).astype(BF)
        part = jnp.einsum("shd,she->hed", tailed, values, preferred_element_type=F32)
        part = part.reshape(HEADS, NX, QUART, HDIM).transpose(1, 0, 2, 3)
        parts.append(part.reshape(NDEV, QUART, HDIM))
    got = exchange(jnp.concatenate(parts, axis=1), SEQ)
    both = jnp.sum(got, axis=0)
    blank = jnp.zeros((QUART, HDIM), F32)
    return jnp.stack([blank, both[:QUART], both[QUART:], blank])


def local(
    query_in,
    key_in,
    value_in,
    log_decay,
    norm_gain,
    prompt_lengths,
    step_query,
    step_key,
    step_value,
    step_decay,
    row_prompt,
):
    me = lax.axis_index(SEQ).astype(jnp.int32)
    here = me[None]
    width = HEADS * HDIM
    n = STEPS * ROWS_DEV

    logd = log_decay.T
    ask, crowded = pl.pallas_call(
        ask_kernel,
        out_shape=(shape(NDEV, ASK, HDIM), shape(1, dtype=jnp.int32)),
        in_specs=[SMEM] * 3 + [VMEM] * 2,
        out_specs=(VMEM, SMEM),
        scratch_shapes=[pltpu.VMEM((BLOCK, HEADS), F32)],
        compiler_params=params(),
        cost_estimate=cost(2),
        name="ask",
    )(prompt_lengths, here, row_prompt, logd, step_query)
    asked = exchange(ask, SEQ)

    give = pl.pallas_call(
        update_kernel,
        out_shape=shape(NDEV, GIVE, HDIM),
        in_specs=[SMEM] * 2 + [VMEM] * 3,
        out_specs=VMEM,
        scratch_shapes=[pltpu.VMEM((BLOCK, HEADS), F32)],
        compiler_params=params(),
        cost_estimate=cost(3),
        name="update",
    )(prompt_lengths, here, key_in, value_in, logd)
    asked, give = lax.optimization_barrier((asked, give))
    given = exchange(give, SEQ)
    queries = asked[:, :S0, :]
    shifted = [
        lax.ppermute(queries, "seq_0", [(i, (i + d) % NX) for i in range(NX)])
        for d in range(1, NX)
    ]

    intra, carried, local_dec, scarried = pl.pallas_call(
        intra_kernel,
        out_shape=(shape(BLOCK, width), shape(BLOCK, HEADS), shape(n, width), shape(n, HEADS)),
        in_specs=[SMEM] * 2 + [VMEM] * 8,
        out_specs=(VMEM,) * 4,
        compiler_params=params(),
        cost_estimate=cost(6),
        name="intra",
    )(
        prompt_lengths, here, query_in, key_in, value_in, logd,
        step_query, step_key, step_value, step_decay.transpose(0, 2, 1),
    )

    crowded, shifted = lax.optimization_barrier((crowded, shifted))
    extra = lax.cond(
        crowded[0] > 0,
        lambda: more_tails(key_in, value_in, log_decay, prompt_lengths, me * BLOCK),
        lambda: jnp.zeros((PROMPTS, QUART, HDIM), F32),
    )
    given, intra, carried, local_dec, scarried, extra, shifted = lax.optimization_barrier(
        (given, intra, carried, local_dec, scarried, extra, shifted)
    )
    out = pl.pallas_call(
        scan_kernel,
        out_shape=shape(NDEV, BACK, HDIM),
        in_specs=[SMEM] * 2 + [VMEM] * 6,
        out_specs=VMEM,
        scratch_shapes=[pltpu.VMEM((NX, HDIM, PROMPTS * HDIM), F32)],
        compiler_params=params(),
        cost_estimate=cost(3),
        name="scan",
    )(prompt_lengths, here, asked, *shifted, given, extra)
    back = exchange(out, SEQ)

    mixed, dec, sums_send = pl.pallas_call(
        mixed_kernel,
        out_shape=(shape(BLOCK, width), shape(n, width), shape(HEADS, 8, HDIM)),
        in_specs=[VMEM] * 6,
        out_specs=(VMEM,) * 3,
        compiler_params=params(),
        cost_estimate=cost(2),
        name="mixed",
    )(query_in, back, intra, carried, local_dec, scarried)
    sums_all = exchange(sums_send, "head")

    return pl.pallas_call(
        final_kernel,
        out_shape=(shape(BLOCK, width, dtype=BF), shape(STEPS, ROWS_DEV, width, dtype=BF)),
        in_specs=[VMEM] * 4,
        out_specs=(VMEM,) * 2,
        compiler_params=params(),
        cost_estimate=cost(2),
        name="final",
    )(sums_all, mixed, dec, norm_gain.reshape(1, width))


def solution(mesh):
    split = Mesh(mesh.devices.reshape(NX, HEADS, mesh.shape["head"]), ("seq_0", "seq_1", "head"))
    placed = (
        P(SEQ, "head"),
        P(SEQ, "head"),
        P(SEQ, "head"),
        P(SEQ, "head"),
        P("head"),
        P(),
        P(None, SEQ, "head"),
        P(None, SEQ, "head"),
        P(None, SEQ, "head"),
        P(None, SEQ, "head"),
        P(SEQ),
    )
    return jax.shard_map(
        local,
        mesh=split,
        in_specs=placed,
        out_specs=(P(SEQ, "head"), P(None, SEQ, "head")),
        check_vma=False,
    )
```

```python
import functools

import jax
import jax.numpy as jnp
from jax import lax
from jax.experimental import pallas as pl
from jax.experimental.pallas import tpu as pltpu
from jax.sharding import Mesh
from jax.sharding import PartitionSpec as P

HEAD_COUNT = 64
HDIM = 128
BLOCK = 256
PROMPTS = 4
STEPS = 4
SEQ = ("seq_0", "seq_1")
EPSILON = 1e-06

NX = 4
NZ = 8
PAIR = 2
HEADS = NX * PAIR
NDEV = NX * NZ
SLAB = HDIM // NZ
ROWS_DEV = 16
NROW = STEPS * ROWS_DEV
LAST = PROMPTS - 1

PART = PAIR * SLAB
S0 = 2 * PART
GIVE = S0 + PAIR * PROMPTS

BF = jnp.bfloat16
F32 = jnp.float32
HI = lax.Precision.HIGHEST

SMEM = pl.BlockSpec(memory_space=pltpu.SMEM)
VMEM = pl.BlockSpec(memory_space=pltpu.VMEM)


def params(mib=24):
    return pltpu.CompilerParams(vmem_limit_bytes=mib << 20)


def cost(us):
    return pl.CostEstimate(flops=int(us * 1e9), bytes_accessed=int(us * 3e6), transcendentals=0)


def bounds(lens):
    ends = []
    total = lens[0]
    for p in range(PROMPTS):
        if p:
            total = total + lens[p]
        ends.append(total)
    return ends


def seg_of(pos, ends):
    out = (pos >= ends[0]).astype(jnp.int32)
    for p in range(1, PROMPTS):
        out = out + (pos >= ends[p]).astype(jnp.int32)
    return out


def entry_seg(first, ends):
    return jnp.where(first > 0, seg_of(first - 1, ends), -1)


def cum_columns(logd):
    t = lax.broadcasted_iota(jnp.int32, (BLOCK, BLOCK), 0)
    s = lax.broadcasted_iota(jnp.int32, (BLOCK, BLOCK), 1)
    return lax.dot_general(
        (s <= t).astype(F32), logd, (((1,), (1,)), ((), ())), precision=HI, preferred_element_type=F32
    )


def contract_rows(a, b):
    return lax.dot_general(a, b, (((0,), (0,)), ((), ())), preferred_element_type=F32)


def contract_cols(a, b):
    return lax.dot_general(a, b, (((1,), (1,)), ((), ())), preferred_element_type=F32)


def send_kernel(lens, here, key_ref, value_ref, logd_ref, out_ref, flag_ref, cum_ref):
    first = here[0] * BLOCK
    ends = bounds(lens)
    front = entry_seg(first, ends)
    seg_last = seg_of(first + (BLOCK - 1), ends)
    cum = cum_columns(logd_ref[...])
    cum_ref[...] = cum
    tok = lax.broadcasted_iota(jnp.int32, (BLOCK, HEADS), 0)
    seg = seg_of(tok + first, ends)
    last = cum[BLOCK - 1 : BLOCK, :]
    keep = jnp.where(seg == seg_last, jnp.exp(last - cum), 0.0)
    factors = [jnp.exp(last) * (seg_last == front).astype(F32)]
    found = jnp.int32(-1)
    spot = jnp.int32(0)
    crowded = jnp.int32(0)
    for p in range(LAST):
        at = ends[p] - 1 - first
        inside = (at >= 0) & (at < BLOCK)
        reached = cum_ref[pl.ds(jnp.clip(at, 0, BLOCK - 1), 1), :]
        factors.append(jnp.exp(reached) * (inside & (front == p)).astype(F32))
        take = (at >= 0) & (at < BLOCK - 1) & (found < 0)
        found = jnp.where(take, p, found)
        spot = jnp.where(take, at, spot)
        if p:
            same = (ends[p] - 1) // BLOCK == (ends[p - 1] - 1) // BLOCK
            crowded = crowded | (same & (ends[p] % BLOCK != 0)).astype(jnp.int32)
    flag_ref[0] = crowded

    def emit(factor, row):
        for h in range(HEADS):
            x, j = h // PAIR, h % PAIR
            cols = slice(h * HDIM, (h + 1) * HDIM)
            keyed = (key_ref[:, cols].astype(F32) * factor[:, h : h + 1]).astype(BF)
            total = contract_rows(keyed, value_ref[:, cols])
            at = row + j * SLAB
            for z in range(NZ):
                out_ref[x * NZ + z, at : at + SLAB, :] = total[z * SLAB : (z + 1) * SLAB, :]

    emit(keep, 0)
    for x in range(NX):
        scal = jnp.concatenate(
            [
                jnp.broadcast_to(f[:, x * PAIR + j : x * PAIR + j + 1], (1, HDIM))
                for f in factors
                for j in range(PAIR)
            ],
            axis=0,
        )
        for z in range(NZ):
            out_ref[x * NZ + z, S0:GIVE, :] = scal

    @pl.when(found < 0)
    def _():
        out_ref[:, PART:S0, :] = jnp.zeros((NDEV, PART, HDIM), F32)

    @pl.when(found >= 0)
    def _():
        reached = cum_ref[pl.ds(spot, 1), :]
        taken = (tok <= spot) & (seg == found)
        emit(jnp.where(taken, jnp.exp(jnp.where(taken, reached - cum, 0.0)), 0.0), PART)


def query_kernel(here, rows, query_ref, *out_refs):
    x = here[0] // NZ
    r = lax.broadcasted_iota(jnp.int32, (NROW, HDIM), 0) % ROWS_DEV
    ids = jnp.zeros((NROW, HDIM), F32)
    for k in range(ROWS_DEV):
        ids = jnp.where(r == k, rows[k].astype(F32), ids)
    for d, out_ref in enumerate(out_refs):
        pair = lax.rem(x + d, NX)
        cols = pl.ds(pl.multiple_of(pair * (PAIR * HDIM), PAIR * HDIM), PAIR * HDIM)
        q = query_ref[:, :, cols].astype(F32).reshape(NROW, PAIR * HDIM)
        out_ref[:, : PAIR * HDIM] = q
        out_ref[:, PAIR * HDIM :] = ids


def intra_kernel(
    lens, here, query_ref, key_ref, value_ref, logd_ref, sq_ref, sk_ref, sv_ref, sd_ref,
    intra_ref, carried_ref, local_ref, scarried_ref,
):
    first = here[0] * BLOCK
    ends = bounds(lens)
    front = entry_seg(first, ends)
    logd = logd_ref[...]
    t = lax.broadcasted_iota(jnp.int32, (BLOCK, BLOCK), 0)
    s = lax.broadcasted_iota(jnp.int32, (BLOCK, BLOCK), 1)
    cum = cum_columns(logd)
    cum_rows = jnp.dot(logd, (t <= s).astype(F32), precision=HI, preferred_element_type=F32)
    linked = (s <= t) & (seg_of(t + first, ends) == seg_of(s + first, ends))
    tok = lax.broadcasted_iota(jnp.int32, (BLOCK, HEADS), 0)
    carried_ref[...] = jnp.where(seg_of(tok + first, ends) == front, jnp.exp(cum), 0.0)
    for h in range(HEADS):
        cols = slice(h * HDIM, (h + 1) * HDIM)
        scores = contract_cols(query_ref[:, cols], key_ref[:, cols])
        spread = cum[:, h : h + 1] - cum_rows[h : h + 1, :]
        factor = jnp.exp(jnp.where(linked, spread, -1e30))
        weights = (scores * factor).astype(BF)
        intra_ref[:, cols] = jnp.dot(weights, value_ref[:, cols], preferred_element_type=F32)

    n = STEPS * ROWS_DEV
    a = lax.broadcasted_iota(jnp.int32, (n, n), 0)
    b = lax.broadcasted_iota(jnp.int32, (n, n), 1)
    same = (b <= a) & ((a - b) % ROWS_DEV == 0)
    total = sd_ref[0]
    pieces = [total]
    for step in range(1, STEPS):
        total = total + sd_ref[step]
        pieces.append(total)
    scum_rows = jnp.concatenate(pieces, axis=1)
    scum = lax.dot_general(
        (a == b).astype(F32), scum_rows, (((1,), (1,)), ((), ())), precision=HI,
        preferred_element_type=F32,
    )
    scarried_ref[...] = jnp.exp(scum)
    for h in range(HEADS):
        cols = slice(h * HDIM, (h + 1) * HDIM)
        q = sq_ref[:, :, cols].reshape(n, HDIM)
        k = sk_ref[:, :, cols].reshape(n, HDIM)
        v = sv_ref[:, :, cols].reshape(n, HDIM)
        spread = scum[:, h : h + 1] - scum_rows[h : h + 1, :]
        weights = contract_cols(q, k) * jnp.exp(jnp.where(same, spread, -1e30))
        high = weights.astype(BF)
        low = (weights - high.astype(F32)).astype(BF)
        local_ref[:, cols] = jnp.dot(high, v, preferred_element_type=F32) + jnp.dot(
            low, v, preferred_element_type=F32
        )


def scan_kernel(lens, give_ref, extra_ref, entry_ref, slice_ref):
    ends = bounds(lens)
    states = [jnp.zeros((SLAB, HDIM), F32) for _ in range(PAIR)]
    for k in range(NDEV):
        for j in range(PAIR):
            rows = slice(j * SLAB, (j + 1) * SLAB)
            entry_ref[k, rows, :] = states[j]
            states[j] = give_ref[k, S0 + j : S0 + j + 1, :] * states[j] + give_ref[k, rows, :]
    for j in range(PAIR):
        slice_ref[LAST, j] = states[j]
    earlier = []
    for p in range(LAST):
        e = ends[p] - 1
        b = e // BLOCK
        slot = jnp.int32(0)
        for other in earlier:
            slot = slot + (other == b).astype(jnp.int32)
        earlier.append(b)
        whole = e % BLOCK == BLOCK - 1
        for j in range(PAIR):
            rows = slice(j * SLAB, (j + 1) * SLAB)
            at = S0 + (p + 1) * PAIR + j
            lead = give_ref[b, at : at + 1, :]
            tail = give_ref[b, PART + j * SLAB : PART + (j + 1) * SLAB, :]
            tail = jnp.where(slot == 0, tail, extra_ref[p, rows, :])
            tail = jnp.where(whole, give_ref[b, rows, :], tail)
            slice_ref[p, j] = lead * entry_ref[b, rows, :] + tail


def project_kernel(here, *refs):
    queries = refs[:NX]
    slabs = refs[NX : NX + NZ]
    outs = refs[NX + NZ : NX + NZ + NX]
    st_ref = refs[-1]
    z = lax.rem(here[0], NZ)
    for d, ref in enumerate(slabs):
        origin = lax.rem(z - d + NZ, NZ)
        for p in range(PROMPTS):
            at = pl.multiple_of(p * HDIM + origin * SLAB, SLAB)
            for j in range(PAIR):
                st_ref[j, pl.ds(at, SLAB), :] = ref[p, j]
    for j in range(PAIR):
        st = st_ref[j]
        high = st.astype(BF)
        low = (st - high.astype(F32)).astype(BF)
        cols = slice(j * HDIM, (j + 1) * HDIM)
        rows = []
        for ref in queries:
            q = ref[:, cols]
            ids = ref[:, PAIR * HDIM :]
            rows.append(
                jnp.concatenate(
                    [jnp.where(ids == float(p), q, 0.0).astype(BF) for p in range(PROMPTS)], axis=1
                )
            )
        wide = jnp.concatenate(rows, axis=0)
        res = jnp.dot(wide, high, preferred_element_type=F32) + jnp.dot(
            wide, low, preferred_element_type=F32
        )
        for d, ref in enumerate(outs):
            ref[:, cols] = res[d * NROW : (d + 1) * NROW, :]


def mixed_kernel(query_ref, back_ref, intra_ref, carried_ref, mixed_ref, sums_ref):
    acc = jnp.zeros((BLOCK, HDIM), F32)
    for h in range(HEADS):
        x, j = h // PAIR, h % PAIR
        cols = slice(h * HDIM, (h + 1) * HDIM)
        state = jnp.concatenate(
            [back_ref[x * NZ + z, j * SLAB : (j + 1) * SLAB, :] for z in range(NZ)], axis=0
        ).astype(BF)
        outer = jnp.dot(query_ref[:, cols], state, preferred_element_type=F32)
        mixed = intra_ref[:, cols] + outer * carried_ref[:, h : h + 1]
        mixed_ref[:, cols] = mixed
        acc = acc + mixed * mixed
    flat = jnp.sum(acc.T, axis=0, keepdims=True)
    sums_ref[...] = jnp.concatenate(
        [flat[:, :HDIM], flat[:, HDIM:], jnp.zeros((6, HDIM), F32)], axis=0
    )


def decode_kernel(here, o0, o1, o2, o3, local_ref, scarried_ref, sums_ref, dec_ref, send_ref, carry_ref):
    x = here[0] // NZ
    for d, ref in enumerate((o0, o1, o2, o3)):
        carry_ref[lax.rem(x + d, NX)] = ref[...]
    acc = jnp.zeros((NROW, HDIM), F32)
    for h in range(HEADS):
        cols = slice(h * HDIM, (h + 1) * HDIM)
        part = slice((h % PAIR) * HDIM, (h % PAIR + 1) * HDIM)
        dec = local_ref[:, cols] + carry_ref[h // PAIR, :, part] * scarried_ref[:, h : h + 1]
        dec_ref[:, cols] = dec
        acc = acc + dec * dec
    full = jnp.concatenate([acc, jnp.zeros((HDIM - NROW, HDIM), F32)], axis=0)
    flat = jnp.sum(full.T, axis=0, keepdims=True)
    both = jnp.concatenate([sums_ref[0:2, :], flat, jnp.zeros((5, HDIM), F32)], axis=0)
    for k in range(HEADS):
        send_ref[k] = both


def final_kernel(sums_ref, mixed_ref, dec_ref, gain_ref, attn_ref, out_ref):
    total = sums_ref[0]
    for k in range(1, HEADS):
        total = total + sums_ref[k]
    scale = lax.rsqrt(total / (HEAD_COUNT * HDIM) + EPSILON)
    gain = gain_ref[...]

    def column(row):
        return jnp.broadcast_to(scale[row : row + 1, :], (HDIM, HDIM)).T

    for half in range(2):
        part = slice(half * HDIM, (half + 1) * HDIM)
        col = column(half)
        for h in range(HEADS):
            cols = slice(h * HDIM, (h + 1) * HDIM)
            attn_ref[part, cols] = (mixed_ref[part, cols] * col * gain[:, cols]).astype(BF)
    col = column(2)
    for h in range(HEADS):
        cols = slice(h * HDIM, (h + 1) * HDIM)
        res = (dec_ref[:, cols] * col[: STEPS * ROWS_DEV, :] * gain[:, cols]).astype(BF)
        for step in range(STEPS):
            out_ref[step, :, cols] = res[step * ROWS_DEV : (step + 1) * ROWS_DEV, :]


def shape(*dims, dtype=F32):
    return jax.ShapeDtypeStruct(dims, dtype)


def shift(x, axis, size, d):
    return lax.ppermute(x, axis, [(i, (i + d) % size) for i in range(size)])


def exchange(x, axis):
    return lax.all_to_all(x, axis, split_axis=0, concat_axis=0, tiled=True)


def more_tails(key_in, value_in, log_decay, prompt_lengths, first):
    ends = jnp.cumsum(prompt_lengths)
    positions = first + jnp.arange(BLOCK, dtype=jnp.int32)
    segs = jnp.sum((positions[:, None] >= ends[None, :]).astype(jnp.int32), axis=1)
    cum = jnp.cumsum(log_decay, axis=0)
    keys = key_in.reshape(BLOCK, HEADS, HDIM)
    values = value_in.reshape(BLOCK, HEADS, HDIM)
    parts = []
    for p in (1, 2):
        local = ends[p] - 1 - first
        owned = (local >= 0) & (local < BLOCK) & (ends[p - 1] - 1 >= first)
        safe = jnp.clip(local, 0, BLOCK - 1)
        taken = (jnp.arange(BLOCK) <= safe) & (segs == p) & owned
        spread = jnp.where(taken[:, None], cum[safe][None, :] - cum, 0.0)
        keep = jnp.where(taken[:, None], jnp.exp(spread), 0.0)
        tailed = (keys.astype(F32) * keep[:, :, None]).astype(BF)
        part = jnp.einsum("shd,she->hde", tailed, values, preferred_element_type=F32)
        part = part.reshape(NX, PAIR, NZ, SLAB, HDIM).transpose(0, 2, 1, 3, 4)
        parts.append(part.reshape(NDEV, PART, HDIM))
    got = exchange(jnp.concatenate(parts, axis=1), SEQ)
    both = jnp.sum(got, axis=0)
    return jnp.stack([jnp.zeros((PART, HDIM), F32), both[:PART], both[PART:]])


def local(
    query_in,
    key_in,
    value_in,
    log_decay,
    norm_gain,
    prompt_lengths,
    step_query,
    step_key,
    step_value,
    step_decay,
    row_prompt,
):
    me = lax.axis_index(SEQ).astype(jnp.int32)
    here = me[None]
    width = HEADS * HDIM
    n = STEPS * ROWS_DEV

    logd = log_decay.T
    give, crowded = pl.pallas_call(
        send_kernel,
        out_shape=(shape(NDEV, GIVE, HDIM), shape(1, dtype=jnp.int32)),
        in_specs=[SMEM] * 2 + [VMEM] * 3,
        out_specs=(VMEM, SMEM),
        scratch_shapes=[pltpu.VMEM((BLOCK, HEADS), F32)],
        compiler_params=params(),
        cost_estimate=cost(3),
        name="send",
    )(prompt_lengths, here, key_in, value_in, logd)
    given = exchange(give, SEQ)

    queries = pl.pallas_call(
        query_kernel,
        out_shape=(shape(NROW, (PAIR + 1) * HDIM),) * NX,
        in_specs=[SMEM] * 2 + [VMEM],
        out_specs=(VMEM,) * NX,
        compiler_params=params(),
        cost_estimate=cost(1),
        name="query",
    )(here, row_prompt, step_query)
    queries = [queries[0]] + [shift(queries[d], "seq_0", NX, d) for d in range(1, NX)]

    intra, carried, local_dec, scarried = pl.pallas_call(
        intra_kernel,
        out_shape=(shape(BLOCK, width), shape(BLOCK, HEADS), shape(n, width), shape(n, HEADS)),
        in_specs=[SMEM] * 2 + [VMEM] * 8,
        out_specs=(VMEM,) * 4,
        compiler_params=params(),
        cost_estimate=cost(6),
        name="intra",
    )(
        prompt_lengths, here, query_in, key_in, value_in, logd,
        step_query, step_key, step_value, step_decay.transpose(0, 2, 1),
    )

    given, intra, carried, local_dec, scarried, queries, crowded = lax.optimization_barrier(
        (given, intra, carried, local_dec, scarried, queries, crowded)
    )
    extra = lax.cond(
        crowded[0] > 0,
        lambda: more_tails(key_in, value_in, log_decay, prompt_lengths, me * BLOCK),
        lambda: jnp.zeros((LAST, PART, HDIM), F32),
    )
    entry, own = pl.pallas_call(
        scan_kernel,
        out_shape=(shape(NDEV, PART, HDIM), shape(PROMPTS, PAIR, SLAB, HDIM)),
        in_specs=[SMEM] + [VMEM] * 2,
        out_specs=(VMEM,) * 2,
        compiler_params=params(),
        cost_estimate=cost(2),
        name="scan",
    )(prompt_lengths, given, extra)
    back = exchange(entry, SEQ)

    slabs = [own] * NZ
    for d in range(1, NZ // 2 + 1):
        slabs[d] = shift(slabs[d - 1], "seq_1", NZ, 1)
        if d < NZ // 2:
            slabs[NZ - d] = shift(slabs[(NZ - d + 1) % NZ], "seq_1", NZ, -1)
    products = pl.pallas_call(
        project_kernel,
        out_shape=(shape(NROW, PAIR * HDIM),) * NX,
        in_specs=[SMEM] + [VMEM] * (NX + NZ),
        out_specs=(VMEM,) * NX,
        scratch_shapes=[pltpu.VMEM((PAIR, PROMPTS * HDIM, HDIM), F32)],
        compiler_params=params(),
        cost_estimate=cost(2),
        name="project",
    )(here, *queries, *slabs)
    products = [products[0]] + [shift(products[d], "seq_0", NX, -d) for d in range(1, NX)]

    mixed, sums = pl.pallas_call(
        mixed_kernel,
        out_shape=(shape(BLOCK, width), shape(8, HDIM)),
        in_specs=[VMEM] * 4,
        out_specs=(VMEM,) * 2,
        compiler_params=params(),
        cost_estimate=cost(2),
        name="mixed",
    )(query_in, back, intra, carried)
    dec, sums_send = pl.pallas_call(
        decode_kernel,
        out_shape=(shape(n, width), shape(HEADS, 8, HDIM)),
        in_specs=[SMEM] + [VMEM] * 7,
        out_specs=(VMEM,) * 2,
        scratch_shapes=[pltpu.VMEM((NX, NROW, PAIR * HDIM), F32)],
        compiler_params=params(),
        cost_estimate=cost(1),
        name="decode",
    )(here, *products, local_dec, scarried, sums)
    sums_all = exchange(sums_send, "head")

    return pl.pallas_call(
        final_kernel,
        out_shape=(shape(BLOCK, width, dtype=BF), shape(STEPS, ROWS_DEV, width, dtype=BF)),
        in_specs=[VMEM] * 4,
        out_specs=(VMEM,) * 2,
        compiler_params=params(),
        cost_estimate=cost(2),
        name="final",
    )(sums_all, mixed, dec, norm_gain.reshape(1, width))


def solution(mesh):
    split = Mesh(mesh.devices.reshape(NX, NZ, mesh.shape["head"]), ("seq_0", "seq_1", "head"))
    placed = (
        P(SEQ, "head"),
        P(SEQ, "head"),
        P(SEQ, "head"),
        P(SEQ, "head"),
        P("head"),
        P(),
        P(None, SEQ, "head"),
        P(None, SEQ, "head"),
        P(None, SEQ, "head"),
        P(None, SEQ, "head"),
        P(SEQ),
    )
    return jax.shard_map(
        local,
        mesh=split,
        in_specs=placed,
        out_specs=(P(SEQ, "head"), P(None, SEQ, "head")),
        check_vma=False,
    )
```

```python
import functools

import jax
import jax.numpy as jnp
from jax import lax
from jax.experimental import pallas as pl
from jax.experimental.pallas import tpu as pltpu
from jax.sharding import Mesh
from jax.sharding import PartitionSpec as P

HEAD_COUNT = 64
HDIM = 128
BLOCK = 256
PROMPTS = 4
STEPS = 4
SEQ = ("seq_0", "seq_1")
EPSILON = 1e-06

NX = 4
NZ = 8
PAIR = 2
HEADS = NX * PAIR
NDEV = NX * NZ
SLAB = HDIM // NZ
ROWS_DEV = 16
NROW = STEPS * ROWS_DEV
LAST = PROMPTS - 1

PART = PAIR * SLAB
S0 = 2 * PART
GIVE = S0 + PAIR * PROMPTS

BF = jnp.bfloat16
F32 = jnp.float32
HI = lax.Precision.HIGHEST

SMEM = pl.BlockSpec(memory_space=pltpu.SMEM)
VMEM = pl.BlockSpec(memory_space=pltpu.VMEM)


def params(mib=24):
    return pltpu.CompilerParams(vmem_limit_bytes=mib << 20)


def cost(us):
    return pl.CostEstimate(flops=int(us * 1e9), bytes_accessed=int(us * 3e6), transcendentals=0)


def bounds(lens):
    ends = []
    total = lens[0]
    for p in range(PROMPTS):
        if p:
            total = total + lens[p]
        ends.append(total)
    return ends


def seg_of(pos, ends):
    out = (pos >= ends[0]).astype(jnp.int32)
    for p in range(1, PROMPTS):
        out = out + (pos >= ends[p]).astype(jnp.int32)
    return out


def entry_seg(first, ends):
    return jnp.where(first > 0, seg_of(first - 1, ends), -1)


def cum_columns(logd):
    t = lax.broadcasted_iota(jnp.int32, (BLOCK, BLOCK), 0)
    s = lax.broadcasted_iota(jnp.int32, (BLOCK, BLOCK), 1)
    return lax.dot_general(
        (s <= t).astype(F32), logd, (((1,), (1,)), ((), ())), precision=HI, preferred_element_type=F32
    )


def contract_rows(a, b):
    return lax.dot_general(a, b, (((0,), (0,)), ((), ())), preferred_element_type=F32)


def contract_cols(a, b):
    return lax.dot_general(a, b, (((1,), (1,)), ((), ())), preferred_element_type=F32)


def send_kernel(lens, here, key_ref, value_ref, logd_ref, out_ref, flag_ref, keep_ref, tail_ref, scal_ref):
    x = pl.program_id(0)
    first = here[0] * BLOCK
    ends = bounds(lens)
    front = entry_seg(first, ends)
    seg_last = seg_of(first + (BLOCK - 1), ends)
    found = jnp.int32(-1)
    spot = jnp.int32(0)
    crowded = jnp.int32(0)
    for p in range(LAST):
        at = ends[p] - 1 - first
        take = (at >= 0) & (at < BLOCK - 1) & (found < 0)
        found = jnp.where(take, p, found)
        spot = jnp.where(take, at, spot)
        if p:
            same = (ends[p] - 1) // BLOCK == (ends[p - 1] - 1) // BLOCK
            crowded = crowded | (same & (ends[p] % BLOCK != 0)).astype(jnp.int32)

    @pl.when(x == 0)
    def _():
        flag_ref[0] = crowded
        cum = cum_columns(logd_ref[...])
        tok = lax.broadcasted_iota(jnp.int32, (BLOCK, HEADS), 0)
        seg = seg_of(tok + first, ends)
        last = cum[BLOCK - 1 : BLOCK, :]
        keep = jnp.where(seg == seg_last, jnp.exp(last - cum), 0.0)
        tail_ref[0] = cum
        factors = [jnp.exp(last) * (seg_last == front).astype(F32)]
        for p in range(LAST):
            at = ends[p] - 1 - first
            inside = (at >= 0) & (at < BLOCK)
            reached = tail_ref[0, pl.ds(jnp.clip(at, 0, BLOCK - 1), 1), :]
            factors.append(jnp.exp(reached) * (inside & (front == p)).astype(F32))
        reached = tail_ref[0, pl.ds(spot, 1), :]
        taken = (tok <= spot) & (seg == found)
        tail = jnp.where(taken, jnp.exp(jnp.where(taken, reached - cum, 0.0)), 0.0)
        for k in range(NX):
            keep_ref[k] = keep[:, k * PAIR : (k + 1) * PAIR]
            tail_ref[k] = jnp.concatenate(
                [tail[:, k * PAIR : (k + 1) * PAIR]] * (HEADS // PAIR), axis=1
            )
            scal_ref[k] = jnp.concatenate(
                [
                    jnp.broadcast_to(f[:, k * PAIR + j : k * PAIR + j + 1], (1, HDIM))
                    for f in factors
                    for j in range(PAIR)
                ],
                axis=0,
            )

    def emit(factor, row):
        for j in range(PAIR):
            cols = slice(j * HDIM, (j + 1) * HDIM)
            keyed = (key_ref[:, cols].astype(F32) * factor[:, j : j + 1]).astype(BF)
            total = contract_rows(keyed, value_ref[:, cols])
            at = row + j * SLAB
            for z in range(NZ):
                out_ref[z, at : at + SLAB, :] = total[z * SLAB : (z + 1) * SLAB, :]

    emit(keep_ref[x], 0)
    scal = scal_ref[x]
    for z in range(NZ):
        out_ref[z, S0:GIVE, :] = scal

    @pl.when(found < 0)
    def _():
        out_ref[:, PART:S0, :] = jnp.zeros((NZ, PART, HDIM), F32)

    @pl.when(found >= 0)
    def _():
        emit(tail_ref[x], PART)


def query_kernel(here, rows, query_ref, *out_refs):
    x = here[0] // NZ
    r = lax.broadcasted_iota(jnp.int32, (NROW, HDIM), 0) % ROWS_DEV
    ids = jnp.zeros((NROW, HDIM), F32)
    for k in range(ROWS_DEV):
        ids = jnp.where(r == k, rows[k].astype(F32), ids)
    for d, out_ref in enumerate(out_refs):
        pair = lax.rem(x + d, NX)
        cols = pl.ds(pl.multiple_of(pair * (PAIR * HDIM), PAIR * HDIM), PAIR * HDIM)
        q = query_ref[:, :, cols].astype(F32).reshape(NROW, PAIR * HDIM)
        out_ref[:, : PAIR * HDIM] = q
        out_ref[:, PAIR * HDIM :] = ids


def intra_kernel(
    lens, here, query_ref, key_ref, value_ref, logd_ref, sq_ref, sk_ref, sv_ref, sd_ref,
    intra_ref, carried_ref, local_ref, scarried_ref,
):
    first = here[0] * BLOCK
    ends = bounds(lens)
    front = entry_seg(first, ends)
    logd = logd_ref[...]
    t = lax.broadcasted_iota(jnp.int32, (BLOCK, BLOCK), 0)
    s = lax.broadcasted_iota(jnp.int32, (BLOCK, BLOCK), 1)
    cum = cum_columns(logd)
    cum_rows = jnp.dot(logd, (t <= s).astype(F32), precision=HI, preferred_element_type=F32)
    linked = (s <= t) & (seg_of(t + first, ends) == seg_of(s + first, ends))
    tok = lax.broadcasted_iota(jnp.int32, (BLOCK, HEADS), 0)
    carried_ref[...] = jnp.where(seg_of(tok + first, ends) == front, jnp.exp(cum), 0.0)
    for h in range(HEADS):
        cols = slice(h * HDIM, (h + 1) * HDIM)
        scores = contract_cols(query_ref[:, cols], key_ref[:, cols])
        spread = cum[:, h : h + 1] - cum_rows[h : h + 1, :]
        factor = jnp.exp(jnp.where(linked, spread, -1e30))
        weights = (scores * factor).astype(BF)
        intra_ref[:, cols] = jnp.dot(weights, value_ref[:, cols], preferred_element_type=F32)

    n = STEPS * ROWS_DEV
    a = lax.broadcasted_iota(jnp.int32, (n, n), 0)
    b = lax.broadcasted_iota(jnp.int32, (n, n), 1)
    same = (b <= a) & ((a - b) % ROWS_DEV == 0)
    total = sd_ref[0]
    pieces = [total]
    for step in range(1, STEPS):
        total = total + sd_ref[step]
        pieces.append(total)
    scum_rows = jnp.concatenate(pieces, axis=1)
    scum = lax.dot_general(
        (a == b).astype(F32), scum_rows, (((1,), (1,)), ((), ())), precision=HI,
        preferred_element_type=F32,
    )
    scarried_ref[...] = jnp.exp(scum)
    for h in range(HEADS):
        cols = slice(h * HDIM, (h + 1) * HDIM)
        q = sq_ref[:, :, cols].reshape(n, HDIM)
        k = sk_ref[:, :, cols].reshape(n, HDIM)
        v = sv_ref[:, :, cols].reshape(n, HDIM)
        spread = scum[:, h : h + 1] - scum_rows[h : h + 1, :]
        weights = contract_cols(q, k) * jnp.exp(jnp.where(same, spread, -1e30))
        high = weights.astype(BF)
        low = (weights - high.astype(F32)).astype(BF)
        local_ref[:, cols] = jnp.dot(high, v, preferred_element_type=F32) + jnp.dot(
            low, v, preferred_element_type=F32
        )


def scan_kernel(lens, give_ref, extra_ref, entry_ref, slice_ref):
    ends = bounds(lens)
    states = [jnp.zeros((SLAB, HDIM), F32) for _ in range(PAIR)]
    for k in range(NDEV):
        for j in range(PAIR):
            rows = slice(j * SLAB, (j + 1) * SLAB)
            entry_ref[k, rows, :] = states[j]
            states[j] = give_ref[k, S0 + j : S0 + j + 1, :] * states[j] + give_ref[k, rows, :]
    for j in range(PAIR):
        slice_ref[LAST, j] = states[j]
    earlier = []
    for p in range(LAST):
        e = ends[p] - 1
        b = e // BLOCK
        slot = jnp.int32(0)
        for other in earlier:
            slot = slot + (other == b).astype(jnp.int32)
        earlier.append(b)
        whole = e % BLOCK == BLOCK - 1
        for j in range(PAIR):
            rows = slice(j * SLAB, (j + 1) * SLAB)
            at = S0 + (p + 1) * PAIR + j
            lead = give_ref[b, at : at + 1, :]
            tail = give_ref[b, PART + j * SLAB : PART + (j + 1) * SLAB, :]
            tail = jnp.where(slot == 0, tail, extra_ref[p, rows, :])
            tail = jnp.where(whole, give_ref[b, rows, :], tail)
            slice_ref[p, j] = lead * entry_ref[b, rows, :] + tail


def project_kernel(here, *refs):
    queries = refs[:NX]
    slabs = refs[NX : NX + NZ]
    outs = refs[NX + NZ : NX + NZ + NX]
    st_ref = refs[-1]
    z = lax.rem(here[0], NZ)
    for d, ref in enumerate(slabs):
        origin = lax.rem(z - d + NZ, NZ)
        for p in range(PROMPTS):
            at = pl.multiple_of(p * HDIM + origin * SLAB, SLAB)
            for j in range(PAIR):
                st_ref[j, pl.ds(at, SLAB), :] = ref[p, j]
    for j in range(PAIR):
        st = st_ref[j]
        high = st.astype(BF)
        low = (st - high.astype(F32)).astype(BF)
        cols = slice(j * HDIM, (j + 1) * HDIM)
        rows = []
        for ref in queries:
            q = ref[:, cols]
            ids = ref[:, PAIR * HDIM :]
            rows.append(
                jnp.concatenate(
                    [jnp.where(ids == float(p), q, 0.0).astype(BF) for p in range(PROMPTS)], axis=1
                )
            )
        wide = jnp.concatenate(rows, axis=0)
        res = jnp.dot(wide, high, preferred_element_type=F32) + jnp.dot(
            wide, low, preferred_element_type=F32
        )
        for d, ref in enumerate(outs):
            ref[:, cols] = res[d * NROW : (d + 1) * NROW, :]


def mixed_kernel(
    here, query_ref, back_ref, intra_ref, carried_ref, o0, o1, o2, o3, local_ref, scarried_ref,
    mixed_ref, dec_ref, send_ref, carry_ref,
):
    x = here[0] // NZ
    for d, ref in enumerate((o0, o1, o2, o3)):
        carry_ref[lax.rem(x + d, NX)] = ref[...]
    acc = jnp.zeros((NROW, HDIM), F32)
    for h in range(HEADS):
        cols = slice(h * HDIM, (h + 1) * HDIM)
        part = slice((h % PAIR) * HDIM, (h % PAIR + 1) * HDIM)
        dec = local_ref[:, cols] + carry_ref[h // PAIR, :, part] * scarried_ref[:, h : h + 1]
        dec_ref[:, cols] = dec
        acc = acc + dec * dec
    full = jnp.concatenate([acc, jnp.zeros((HDIM - NROW, HDIM), F32)], axis=0)
    dflat = jnp.sum(full.T, axis=0, keepdims=True)

    acc = jnp.zeros((BLOCK, HDIM), F32)
    for h in range(HEADS):
        x, j = h // PAIR, h % PAIR
        cols = slice(h * HDIM, (h + 1) * HDIM)
        state = jnp.concatenate(
            [back_ref[x * NZ + z, j * SLAB : (j + 1) * SLAB, :] for z in range(NZ)], axis=0
        ).astype(BF)
        outer = jnp.dot(query_ref[:, cols], state, preferred_element_type=F32)
        mixed = intra_ref[:, cols] + outer * carried_ref[:, h : h + 1]
        mixed_ref[:, cols] = mixed
        acc = acc + mixed * mixed
    flat = jnp.sum(acc.T, axis=0, keepdims=True)
    both = jnp.concatenate([flat[:, :HDIM], flat[:, HDIM:], dflat, dflat], axis=0)
    for k in range(HEADS):
        send_ref[k] = both


def final_kernel(sums_ref, mixed_ref, dec_ref, gain_ref, attn_ref, out_ref):
    total = sums_ref[0]
    for k in range(1, HEADS):
        total = total + sums_ref[k]
    scale = lax.rsqrt(total / (HEAD_COUNT * HDIM) + EPSILON)
    gain = gain_ref[...]

    def column(row):
        return jnp.broadcast_to(scale[row : row + 1, :], (HDIM, HDIM)).T

    for half in range(2):
        part = slice(half * HDIM, (half + 1) * HDIM)
        col = column(half)
        for h in range(HEADS):
            cols = slice(h * HDIM, (h + 1) * HDIM)
            attn_ref[part, cols] = (mixed_ref[part, cols] * col * gain[:, cols]).astype(BF)
    col = column(2)
    for h in range(HEADS):
        cols = slice(h * HDIM, (h + 1) * HDIM)
        res = (dec_ref[:, cols] * col[: STEPS * ROWS_DEV, :] * gain[:, cols]).astype(BF)
        for step in range(STEPS):
            out_ref[step, :, cols] = res[step * ROWS_DEV : (step + 1) * ROWS_DEV, :]


def shape(*dims, dtype=F32):
    return jax.ShapeDtypeStruct(dims, dtype)


def shift(x, axis, size, d):
    return lax.ppermute(x, axis, [(i, (i + d) % size) for i in range(size)])


def exchange(x, axis):
    return lax.all_to_all(x, axis, split_axis=0, concat_axis=0, tiled=True)


def more_tails(key_in, value_in, log_decay, prompt_lengths, first):
    ends = jnp.cumsum(prompt_lengths)
    positions = first + jnp.arange(BLOCK, dtype=jnp.int32)
    segs = jnp.sum((positions[:, None] >= ends[None, :]).astype(jnp.int32), axis=1)
    cum = jnp.cumsum(log_decay, axis=0)
    keys = key_in.reshape(BLOCK, HEADS, HDIM)
    values = value_in.reshape(BLOCK, HEADS, HDIM)
    parts = []
    for p in (1, 2):
        local = ends[p] - 1 - first
        owned = (local >= 0) & (local < BLOCK) & (ends[p - 1] - 1 >= first)
        safe = jnp.clip(local, 0, BLOCK - 1)
        taken = (jnp.arange(BLOCK) <= safe) & (segs == p) & owned
        spread = jnp.where(taken[:, None], cum[safe][None, :] - cum, 0.0)
        keep = jnp.where(taken[:, None], jnp.exp(spread), 0.0)
        tailed = (keys.astype(F32) * keep[:, :, None]).astype(BF)
        part = jnp.einsum("shd,she->hde", tailed, values, preferred_element_type=F32)
        part = part.reshape(NX, PAIR, NZ, SLAB, HDIM).transpose(0, 2, 1, 3, 4)
        parts.append(part.reshape(NDEV, PART, HDIM))
    got = exchange(jnp.concatenate(parts, axis=1), SEQ)
    both = jnp.sum(got, axis=0)
    return jnp.stack([jnp.zeros((PART, HDIM), F32), both[:PART], both[PART:]])


def local(
    query_in,
    key_in,
    value_in,
    log_decay,
    norm_gain,
    prompt_lengths,
    step_query,
    step_key,
    step_value,
    step_decay,
    row_prompt,
):
    me = lax.axis_index(SEQ).astype(jnp.int32)
    here = me[None]
    width = HEADS * HDIM
    n = STEPS * ROWS_DEV

    logd = log_decay.T
    pair = PAIR * HDIM
    give, crowded = pl.pallas_call(
        send_kernel,
        out_shape=(shape(NDEV, GIVE, HDIM), shape(1, dtype=jnp.int32)),
        grid=(NX,),
        in_specs=[
            SMEM,
            SMEM,
            pl.BlockSpec((BLOCK, pair), lambda i: (0, i)),
            pl.BlockSpec((BLOCK, pair), lambda i: (0, i)),
            pl.BlockSpec((HEADS, BLOCK), lambda i: (0, 0)),
        ],
        out_specs=(pl.BlockSpec((NZ, GIVE, HDIM), lambda i: (i, 0, 0)), SMEM),
        scratch_shapes=[
            pltpu.VMEM((NX, BLOCK, PAIR), F32),
            pltpu.VMEM((NX, BLOCK, HEADS), F32),
            pltpu.VMEM((NX, PAIR * PROMPTS, HDIM), F32),
        ],
        compiler_params=params(),
        cost_estimate=cost(3),
        name="send",
    )(prompt_lengths, here, key_in, value_in, logd)
    given = exchange(give, SEQ)

    queries = pl.pallas_call(
        query_kernel,
        out_shape=(shape(NROW, (PAIR + 1) * HDIM),) * NX,
        in_specs=[SMEM] * 2 + [VMEM],
        out_specs=(VMEM,) * NX,
        compiler_params=params(),
        cost_estimate=cost(1),
        name="query",
    )(here, row_prompt, step_query)
    queries = [queries[0]] + [shift(queries[d], "seq_0", NX, d) for d in range(1, NX)]

    intra, carried, local_dec, scarried = pl.pallas_call(
        intra_kernel,
        out_shape=(shape(BLOCK, width), shape(BLOCK, HEADS), shape(n, width), shape(n, HEADS)),
        in_specs=[SMEM] * 2 + [VMEM] * 8,
        out_specs=(VMEM,) * 4,
        compiler_params=params(),
        cost_estimate=cost(6),
        name="intra",
    )(
        prompt_lengths, here, query_in, key_in, value_in, logd,
        step_query, step_key, step_value, step_decay.transpose(0, 2, 1),
    )

    given, intra, carried, local_dec, scarried, queries, crowded = lax.optimization_barrier(
        (given, intra, carried, local_dec, scarried, queries, crowded)
    )
    extra = lax.cond(
        crowded[0] > 0,
        lambda: more_tails(key_in, value_in, log_decay, prompt_lengths, me * BLOCK),
        lambda: jnp.zeros((LAST, PART, HDIM), F32),
    )
    entry, own = pl.pallas_call(
        scan_kernel,
        out_shape=(shape(NDEV, PART, HDIM), shape(PROMPTS, PAIR, SLAB, HDIM)),
        in_specs=[SMEM] + [VMEM] * 2,
        out_specs=(VMEM,) * 2,
        compiler_params=params(),
        cost_estimate=cost(2),
        name="scan",
    )(prompt_lengths, given, extra)
    slabs = [own] * NZ
    for d in range(1, NZ // 2 + 1):
        slabs[d] = shift(slabs[d - 1], "seq_1", NZ, 1)
        if d < NZ // 2:
            slabs[NZ - d] = shift(slabs[(NZ - d + 1) % NZ], "seq_1", NZ, -1)
    entry, slabs = lax.optimization_barrier((entry, slabs))
    back = exchange(entry, SEQ)
    products = pl.pallas_call(
        project_kernel,
        out_shape=(shape(NROW, PAIR * HDIM),) * NX,
        in_specs=[SMEM] + [VMEM] * (NX + NZ),
        out_specs=(VMEM,) * NX,
        scratch_shapes=[pltpu.VMEM((PAIR, PROMPTS * HDIM, HDIM), F32)],
        compiler_params=params(),
        cost_estimate=cost(2),
        name="project",
    )(here, *queries, *slabs)
    products = [products[0]] + [shift(products[d], "seq_0", NX, -d) for d in range(1, NX)]

    mixed, dec, sums_send = pl.pallas_call(
        mixed_kernel,
        out_shape=(shape(BLOCK, width), shape(n, width), shape(HEADS, 4, HDIM)),
        in_specs=[SMEM] + [VMEM] * 10,
        out_specs=(VMEM,) * 3,
        scratch_shapes=[pltpu.VMEM((NX, NROW, PAIR * HDIM), F32)],
        compiler_params=params(),
        cost_estimate=cost(2),
        name="mixed",
    )(here, query_in, back, intra, carried, *products, local_dec, scarried)
    sums_all = exchange(sums_send, "head")

    return pl.pallas_call(
        final_kernel,
        out_shape=(shape(BLOCK, width, dtype=BF), shape(STEPS, ROWS_DEV, width, dtype=BF)),
        in_specs=[VMEM] * 4,
        out_specs=(VMEM,) * 2,
        compiler_params=params(),
        cost_estimate=cost(2),
        name="final",
    )(sums_all, mixed, dec, norm_gain.reshape(1, width))


def solution(mesh):
    split = Mesh(mesh.devices.reshape(NX, NZ, mesh.shape["head"]), ("seq_0", "seq_1", "head"))
    placed = (
        P(SEQ, "head"),
        P(SEQ, "head"),
        P(SEQ, "head"),
        P(SEQ, "head"),
        P("head"),
        P(),
        P(None, SEQ, "head"),
        P(None, SEQ, "head"),
        P(None, SEQ, "head"),
        P(None, SEQ, "head"),
        P(SEQ),
    )
    return jax.shard_map(
        local,
        mesh=split,
        in_specs=placed,
        out_specs=(P(SEQ, "head"), P(None, SEQ, "head")),
        check_vma=False,
    )
```

```python
import functools

import jax
import jax.numpy as jnp
from jax import lax
from jax.experimental import pallas as pl
from jax.experimental.pallas import tpu as pltpu
from jax.sharding import Mesh
from jax.sharding import PartitionSpec as P

HEAD_COUNT = 64
HDIM = 128
BLOCK = 256
PROMPTS = 4
STEPS = 4
SEQ = ("seq_0", "seq_1")
EPSILON = 1e-06

NX = 4
NZ = 8
HEADS = 8
NDEV = NX * NZ
NQ = NZ // 2
QUART = HDIM // NQ
ROWS_DEV = 16
NROW = STEPS * ROWS_DEV
LAST = PROMPTS - 1
MATES = [(dx, db) for db in range(2) for dx in range(NX)]

T0 = QUART
S0 = 2 * QUART
GIVE = S0 + 8

BF = jnp.bfloat16
F32 = jnp.float32
HI = lax.Precision.HIGHEST

SMEM = pl.BlockSpec(memory_space=pltpu.SMEM)
VMEM = pl.BlockSpec(memory_space=pltpu.VMEM)


def params(mib=24):
    return pltpu.CompilerParams(vmem_limit_bytes=mib << 20)


def cost(us):
    return pl.CostEstimate(flops=int(us * 1e9), bytes_accessed=int(us * 3e6), transcendentals=0)


def bounds(lens):
    ends = []
    total = lens[0]
    for p in range(PROMPTS):
        if p:
            total = total + lens[p]
        ends.append(total)
    return ends


def seg_of(pos, ends):
    out = (pos >= ends[0]).astype(jnp.int32)
    for p in range(1, PROMPTS):
        out = out + (pos >= ends[p]).astype(jnp.int32)
    return out


def entry_seg(first, ends):
    return jnp.where(first > 0, seg_of(first - 1, ends), -1)


def cum_columns(logd):
    t = lax.broadcasted_iota(jnp.int32, (BLOCK, BLOCK), 0)
    s = lax.broadcasted_iota(jnp.int32, (BLOCK, BLOCK), 1)
    return lax.dot_general(
        (s <= t).astype(F32), logd, (((1,), (1,)), ((), ())), precision=HI, preferred_element_type=F32
    )


def contract_rows(a, b):
    return lax.dot_general(a, b, (((0,), (0,)), ((), ())), preferred_element_type=F32)


def contract_cols(a, b):
    return lax.dot_general(a, b, (((1,), (1,)), ((), ())), preferred_element_type=F32)


def owner(head, quarter):
    return (head // 2) * NZ + 2 * quarter + head % 2


def send_kernel(lens, here, key_ref, value_ref, logd_ref, out_ref, flag_ref, cum_ref):
    first = here[0] * BLOCK
    ends = bounds(lens)
    front = entry_seg(first, ends)
    seg_last = seg_of(first + (BLOCK - 1), ends)
    cum = cum_columns(logd_ref[...])
    cum_ref[...] = cum
    tok = lax.broadcasted_iota(jnp.int32, (BLOCK, HEADS), 0)
    seg = seg_of(tok + first, ends)
    last = cum[BLOCK - 1 : BLOCK, :]
    keep = jnp.where(seg == seg_last, jnp.exp(last - cum), 0.0)
    factors = [jnp.exp(last) * (seg_last == front).astype(F32)]
    found = jnp.int32(-1)
    spot = jnp.int32(0)
    crowded = jnp.int32(0)
    for p in range(LAST):
        at = ends[p] - 1 - first
        inside = (at >= 0) & (at < BLOCK)
        reached = cum_ref[pl.ds(jnp.clip(at, 0, BLOCK - 1), 1), :]
        factors.append(jnp.exp(reached) * (inside & (front == p)).astype(F32))
        take = (at >= 0) & (at < BLOCK - 1) & (found < 0)
        found = jnp.where(take, p, found)
        spot = jnp.where(take, at, spot)
        if p:
            same = (ends[p] - 1) // BLOCK == (ends[p - 1] - 1) // BLOCK
            crowded = crowded | (same & (ends[p] % BLOCK != 0)).astype(jnp.int32)
    flag_ref[0] = crowded

    def emit(factor, row):
        for h in range(HEADS):
            cols = slice(h * HDIM, (h + 1) * HDIM)
            keyed = (key_ref[:, cols].astype(F32) * factor[:, h : h + 1]).astype(BF)
            total = contract_rows(keyed, value_ref[:, cols])
            for g in range(NQ):
                out_ref[owner(h, g), row : row + QUART, :] = total[g * QUART : (g + 1) * QUART, :]

    emit(keep, 0)
    for h in range(HEADS):
        scal = jnp.concatenate(
            [jnp.broadcast_to(f[:, h : h + 1], (1, HDIM)) for f in factors]
            + [jnp.zeros((8 - len(factors), HDIM), F32)],
            axis=0,
        )
        for g in range(NQ):
            out_ref[owner(h, g), S0:GIVE, :] = scal

    @pl.when(found < 0)
    def _():
        out_ref[:, T0:S0, :] = jnp.zeros((NDEV, QUART, HDIM), F32)

    @pl.when(found >= 0)
    def _():
        reached = cum_ref[pl.ds(spot, 1), :]
        taken = (tok <= spot) & (seg == found)
        emit(jnp.where(taken, jnp.exp(jnp.where(taken, reached - cum, 0.0)), 0.0), T0)


def mate_head(here, dx, db):
    x = here[0] // NZ
    parity = lax.rem(here[0], 2)
    return 2 * lax.rem(x + dx, NX) + (1 - parity if db else parity)


def query_kernel(here, rows, query_ref, *out_refs):
    r = lax.broadcasted_iota(jnp.int32, (NROW, HDIM), 0) % ROWS_DEV
    ids = jnp.zeros((NROW, HDIM), F32)
    for k in range(ROWS_DEV):
        ids = jnp.where(r == k, rows[k].astype(F32), ids)
    for (dx, db), out_ref in zip(MATES, out_refs):
        cols = pl.ds(pl.multiple_of(mate_head(here, dx, db) * HDIM, HDIM), HDIM)
        out_ref[:, :HDIM] = query_ref[:, :, cols].astype(F32).reshape(NROW, HDIM)
        out_ref[:, HDIM:] = ids


def intra_kernel(
    lens, here, query_ref, key_ref, value_ref, logd_ref, sq_ref, sk_ref, sv_ref, sd_ref,
    intra_ref, carried_ref, local_ref, scarried_ref,
):
    first = here[0] * BLOCK
    ends = bounds(lens)
    front = entry_seg(first, ends)
    logd = logd_ref[...]
    t = lax.broadcasted_iota(jnp.int32, (BLOCK, BLOCK), 0)
    s = lax.broadcasted_iota(jnp.int32, (BLOCK, BLOCK), 1)
    cum = cum_columns(logd)
    cum_rows = jnp.dot(logd, (t <= s).astype(F32), precision=HI, preferred_element_type=F32)
    linked = (s <= t) & (seg_of(t + first, ends) == seg_of(s + first, ends))
    tok = lax.broadcasted_iota(jnp.int32, (BLOCK, HEADS), 0)
    carried_ref[...] = jnp.where(seg_of(tok + first, ends) == front, jnp.exp(cum), 0.0)
    for h in range(HEADS):
        cols = slice(h * HDIM, (h + 1) * HDIM)
        scores = contract_cols(query_ref[:, cols], key_ref[:, cols])
        spread = cum[:, h : h + 1] - cum_rows[h : h + 1, :]
        factor = jnp.exp(jnp.where(linked, spread, -1e30))
        weights = (scores * factor).astype(BF)
        intra_ref[:, cols] = jnp.dot(weights, value_ref[:, cols], preferred_element_type=F32)

    n = STEPS * ROWS_DEV
    a = lax.broadcasted_iota(jnp.int32, (n, n), 0)
    b = lax.broadcasted_iota(jnp.int32, (n, n), 1)
    same = (b <= a) & ((a - b) % ROWS_DEV == 0)
    total = sd_ref[0]
    pieces = [total]
    for step in range(1, STEPS):
        total = total + sd_ref[step]
        pieces.append(total)
    scum_rows = jnp.concatenate(pieces, axis=1)
    scum = lax.dot_general(
        (a == b).astype(F32), scum_rows, (((1,), (1,)), ((), ())), precision=HI,
        preferred_element_type=F32,
    )
    scarried_ref[...] = jnp.exp(scum)
    for h in range(HEADS):
        cols = slice(h * HDIM, (h + 1) * HDIM)
        q = sq_ref[:, :, cols].reshape(n, HDIM)
        k = sk_ref[:, :, cols].reshape(n, HDIM)
        v = sv_ref[:, :, cols].reshape(n, HDIM)
        spread = scum[:, h : h + 1] - scum_rows[h : h + 1, :]
        weights = contract_cols(q, k) * jnp.exp(jnp.where(same, spread, -1e30))
        high = weights.astype(BF)
        low = (weights - high.astype(F32)).astype(BF)
        local_ref[:, cols] = jnp.dot(high, v, preferred_element_type=F32) + jnp.dot(
            low, v, preferred_element_type=F32
        )


def scan_kernel(lens, give_ref, extra_ref, entry_ref, slice_ref):
    ends = bounds(lens)
    state = jnp.zeros((QUART, HDIM), F32)
    for k in range(NDEV):
        entry_ref[k] = state
        state = give_ref[k, S0 : S0 + 1, :] * state + give_ref[k, 0:T0, :]
    slice_ref[LAST] = state
    earlier = []
    for p in range(LAST):
        e = ends[p] - 1
        b = e // BLOCK
        slot = jnp.int32(0)
        for other in earlier:
            slot = slot + (other == b).astype(jnp.int32)
        earlier.append(b)
        whole = e % BLOCK == BLOCK - 1
        lead = give_ref[b, S0 + 1 + p : S0 + 2 + p, :]
        tail = jnp.where(slot == 0, give_ref[b, T0:S0, :], extra_ref[p])
        tail = jnp.where(whole, give_ref[b, 0:T0, :], tail)
        slice_ref[p] = lead * entry_ref[b] + tail


def project_kernel(here, *refs):
    n = len(MATES)
    queries, slabs, outs, st_ref = refs[:n], refs[n : n + NQ], refs[n + NQ : 2 * n + NQ], refs[-1]
    quarter = lax.rem(here[0], NZ) // 2
    for d, ref in enumerate(slabs):
        origin = lax.rem(quarter - d + NQ, NQ)
        for p in range(PROMPTS):
            at = pl.multiple_of(p * HDIM + origin * QUART, QUART)
            st_ref[pl.ds(at, QUART), :] = ref[p]
    st = st_ref[...]
    high = st.astype(BF)
    low = (st - high.astype(F32)).astype(BF)
    rows = []
    for ref in queries:
        q = ref[:, :HDIM]
        ids = ref[:, HDIM:]
        rows.append(
            jnp.concatenate(
                [jnp.where(ids == float(p), q, 0.0).astype(BF) for p in range(PROMPTS)], axis=1
            )
        )
    wide = jnp.concatenate(rows, axis=0)
    res = jnp.dot(wide, high, preferred_element_type=F32) + jnp.dot(
        wide, low, preferred_element_type=F32
    )
    for d, ref in enumerate(outs):
        ref[...] = res[d * NROW : (d + 1) * NROW, :]


def mixed_kernel(here, query_ref, back_ref, intra_ref, carried_ref, local_ref, scarried_ref, *refs):
    products = refs[: len(MATES)]
    mixed_ref, dec_ref, send_ref, carry_ref = refs[len(MATES) :]
    for (dx, db), ref in zip(MATES, products):
        carry_ref[mate_head(here, dx, db)] = ref[...]
    acc = jnp.zeros((NROW, HDIM), F32)
    for h in range(HEADS):
        cols = slice(h * HDIM, (h + 1) * HDIM)
        dec = local_ref[:, cols] + carry_ref[h] * scarried_ref[:, h : h + 1]
        dec_ref[:, cols] = dec
        acc = acc + dec * dec
    full = jnp.concatenate([acc, jnp.zeros((HDIM - NROW, HDIM), F32)], axis=0)
    dflat = jnp.sum(full.T, axis=0, keepdims=True)

    acc = jnp.zeros((BLOCK, HDIM), F32)
    for h in range(HEADS):
        cols = slice(h * HDIM, (h + 1) * HDIM)
        state = jnp.concatenate([back_ref[owner(h, g)] for g in range(NQ)], axis=0).astype(BF)
        outer = jnp.dot(query_ref[:, cols], state, preferred_element_type=F32)
        mixed = intra_ref[:, cols] + outer * carried_ref[:, h : h + 1]
        mixed_ref[:, cols] = mixed
        acc = acc + mixed * mixed
    flat = jnp.sum(acc.T, axis=0, keepdims=True)
    both = jnp.concatenate([flat[:, :HDIM], flat[:, HDIM:], dflat, dflat], axis=0)
    for k in range(HEADS):
        send_ref[k] = both


def final_kernel(sums_ref, mixed_ref, dec_ref, gain_ref, attn_ref, out_ref):
    total = sums_ref[0]
    for k in range(1, HEADS):
        total = total + sums_ref[k]
    scale = lax.rsqrt(total / (HEAD_COUNT * HDIM) + EPSILON)
    gain = gain_ref[...]

    def column(row):
        return jnp.broadcast_to(scale[row : row + 1, :], (HDIM, HDIM)).T

    for half in range(2):
        part = slice(half * HDIM, (half + 1) * HDIM)
        col = column(half)
        for h in range(HEADS):
            cols = slice(h * HDIM, (h + 1) * HDIM)
            attn_ref[part, cols] = (mixed_ref[part, cols] * col * gain[:, cols]).astype(BF)
    col = column(2)
    for h in range(HEADS):
        cols = slice(h * HDIM, (h + 1) * HDIM)
        res = (dec_ref[:, cols] * col[: STEPS * ROWS_DEV, :] * gain[:, cols]).astype(BF)
        for step in range(STEPS):
            out_ref[step, :, cols] = res[step * ROWS_DEV : (step + 1) * ROWS_DEV, :]


def shape(*dims, dtype=F32):
    return jax.ShapeDtypeStruct(dims, dtype)


def shift(x, axis, size, d):
    return lax.ppermute(x, axis, [(i, (i + d) % size) for i in range(size)])


def to_mate(x, dx, db):
    moves = []
    for i in range(NDEV):
        there = (i // NZ + dx) % NX * NZ + (i % NZ ^ db)
        moves.append((i, there))
    return lax.ppermute(x, SEQ, moves)


def exchange(x, axis):
    return lax.all_to_all(x, axis, split_axis=0, concat_axis=0, tiled=True)


def more_tails(key_in, value_in, log_decay, prompt_lengths, first):
    ends = jnp.cumsum(prompt_lengths)
    positions = first + jnp.arange(BLOCK, dtype=jnp.int32)
    segs = jnp.sum((positions[:, None] >= ends[None, :]).astype(jnp.int32), axis=1)
    cum = jnp.cumsum(log_decay, axis=0)
    keys = key_in.reshape(BLOCK, HEADS, HDIM)
    values = value_in.reshape(BLOCK, HEADS, HDIM)
    parts = []
    for p in (1, 2):
        local = ends[p] - 1 - first
        owned = (local >= 0) & (local < BLOCK) & (ends[p - 1] - 1 >= first)
        safe = jnp.clip(local, 0, BLOCK - 1)
        taken = (jnp.arange(BLOCK) <= safe) & (segs == p) & owned
        spread = jnp.where(taken[:, None], cum[safe][None, :] - cum, 0.0)
        keep = jnp.where(taken[:, None], jnp.exp(spread), 0.0)
        tailed = (keys.astype(F32) * keep[:, :, None]).astype(BF)
        part = jnp.einsum("shd,she->hde", tailed, values, preferred_element_type=F32)
        part = part.reshape(NX, 2, NQ, QUART, HDIM).transpose(0, 2, 1, 3, 4)
        parts.append(part.reshape(NDEV, QUART, HDIM))
    got = exchange(jnp.concatenate(parts, axis=1), SEQ)
    both = jnp.sum(got, axis=0)
    return jnp.stack([jnp.zeros((QUART, HDIM), F32), both[:QUART], both[QUART:]])


def local(
    query_in,
    key_in,
    value_in,
    log_decay,
    norm_gain,
    prompt_lengths,
    step_query,
    step_key,
    step_value,
    step_decay,
    row_prompt,
):
    me = lax.axis_index(SEQ).astype(jnp.int32)
    here = me[None]
    width = HEADS * HDIM
    n = STEPS * ROWS_DEV

    logd = log_decay.T
    give, crowded = pl.pallas_call(
        send_kernel,
        out_shape=(shape(NDEV, GIVE, HDIM), shape(1, dtype=jnp.int32)),
        in_specs=[SMEM] * 2 + [VMEM] * 3,
        out_specs=(VMEM, SMEM),
        scratch_shapes=[pltpu.VMEM((BLOCK, HEADS), F32)],
        compiler_params=params(),
        cost_estimate=cost(3),
        name="send",
    )(prompt_lengths, here, key_in, value_in, logd)
    given = exchange(give, SEQ)

    queries = pl.pallas_call(
        query_kernel,
        out_shape=(shape(NROW, 2 * HDIM),) * len(MATES),
        in_specs=[SMEM] * 2 + [VMEM],
        out_specs=(VMEM,) * len(MATES),
        compiler_params=params(),
        cost_estimate=cost(1),
        name="query",
    )(here, row_prompt, step_query)
    queries = [queries[0]] + [to_mate(q, dx, db) for q, (dx, db) in zip(queries[1:], MATES[1:])]

    intra, carried, local_dec, scarried = pl.pallas_call(
        intra_kernel,
        out_shape=(shape(BLOCK, width), shape(BLOCK, HEADS), shape(n, width), shape(n, HEADS)),
        in_specs=[SMEM] * 2 + [VMEM] * 8,
        out_specs=(VMEM,) * 4,
        compiler_params=params(),
        cost_estimate=cost(6),
        name="intra",
    )(
        prompt_lengths, here, query_in, key_in, value_in, logd,
        step_query, step_key, step_value, step_decay.transpose(0, 2, 1),
    )

    given, intra, carried, local_dec, scarried, queries, crowded = lax.optimization_barrier(
        (given, intra, carried, local_dec, scarried, queries, crowded)
    )
    extra = lax.cond(
        crowded[0] > 0,
        lambda: more_tails(key_in, value_in, log_decay, prompt_lengths, me * BLOCK),
        lambda: jnp.zeros((LAST, QUART, HDIM), F32),
    )
    entry, own = pl.pallas_call(
        scan_kernel,
        out_shape=(shape(NDEV, QUART, HDIM), shape(PROMPTS, QUART, HDIM)),
        in_specs=[SMEM] + [VMEM] * 2,
        out_specs=(VMEM,) * 2,
        compiler_params=params(),
        cost_estimate=cost(2),
        name="scan",
    )(prompt_lengths, given, extra)
    slabs = [own] + [shift(own, "seq_1", NZ, 2 * d) for d in range(1, NQ)]
    entry, slabs = lax.optimization_barrier((entry, slabs))
    back = exchange(entry, SEQ)

    products = pl.pallas_call(
        project_kernel,
        out_shape=(shape(NROW, HDIM),) * len(MATES),
        in_specs=[SMEM] + [VMEM] * (len(MATES) + NQ),
        out_specs=(VMEM,) * len(MATES),
        scratch_shapes=[pltpu.VMEM((PROMPTS * HDIM, HDIM), F32)],
        compiler_params=params(),
        cost_estimate=cost(2),
        name="project",
    )(here, *queries, *slabs)
    products = [products[0]] + [to_mate(q, -dx, db) for q, (dx, db) in zip(products[1:], MATES[1:])]

    mixed, dec, sums_send = pl.pallas_call(
        mixed_kernel,
        out_shape=(shape(BLOCK, width), shape(n, width), shape(HEADS, 4, HDIM)),
        in_specs=[SMEM] + [VMEM] * (6 + len(MATES)),
        out_specs=(VMEM,) * 3,
        scratch_shapes=[pltpu.VMEM((HEADS, NROW, HDIM), F32)],
        compiler_params=params(),
        cost_estimate=cost(2),
        name="mixed",
    )(here, query_in, back, intra, carried, local_dec, scarried, *products)
    sums_all = exchange(sums_send, "head")

    return pl.pallas_call(
        final_kernel,
        out_shape=(shape(BLOCK, width, dtype=BF), shape(STEPS, ROWS_DEV, width, dtype=BF)),
        in_specs=[VMEM] * 4,
        out_specs=(VMEM,) * 2,
        compiler_params=params(),
        cost_estimate=cost(2),
        name="final",
    )(sums_all, mixed, dec, norm_gain.reshape(1, width))


def solution(mesh):
    split = Mesh(mesh.devices.reshape(NX, NZ, mesh.shape["head"]), ("seq_0", "seq_1", "head"))
    placed = (
        P(SEQ, "head"),
        P(SEQ, "head"),
        P(SEQ, "head"),
        P(SEQ, "head"),
        P("head"),
        P(),
        P(None, SEQ, "head"),
        P(None, SEQ, "head"),
        P(None, SEQ, "head"),
        P(None, SEQ, "head"),
        P(SEQ),
    )
    return jax.shard_map(
        local,
        mesh=split,
        in_specs=placed,
        out_specs=(P(SEQ, "head"), P(None, SEQ, "head")),
        check_vma=False,
    )
```

```python
import functools

import jax
import jax.numpy as jnp
from jax import lax
from jax.experimental import pallas as pl
from jax.experimental.pallas import tpu as pltpu
from jax.sharding import Mesh
from jax.sharding import PartitionSpec as P

HEAD_COUNT = 64
HDIM = 128
BLOCK = 256
PROMPTS = 4
STEPS = 4
SEQ = ("seq_0", "seq_1")
EPSILON = 1e-06

NX = 4
NZ = 8
HEADS = 8
NDEV = NX * NZ
NQ = NZ // 2
QUART = HDIM // NQ
ROWS_DEV = 16
NROW = STEPS * ROWS_DEV
LAST = PROMPTS - 1
ASK = NROW + 8

T0 = QUART
S0 = 2 * QUART
GIVE = S0 + 8

BF = jnp.bfloat16
F32 = jnp.float32
HI = lax.Precision.HIGHEST

SMEM = pl.BlockSpec(memory_space=pltpu.SMEM)
VMEM = pl.BlockSpec(memory_space=pltpu.VMEM)


def params(mib=12):
    return pltpu.CompilerParams(vmem_limit_bytes=mib << 20)


def cost(us):
    return pl.CostEstimate(flops=int(us * 1e9), bytes_accessed=int(us * 3e6), transcendentals=0)


def bounds(lens):
    ends = []
    total = lens[0]
    for p in range(PROMPTS):
        if p:
            total = total + lens[p]
        ends.append(total)
    return ends


def seg_of(pos, ends):
    out = (pos >= ends[0]).astype(jnp.int32)
    for p in range(1, PROMPTS):
        out = out + (pos >= ends[p]).astype(jnp.int32)
    return out


def entry_seg(first, ends):
    return jnp.where(first > 0, seg_of(first - 1, ends), -1)


def cum_columns(logd):
    t = lax.broadcasted_iota(jnp.int32, (BLOCK, BLOCK), 0)
    s = lax.broadcasted_iota(jnp.int32, (BLOCK, BLOCK), 1)
    return lax.dot_general(
        (s <= t).astype(F32), logd, (((1,), (1,)), ((), ())), precision=HI, preferred_element_type=F32
    )


def contract_rows(a, b):
    return lax.dot_general(a, b, (((0,), (0,)), ((), ())), preferred_element_type=F32)


def contract_cols(a, b):
    return lax.dot_general(a, b, (((1,), (1,)), ((), ())), preferred_element_type=F32)


def owner(head, quarter):
    return (head // 2) * NZ + 2 * quarter + head % 2


def send_kernel(lens, here, key_ref, value_ref, logd_ref, out_ref, flag_ref, cum_ref):
    first = here[0] * BLOCK
    ends = bounds(lens)
    front = entry_seg(first, ends)
    seg_last = seg_of(first + (BLOCK - 1), ends)
    cum = cum_columns(logd_ref[...])
    cum_ref[...] = cum
    tok = lax.broadcasted_iota(jnp.int32, (BLOCK, HEADS), 0)
    seg = seg_of(tok + first, ends)
    last = cum[BLOCK - 1 : BLOCK, :]
    keep = jnp.where(seg == seg_last, jnp.exp(last - cum), 0.0)
    factors = [jnp.exp(last) * (seg_last == front).astype(F32)]
    found = jnp.int32(-1)
    spot = jnp.int32(0)
    crowded = jnp.int32(0)
    for p in range(LAST):
        at = ends[p] - 1 - first
        inside = (at >= 0) & (at < BLOCK)
        reached = cum_ref[pl.ds(jnp.clip(at, 0, BLOCK - 1), 1), :]
        factors.append(jnp.exp(reached) * (inside & (front == p)).astype(F32))
        take = (at >= 0) & (at < BLOCK - 1) & (found < 0)
        found = jnp.where(take, p, found)
        spot = jnp.where(take, at, spot)
        if p:
            same = (ends[p] - 1) // BLOCK == (ends[p - 1] - 1) // BLOCK
            crowded = crowded | (same & (ends[p] % BLOCK != 0)).astype(jnp.int32)
    flag_ref[0] = crowded

    def emit(factor, row):
        for h in range(HEADS):
            cols = slice(h * HDIM, (h + 1) * HDIM)
            keyed = (key_ref[:, cols].astype(F32) * factor[:, h : h + 1]).astype(BF)
            total = contract_rows(keyed, value_ref[:, cols])
            for g in range(NQ):
                out_ref[owner(h, g), row : row + QUART, :] = total[g * QUART : (g + 1) * QUART, :]

    emit(keep, 0)
    for h in range(HEADS):
        scal = jnp.concatenate(
            [jnp.broadcast_to(f[:, h : h + 1], (1, HDIM)) for f in factors]
            + [jnp.zeros((8 - len(factors), HDIM), F32)],
            axis=0,
        )
        for g in range(NQ):
            out_ref[owner(h, g), S0:GIVE, :] = scal

    @pl.when(found < 0)
    def _():
        out_ref[:, T0:S0, :] = jnp.zeros((NDEV, QUART, HDIM), F32)

    @pl.when(found >= 0)
    def _():
        reached = cum_ref[pl.ds(spot, 1), :]
        taken = (tok <= spot) & (seg == found)
        emit(jnp.where(taken, jnp.exp(jnp.where(taken, reached - cum, 0.0)), 0.0), T0)


def mate_head(here, dx, db):
    x = here[0] // NZ
    parity = lax.rem(here[0], 2)
    return 2 * lax.rem(x + dx, NX) + (1 - parity if db else parity)


def query_kernel(here, rows, query_ref, *out_refs):
    lane = lax.broadcasted_iota(jnp.int32, (8, HDIM), 1)
    ids = jnp.zeros((8, HDIM), F32)
    for k in range(ROWS_DEV):
        ids = jnp.where(lane == k, rows[k].astype(F32), ids)
    for dx, out_ref in enumerate(out_refs):
        for db in range(2):
            cols = pl.ds(pl.multiple_of(mate_head(here, dx, db) * HDIM, HDIM), HDIM)
            out_ref[db, :NROW, :] = query_ref[:, :, cols].astype(F32).reshape(NROW, HDIM)
            out_ref[db, NROW:, :] = ids


def intra_kernel(
    lens, here, query_ref, key_ref, value_ref, logd_ref, sq_ref, sk_ref, sv_ref, sd_ref,
    intra_ref, carried_ref, local_ref, scarried_ref,
):
    first = here[0] * BLOCK
    ends = bounds(lens)
    front = entry_seg(first, ends)
    logd = logd_ref[...]
    t = lax.broadcasted_iota(jnp.int32, (BLOCK, BLOCK), 0)
    s = lax.broadcasted_iota(jnp.int32, (BLOCK, BLOCK), 1)
    cum = cum_columns(logd)
    cum_rows = jnp.dot(logd, (t <= s).astype(F32), precision=HI, preferred_element_type=F32)
    linked = (s <= t) & (seg_of(t + first, ends) == seg_of(s + first, ends))
    tok = lax.broadcasted_iota(jnp.int32, (BLOCK, HEADS), 0)
    carried_ref[...] = jnp.where(seg_of(tok + first, ends) == front, jnp.exp(cum), 0.0)
    for h in range(HEADS):
        cols = slice(h * HDIM, (h + 1) * HDIM)
        scores = contract_cols(query_ref[:, cols], key_ref[:, cols])
        spread = cum[:, h : h + 1] - cum_rows[h : h + 1, :]
        factor = jnp.exp(jnp.where(linked, spread, -1e30))
        weights = (scores * factor).astype(BF)
        intra_ref[:, cols] = jnp.dot(weights, value_ref[:, cols], preferred_element_type=F32)

    n = STEPS * ROWS_DEV
    a = lax.broadcasted_iota(jnp.int32, (n, n), 0)
    b = lax.broadcasted_iota(jnp.int32, (n, n), 1)
    same = (b <= a) & ((a - b) % ROWS_DEV == 0)
    total = sd_ref[0]
    pieces = [total]
    for step in range(1, STEPS):
        total = total + sd_ref[step]
        pieces.append(total)
    scum_rows = jnp.concatenate(pieces, axis=1)
    scum = lax.dot_general(
        (a == b).astype(F32), scum_rows, (((1,), (1,)), ((), ())), precision=HI,
        preferred_element_type=F32,
    )
    scarried_ref[...] = jnp.exp(scum)
    for h in range(HEADS):
        cols = slice(h * HDIM, (h + 1) * HDIM)
        q = sq_ref[:, :, cols].reshape(n, HDIM)
        k = sk_ref[:, :, cols].reshape(n, HDIM)
        v = sv_ref[:, :, cols].reshape(n, HDIM)
        spread = scum[:, h : h + 1] - scum_rows[h : h + 1, :]
        weights = contract_cols(q, k) * jnp.exp(jnp.where(same, spread, -1e30))
        high = weights.astype(BF)
        low = (weights - high.astype(F32)).astype(BF)
        local_ref[:, cols] = jnp.dot(high, v, preferred_element_type=F32) + jnp.dot(
            low, v, preferred_element_type=F32
        )


def scan_kernel(lens, give_ref, extra_ref, entry_ref, slice_ref):
    ends = bounds(lens)
    state = jnp.zeros((QUART, HDIM), F32)
    for k in range(NDEV):
        entry_ref[k] = state
        state = give_ref[k, S0 : S0 + 1, :] * state + give_ref[k, 0:T0, :]
    slice_ref[LAST] = state
    earlier = []
    for p in range(LAST):
        e = ends[p] - 1
        b = e // BLOCK
        slot = jnp.int32(0)
        for other in earlier:
            slot = slot + (other == b).astype(jnp.int32)
        earlier.append(b)
        whole = e % BLOCK == BLOCK - 1
        lead = give_ref[b, S0 + 1 + p : S0 + 2 + p, :]
        tail = jnp.where(slot == 0, give_ref[b, T0:S0, :], extra_ref[p])
        tail = jnp.where(whole, give_ref[b, 0:T0, :], tail)
        slice_ref[p] = lead * entry_ref[b] + tail


def project_kernel(here, *refs):
    near, far, slabs, outs, st_ref = refs[:NX], refs[NX], refs[NX + 1 : NX + 1 + NQ], refs[NX + 1 + NQ : -1], refs[-1]
    quarter = lax.rem(here[0], NZ) // 2
    for d, ref in enumerate(slabs):
        origin = lax.rem(quarter - d + NQ, NQ)
        for p in range(PROMPTS):
            at = pl.multiple_of(p * HDIM + origin * QUART, QUART)
            st_ref[pl.ds(at, QUART), :] = ref[p]
    st = st_ref[...]
    high = st.astype(BF)
    low = (st - high.astype(F32)).astype(BF)
    r = lax.broadcasted_iota(jnp.int32, (NROW, HDIM), 0) % ROWS_DEV
    c = lax.broadcasted_iota(jnp.int32, (NROW, HDIM), 1)
    rows = []
    for msg in [ref[0] for ref in near] + [far[dx] for dx in range(NX)]:
        q = msg[:NROW, :]
        ids = jnp.broadcast_to(msg[NROW : NROW + 1, :], (NROW, HDIM))
        prompt = jnp.sum(jnp.where(r == c, ids, 0.0), axis=1, keepdims=True)
        rows.append(
            jnp.concatenate(
                [jnp.where(prompt == float(p), q, 0.0).astype(BF) for p in range(PROMPTS)], axis=1
            )
        )
    wide = jnp.concatenate(rows, axis=0)
    res = jnp.dot(wide, high, preferred_element_type=F32) + jnp.dot(
        wide, low, preferred_element_type=F32
    )
    for dx, ref in enumerate(outs):
        for db in range(2):
            at = (db * NX + dx) * NROW
            ref[db] = res[at : at + NROW, :]


def mixed_kernel(here, query_ref, back_ref, intra_ref, carried_ref, local_ref, scarried_ref, *refs):
    near, far = refs[:NX], refs[NX]
    mixed_ref, dec_ref, send_ref, carry_ref = refs[NX + 1 :]
    for dx in range(NX):
        carry_ref[mate_head(here, dx, 0)] = near[dx][0]
        carry_ref[mate_head(here, dx, 1)] = far[dx]
    acc = jnp.zeros((NROW, HDIM), F32)
    for h in range(HEADS):
        cols = slice(h * HDIM, (h + 1) * HDIM)
        dec = local_ref[:, cols] + carry_ref[h] * scarried_ref[:, h : h + 1]
        dec_ref[:, cols] = dec
        acc = acc + dec * dec
    full = jnp.concatenate([acc, jnp.zeros((HDIM - NROW, HDIM), F32)], axis=0)
    dflat = jnp.sum(full.T, axis=0, keepdims=True)

    acc = jnp.zeros((BLOCK, HDIM), F32)
    for h in range(HEADS):
        cols = slice(h * HDIM, (h + 1) * HDIM)
        state = jnp.concatenate([back_ref[owner(h, g)] for g in range(NQ)], axis=0).astype(BF)
        outer = jnp.dot(query_ref[:, cols], state, preferred_element_type=F32)
        mixed = intra_ref[:, cols] + outer * carried_ref[:, h : h + 1]
        mixed_ref[:, cols] = mixed
        acc = acc + mixed * mixed
    flat = jnp.sum(acc.T, axis=0, keepdims=True)
    both = jnp.concatenate([flat[:, :HDIM], flat[:, HDIM:], dflat, dflat], axis=0)
    for k in range(HEADS):
        send_ref[k] = both


def final_kernel(sums_ref, mixed_ref, dec_ref, gain_ref, attn_ref, out_ref):
    total = sums_ref[0]
    for k in range(1, HEADS):
        total = total + sums_ref[k]
    scale = lax.rsqrt(total / (HEAD_COUNT * HDIM) + EPSILON)
    gain = gain_ref[...]

    def column(row):
        return jnp.broadcast_to(scale[row : row + 1, :], (HDIM, HDIM)).T

    for half in range(2):
        part = slice(half * HDIM, (half + 1) * HDIM)
        col = column(half)
        for h in range(HEADS):
            cols = slice(h * HDIM, (h + 1) * HDIM)
            attn_ref[part, cols] = (mixed_ref[part, cols] * col * gain[:, cols]).astype(BF)
    col = column(2)
    for h in range(HEADS):
        cols = slice(h * HDIM, (h + 1) * HDIM)
        res = (dec_ref[:, cols] * col[: STEPS * ROWS_DEV, :] * gain[:, cols]).astype(BF)
        for step in range(STEPS):
            out_ref[step, :, cols] = res[step * ROWS_DEV : (step + 1) * ROWS_DEV, :]


def shape(*dims, dtype=F32):
    return jax.ShapeDtypeStruct(dims, dtype)


def shift(x, axis, size, d):
    return lax.ppermute(x, axis, [(i, (i + d) % size) for i in range(size)])


def over_pair(pieces):
    both = jnp.stack([piece[1] for piece in pieces])
    return lax.ppermute(both, "seq_1", [(i, i ^ 1) for i in range(NZ)])


def exchange(x, axis):
    return lax.all_to_all(x, axis, split_axis=0, concat_axis=0, tiled=True)


def more_tails(key_in, value_in, log_decay, prompt_lengths, first):
    ends = jnp.cumsum(prompt_lengths)
    positions = first + jnp.arange(BLOCK, dtype=jnp.int32)
    segs = jnp.sum((positions[:, None] >= ends[None, :]).astype(jnp.int32), axis=1)
    cum = jnp.cumsum(log_decay, axis=0)
    keys = key_in.reshape(BLOCK, HEADS, HDIM)
    values = value_in.reshape(BLOCK, HEADS, HDIM)
    parts = []
    for p in (1, 2):
        local = ends[p] - 1 - first
        owned = (local >= 0) & (local < BLOCK) & (ends[p - 1] - 1 >= first)
        safe = jnp.clip(local, 0, BLOCK - 1)
        taken = (jnp.arange(BLOCK) <= safe) & (segs == p) & owned
        spread = jnp.where(taken[:, None], cum[safe][None, :] - cum, 0.0)
        keep = jnp.where(taken[:, None], jnp.exp(spread), 0.0)
        tailed = (keys.astype(F32) * keep[:, :, None]).astype(BF)
        part = jnp.einsum("shd,she->hde", tailed, values, preferred_element_type=F32)
        part = part.reshape(NX, 2, NQ, QUART, HDIM).transpose(0, 2, 1, 3, 4)
        parts.append(part.reshape(NDEV, QUART, HDIM))
    got = exchange(jnp.concatenate(parts, axis=1), SEQ)
    both = jnp.sum(got, axis=0)
    return jnp.stack([jnp.zeros((QUART, HDIM), F32), both[:QUART], both[QUART:]])


def local(
    query_in,
    key_in,
    value_in,
    log_decay,
    norm_gain,
    prompt_lengths,
    step_query,
    step_key,
    step_value,
    step_decay,
    row_prompt,
):
    me = lax.axis_index(SEQ).astype(jnp.int32)
    here = me[None]
    width = HEADS * HDIM
    n = STEPS * ROWS_DEV

    logd = log_decay.T
    give, crowded = pl.pallas_call(
        send_kernel,
        out_shape=(shape(NDEV, GIVE, HDIM), shape(1, dtype=jnp.int32)),
        in_specs=[SMEM] * 2 + [VMEM] * 3,
        out_specs=(VMEM, SMEM),
        scratch_shapes=[pltpu.VMEM((BLOCK, HEADS), F32)],
        compiler_params=params(),
        cost_estimate=cost(3),
        name="send",
    )(prompt_lengths, here, key_in, value_in, logd)
    given = exchange(give, SEQ)

    queries = pl.pallas_call(
        query_kernel,
        out_shape=(shape(2, ASK, HDIM),) * NX,
        in_specs=[SMEM] * 2 + [VMEM],
        out_specs=(VMEM,) * NX,
        compiler_params=params(),
        cost_estimate=cost(1),
        name="query",
    )(here, row_prompt, step_query)
    queries = [queries[0]] + [shift(queries[d], "seq_0", NX, d) for d in range(1, NX)]
    far_queries = over_pair(queries)

    intra, carried, local_dec, scarried = pl.pallas_call(
        intra_kernel,
        out_shape=(shape(BLOCK, width), shape(BLOCK, HEADS), shape(n, width), shape(n, HEADS)),
        in_specs=[SMEM] * 2 + [VMEM] * 8,
        out_specs=(VMEM,) * 4,
        compiler_params=params(),
        cost_estimate=cost(6),
        name="intra",
    )(
        prompt_lengths, here, query_in, key_in, value_in, logd,
        step_query, step_key, step_value, step_decay.transpose(0, 2, 1),
    )

    given, intra, carried, local_dec, scarried, crowded, queries, far_queries = (
        lax.optimization_barrier(
            (given, intra, carried, local_dec, scarried, crowded, queries, far_queries)
        )
    )
    extra = lax.cond(
        crowded[0] > 0,
        lambda: more_tails(key_in, value_in, log_decay, prompt_lengths, me * BLOCK),
        lambda: jnp.zeros((LAST, QUART, HDIM), F32),
    )
    entry, own = pl.pallas_call(
        scan_kernel,
        out_shape=(shape(NDEV, QUART, HDIM), shape(PROMPTS, QUART, HDIM)),
        in_specs=[SMEM] + [VMEM] * 2,
        out_specs=(VMEM,) * 2,
        compiler_params=params(),
        cost_estimate=cost(2),
        name="scan",
    )(prompt_lengths, given, extra)
    slabs = [own] + [shift(own, "seq_1", NZ, 2 * d) for d in range(1, NQ)]
    entry, slabs = lax.optimization_barrier((entry, slabs))
    back = exchange(entry, SEQ)

    products = pl.pallas_call(
        project_kernel,
        out_shape=(shape(2, NROW, HDIM),) * NX,
        in_specs=[SMEM] + [VMEM] * (NX + 1 + NQ),
        out_specs=(VMEM,) * NX,
        scratch_shapes=[pltpu.VMEM((PROMPTS * HDIM, HDIM), F32)],
        compiler_params=params(),
        cost_estimate=cost(2),
        name="project",
    )(here, *queries, far_queries, *slabs)
    products = [products[0]] + [shift(products[d], "seq_0", NX, -d) for d in range(1, NX)]
    far_products = over_pair(products)

    mixed, dec, sums_send = pl.pallas_call(
        mixed_kernel,
        out_shape=(shape(BLOCK, width), shape(n, width), shape(HEADS, 4, HDIM)),
        in_specs=[SMEM] + [VMEM] * (7 + NX),
        out_specs=(VMEM,) * 3,
        scratch_shapes=[pltpu.VMEM((HEADS, NROW, HDIM), F32)],
        compiler_params=params(),
        cost_estimate=cost(2),
        name="mixed",
    )(here, query_in, back, intra, carried, local_dec, scarried, *products, far_products)
    sums_all = exchange(sums_send, "head")

    return pl.pallas_call(
        final_kernel,
        out_shape=(shape(BLOCK, width, dtype=BF), shape(STEPS, ROWS_DEV, width, dtype=BF)),
        in_specs=[VMEM] * 4,
        out_specs=(VMEM,) * 2,
        compiler_params=params(),
        cost_estimate=cost(2),
        name="final",
    )(sums_all, mixed, dec, norm_gain.reshape(1, width))


def solution(mesh):
    split = Mesh(mesh.devices.reshape(NX, NZ, mesh.shape["head"]), ("seq_0", "seq_1", "head"))
    placed = (
        P(SEQ, "head"),
        P(SEQ, "head"),
        P(SEQ, "head"),
        P(SEQ, "head"),
        P("head"),
        P(),
        P(None, SEQ, "head"),
        P(None, SEQ, "head"),
        P(None, SEQ, "head"),
        P(None, SEQ, "head"),
        P(SEQ),
    )
    return jax.shard_map(
        local,
        mesh=split,
        in_specs=placed,
        out_specs=(P(SEQ, "head"), P(None, SEQ, "head")),
        check_vma=False,
    )
```

```python
import functools

import jax
import jax.numpy as jnp
from jax import lax
from jax.experimental import pallas as pl
from jax.experimental.pallas import tpu as pltpu
from jax.sharding import Mesh
from jax.sharding import PartitionSpec as P

HEAD_COUNT = 64
HDIM = 128
BLOCK = 256
PROMPTS = 4
STEPS = 4
SEQ = ("seq_0", "seq_1")
EPSILON = 1e-06

NX = 4
NZ = 8
HEADS = 8
NDEV = NX * NZ
NQ = NZ // 2
QUART = HDIM // NQ
ROWS_DEV = 16
NROW = STEPS * ROWS_DEV
LAST = PROMPTS - 1
ASK = NROW + 8

T0 = QUART
S0 = 2 * QUART
GIVE = S0 + 8

BF = jnp.bfloat16
F32 = jnp.float32
HI = lax.Precision.HIGHEST

SMEM = pl.BlockSpec(memory_space=pltpu.SMEM)
VMEM = pl.BlockSpec(memory_space=pltpu.VMEM)
PLACE = pl.BlockSpec(memory_space=pl.ANY)


def params(mib=12):
    return pltpu.CompilerParams(vmem_limit_bytes=mib << 20)


def cost(us):
    return pl.CostEstimate(flops=int(us * 1e9), bytes_accessed=int(us * 3e6), transcendentals=0)


def bounds(lens):
    ends = []
    total = lens[0]
    for p in range(PROMPTS):
        if p:
            total = total + lens[p]
        ends.append(total)
    return ends


def seg_of(pos, ends):
    out = (pos >= ends[0]).astype(jnp.int32)
    for p in range(1, PROMPTS):
        out = out + (pos >= ends[p]).astype(jnp.int32)
    return out


def entry_seg(first, ends):
    return jnp.where(first > 0, seg_of(first - 1, ends), -1)


def cum_columns(logd):
    t = lax.broadcasted_iota(jnp.int32, (BLOCK, BLOCK), 0)
    s = lax.broadcasted_iota(jnp.int32, (BLOCK, BLOCK), 1)
    return lax.dot_general(
        (s <= t).astype(F32), logd, (((1,), (1,)), ((), ())), precision=HI, preferred_element_type=F32
    )


def contract_rows(a, b):
    return lax.dot_general(a, b, (((0,), (0,)), ((), ())), preferred_element_type=F32)


def contract_cols(a, b):
    return lax.dot_general(a, b, (((1,), (1,)), ((), ())), preferred_element_type=F32)


def owner(head, quarter):
    return (head // 2) * NZ + 2 * quarter + head % 2


def send_kernel(
    lens, here, key_in, value_in, logd_in, out, flag_ref,
    key_ref, value_ref, logd_ref, out_ref, cum_ref, sems,
):
    moves = [pltpu.make_async_copy(logd_in, logd_ref, sems.at[0])]
    half = HEADS * HDIM // 2
    for k in range(2):
        cols = slice(k * half, (k + 1) * half)
        moves.append(pltpu.make_async_copy(key_in.at[:, cols], key_ref.at[:, cols], sems.at[1 + 2 * k]))
        moves.append(
            pltpu.make_async_copy(value_in.at[:, cols], value_ref.at[:, cols], sems.at[2 + 2 * k])
        )
    for move in moves:
        move.start()
    moves[0].wait()
    first = here[0] * BLOCK
    ends = bounds(lens)
    front = entry_seg(first, ends)
    seg_last = seg_of(first + (BLOCK - 1), ends)
    cum = cum_columns(logd_ref[...])
    cum_ref[...] = cum
    tok = lax.broadcasted_iota(jnp.int32, (BLOCK, HEADS), 0)
    seg = seg_of(tok + first, ends)
    last = cum[BLOCK - 1 : BLOCK, :]
    keep = jnp.where(seg == seg_last, jnp.exp(last - cum), 0.0)
    factors = [jnp.exp(last) * (seg_last == front).astype(F32)]
    found = jnp.int32(-1)
    spot = jnp.int32(0)
    crowded = jnp.int32(0)
    for p in range(LAST):
        at = ends[p] - 1 - first
        inside = (at >= 0) & (at < BLOCK)
        reached = cum_ref[pl.ds(jnp.clip(at, 0, BLOCK - 1), 1), :]
        factors.append(jnp.exp(reached) * (inside & (front == p)).astype(F32))
        take = (at >= 0) & (at < BLOCK - 1) & (found < 0)
        found = jnp.where(take, p, found)
        spot = jnp.where(take, at, spot)
        if p:
            same = (ends[p] - 1) // BLOCK == (ends[p - 1] - 1) // BLOCK
            crowded = crowded | (same & (ends[p] % BLOCK != 0)).astype(jnp.int32)
    flag_ref[0] = crowded

    reached = cum_ref[pl.ds(spot, 1), :]
    taken = (tok <= spot) & (seg == found)
    tail = jnp.where(taken, jnp.exp(jnp.where(taken, reached - cum, 0.0)), 0.0)

    def emit(h, factor, row):
        cols = slice(h * HDIM, (h + 1) * HDIM)
        keyed = (key_ref[:, cols].astype(F32) * factor[:, h : h + 1]).astype(BF)
        total = contract_rows(keyed, value_ref[:, cols])
        for g in range(NQ):
            out_ref[owner(h, g), row : row + QUART, :] = total[g * QUART : (g + 1) * QUART, :]

    leaving = []
    for x in range(NX):
        if x % 2 == 0:
            moves[1 + x].wait()
            moves[2 + x].wait()
        for h in (2 * x, 2 * x + 1):
            emit(h, keep, 0)
            scal = jnp.concatenate(
                [jnp.broadcast_to(f[:, h : h + 1], (1, HDIM)) for f in factors]
                + [jnp.zeros((8 - len(factors), HDIM), F32)],
                axis=0,
            )
            for g in range(NQ):
                out_ref[owner(h, g), S0:GIVE, :] = scal

        @pl.when(found < 0)
        def _(x=x):
            out_ref[x * NZ : (x + 1) * NZ, T0:S0, :] = jnp.zeros((NZ, QUART, HDIM), F32)

        @pl.when(found >= 0)
        def _(x=x):
            for h in (2 * x, 2 * x + 1):
                emit(h, tail, T0)

        group = slice(x * NZ, (x + 1) * NZ)
        leaving.append(pltpu.make_async_copy(out_ref.at[group], out.at[group], sems.at[5 + x]))
        leaving[-1].start()
    for move in leaving:
        move.wait()


def mate_head(here, dx, db):
    x = here[0] // NZ
    parity = lax.rem(here[0], 2)
    return 2 * lax.rem(x + dx, NX) + (1 - parity if db else parity)


def query_kernel(here, rows, query_ref, *out_refs):
    lane = lax.broadcasted_iota(jnp.int32, (8, HDIM), 1)
    ids = jnp.zeros((8, HDIM), F32)
    for k in range(ROWS_DEV):
        ids = jnp.where(lane == k, rows[k].astype(F32), ids)
    for dx, out_ref in enumerate(out_refs):
        for db in range(2):
            cols = pl.ds(pl.multiple_of(mate_head(here, dx, db) * HDIM, HDIM), HDIM)
            out_ref[db, :NROW, :] = query_ref[:, :, cols].astype(F32).reshape(NROW, HDIM)
            out_ref[db, NROW:, :] = ids


def intra_kernel(
    lens, here, query_ref, key_ref, value_ref, logd_ref, intra_ref, carried_ref
):
    first = here[0] * BLOCK
    ends = bounds(lens)
    front = entry_seg(first, ends)
    logd = logd_ref[...]
    t = lax.broadcasted_iota(jnp.int32, (BLOCK, BLOCK), 0)
    s = lax.broadcasted_iota(jnp.int32, (BLOCK, BLOCK), 1)
    cum = cum_columns(logd)
    cum_rows = jnp.dot(logd, (t <= s).astype(F32), precision=HI, preferred_element_type=F32)
    linked = (s <= t) & (seg_of(t + first, ends) == seg_of(s + first, ends))
    tok = lax.broadcasted_iota(jnp.int32, (BLOCK, HEADS), 0)
    carried_ref[...] = jnp.where(seg_of(tok + first, ends) == front, jnp.exp(cum), 0.0)
    for h in range(HEADS):
        cols = slice(h * HDIM, (h + 1) * HDIM)
        scores = contract_cols(query_ref[:, cols], key_ref[:, cols])
        spread = cum[:, h : h + 1] - cum_rows[h : h + 1, :]
        factor = jnp.exp(jnp.where(linked, spread, -1e30))
        weights = (scores * factor).astype(BF)
        intra_ref[:, cols] = jnp.dot(weights, value_ref[:, cols], preferred_element_type=F32)


def local_kernel(sq_ref, sk_ref, sv_ref, sd_ref, local_ref, scarried_ref):
    n = NROW
    a = lax.broadcasted_iota(jnp.int32, (n, n), 0)
    b = lax.broadcasted_iota(jnp.int32, (n, n), 1)
    same = (b <= a) & ((a - b) % ROWS_DEV == 0)
    total = sd_ref[0]
    pieces = [total]
    for step in range(1, STEPS):
        total = total + sd_ref[step]
        pieces.append(total)
    scum_rows = jnp.concatenate(pieces, axis=1)
    scum = lax.dot_general(
        (a == b).astype(F32), scum_rows, (((1,), (1,)), ((), ())), precision=HI,
        preferred_element_type=F32,
    )
    scarried_ref[...] = jnp.exp(scum)
    for h in range(HEADS):
        cols = slice(h * HDIM, (h + 1) * HDIM)
        q = sq_ref[:, :, cols].reshape(n, HDIM)
        k = sk_ref[:, :, cols].reshape(n, HDIM)
        v = sv_ref[:, :, cols].reshape(n, HDIM)
        spread = scum[:, h : h + 1] - scum_rows[h : h + 1, :]
        weights = contract_cols(q, k) * jnp.exp(jnp.where(same, spread, -1e30))
        high = weights.astype(BF)
        low = (weights - high.astype(F32)).astype(BF)
        local_ref[:, cols] = jnp.dot(high, v, preferred_element_type=F32) + jnp.dot(
            low, v, preferred_element_type=F32
        )


def scan_kernel(lens, give_ref, extra_ref, entry_ref, slice_ref):
    ends = bounds(lens)
    state = jnp.zeros((QUART, HDIM), F32)
    for k in range(NDEV):
        entry_ref[k] = state
        state = give_ref[k, S0 : S0 + 1, :] * state + give_ref[k, 0:T0, :]
    slice_ref[LAST] = state
    earlier = []
    for p in range(LAST):
        e = ends[p] - 1
        b = e // BLOCK
        slot = jnp.int32(0)
        for other in earlier:
            slot = slot + (other == b).astype(jnp.int32)
        earlier.append(b)
        whole = e % BLOCK == BLOCK - 1
        lead = give_ref[b, S0 + 1 + p : S0 + 2 + p, :]
        tail = jnp.where(slot == 0, give_ref[b, T0:S0, :], extra_ref[p])
        tail = jnp.where(whole, give_ref[b, 0:T0, :], tail)
        slice_ref[p] = lead * entry_ref[b] + tail


def project_kernel(here, *refs):
    near, far, slabs, outs, st_ref = refs[:NX], refs[NX], refs[NX + 1 : NX + 1 + NQ], refs[NX + 1 + NQ : -1], refs[-1]
    quarter = lax.rem(here[0], NZ) // 2
    for d, ref in enumerate(slabs):
        origin = lax.rem(quarter - d + NQ, NQ)
        for p in range(PROMPTS):
            at = pl.multiple_of(p * HDIM + origin * QUART, QUART)
            st_ref[pl.ds(at, QUART), :] = ref[p]
    st = st_ref[...]
    high = st.astype(BF)
    low = (st - high.astype(F32)).astype(BF)
    r = lax.broadcasted_iota(jnp.int32, (NROW, HDIM), 0) % ROWS_DEV
    c = lax.broadcasted_iota(jnp.int32, (NROW, HDIM), 1)
    rows = []
    for msg in [ref[0] for ref in near] + [far[dx] for dx in range(NX)]:
        q = msg[:NROW, :]
        ids = jnp.broadcast_to(msg[NROW : NROW + 1, :], (NROW, HDIM))
        prompt = jnp.sum(jnp.where(r == c, ids, 0.0), axis=1, keepdims=True)
        rows.append(
            jnp.concatenate(
                [jnp.where(prompt == float(p), q, 0.0).astype(BF) for p in range(PROMPTS)], axis=1
            )
        )
    wide = jnp.concatenate(rows, axis=0)
    res = jnp.dot(wide, high, preferred_element_type=F32) + jnp.dot(
        wide, low, preferred_element_type=F32
    )
    for dx, ref in enumerate(outs):
        for db in range(2):
            at = (db * NX + dx) * NROW
            ref[db] = res[at : at + NROW, :]


def mixed_kernel(here, query_ref, back_ref, intra_ref, carried_ref, local_ref, scarried_ref, *refs):
    near, far = refs[:NX], refs[NX]
    mixed_ref, dec_ref, send_ref, carry_ref = refs[NX + 1 :]
    for dx in range(NX):
        carry_ref[mate_head(here, dx, 0)] = near[dx][0]
        carry_ref[mate_head(here, dx, 1)] = far[dx]
    acc = jnp.zeros((NROW, HDIM), F32)
    for h in range(HEADS):
        cols = slice(h * HDIM, (h + 1) * HDIM)
        dec = local_ref[:, cols] + carry_ref[h] * scarried_ref[:, h : h + 1]
        dec_ref[:, cols] = dec
        acc = acc + dec * dec
    full = jnp.concatenate([acc, jnp.zeros((HDIM - NROW, HDIM), F32)], axis=0)
    dflat = jnp.sum(full.T, axis=0, keepdims=True)

    acc = jnp.zeros((BLOCK, HDIM), F32)
    for h in range(HEADS):
        cols = slice(h * HDIM, (h + 1) * HDIM)
        state = jnp.concatenate([back_ref[owner(h, g)] for g in range(NQ)], axis=0).astype(BF)
        outer = jnp.dot(query_ref[:, cols], state, preferred_element_type=F32)
        mixed = intra_ref[:, cols] + outer * carried_ref[:, h : h + 1]
        mixed_ref[:, cols] = mixed
        acc = acc + mixed * mixed
    flat = jnp.sum(acc.T, axis=0, keepdims=True)
    both = jnp.concatenate([flat[:, :HDIM], flat[:, HDIM:], dflat, dflat], axis=0)
    for k in range(HEADS):
        send_ref[k] = both


def final_kernel(sums_ref, mixed_ref, dec_ref, gain_ref, attn_ref, out_ref):
    total = sums_ref[0]
    for k in range(1, HEADS):
        total = total + sums_ref[k]
    scale = lax.rsqrt(total / (HEAD_COUNT * HDIM) + EPSILON)
    gain = gain_ref[...]

    def column(row):
        return jnp.broadcast_to(scale[row : row + 1, :], (HDIM, HDIM)).T

    for half in range(2):
        part = slice(half * HDIM, (half + 1) * HDIM)
        col = column(half)
        for h in range(HEADS):
            cols = slice(h * HDIM, (h + 1) * HDIM)
            attn_ref[part, cols] = (mixed_ref[part, cols] * col * gain[:, cols]).astype(BF)
    col = column(2)
    for h in range(HEADS):
        cols = slice(h * HDIM, (h + 1) * HDIM)
        res = (dec_ref[:, cols] * col[: STEPS * ROWS_DEV, :] * gain[:, cols]).astype(BF)
        for step in range(STEPS):
            out_ref[step, :, cols] = res[step * ROWS_DEV : (step + 1) * ROWS_DEV, :]


def shape(*dims, dtype=F32):
    return jax.ShapeDtypeStruct(dims, dtype)


def shift(x, axis, size, d):
    return lax.ppermute(x, axis, [(i, (i + d) % size) for i in range(size)])


def over_pair(pieces):
    both = jnp.stack([piece[1] for piece in pieces])
    return lax.ppermute(both, "seq_1", [(i, i ^ 1) for i in range(NZ)])


def exchange(x, axis):
    return lax.all_to_all(x, axis, split_axis=0, concat_axis=0, tiled=True)


def more_tails(key_in, value_in, log_decay, prompt_lengths, first):
    ends = jnp.cumsum(prompt_lengths)
    positions = first + jnp.arange(BLOCK, dtype=jnp.int32)
    segs = jnp.sum((positions[:, None] >= ends[None, :]).astype(jnp.int32), axis=1)
    cum = jnp.cumsum(log_decay, axis=0)
    keys = key_in.reshape(BLOCK, HEADS, HDIM)
    values = value_in.reshape(BLOCK, HEADS, HDIM)
    parts = []
    for p in (1, 2):
        local = ends[p] - 1 - first
        owned = (local >= 0) & (local < BLOCK) & (ends[p - 1] - 1 >= first)
        safe = jnp.clip(local, 0, BLOCK - 1)
        taken = (jnp.arange(BLOCK) <= safe) & (segs == p) & owned
        spread = jnp.where(taken[:, None], cum[safe][None, :] - cum, 0.0)
        keep = jnp.where(taken[:, None], jnp.exp(spread), 0.0)
        tailed = (keys.astype(F32) * keep[:, :, None]).astype(BF)
        part = jnp.einsum("shd,she->hde", tailed, values, preferred_element_type=F32)
        part = part.reshape(NX, 2, NQ, QUART, HDIM).transpose(0, 2, 1, 3, 4)
        parts.append(part.reshape(NDEV, QUART, HDIM))
    got = exchange(jnp.concatenate(parts, axis=1), SEQ)
    both = jnp.sum(got, axis=0)
    return jnp.stack([jnp.zeros((QUART, HDIM), F32), both[:QUART], both[QUART:]])


def local(
    query_in,
    key_in,
    value_in,
    log_decay,
    norm_gain,
    prompt_lengths,
    step_query,
    step_key,
    step_value,
    step_decay,
    row_prompt,
):
    me = lax.axis_index(SEQ).astype(jnp.int32)
    here = me[None]
    width = HEADS * HDIM
    n = STEPS * ROWS_DEV

    logd = log_decay.T
    give, crowded = pl.pallas_call(
        send_kernel,
        out_shape=(shape(NDEV, GIVE, HDIM), shape(1, dtype=jnp.int32)),
        in_specs=[SMEM] * 2 + [PLACE] * 3,
        out_specs=(PLACE, SMEM),
        scratch_shapes=[
            pltpu.VMEM((BLOCK, width), BF),
            pltpu.VMEM((BLOCK, width), BF),
            pltpu.VMEM((HEADS, BLOCK), F32),
            pltpu.VMEM((NDEV, GIVE, HDIM), F32),
            pltpu.VMEM((BLOCK, HEADS), F32),
            pltpu.SemaphoreType.DMA((5 + NX,)),
        ],
        compiler_params=params(),
        cost_estimate=cost(3),
        name="send",
    )(prompt_lengths, here, key_in, value_in, logd)
    given = exchange(give, SEQ)

    queries = pl.pallas_call(
        query_kernel,
        out_shape=(shape(2, ASK, HDIM),) * NX,
        in_specs=[SMEM] * 2 + [VMEM],
        out_specs=(VMEM,) * NX,
        compiler_params=params(),
        cost_estimate=cost(1),
        name="query",
    )(here, row_prompt, step_query)
    queries = [queries[0]] + [shift(queries[d], "seq_0", NX, d) for d in range(1, NX)]
    far_queries = over_pair(queries)

    intra, carried = pl.pallas_call(
        intra_kernel,
        out_shape=(shape(BLOCK, width), shape(BLOCK, HEADS)),
        in_specs=[SMEM] * 2 + [VMEM] * 4,
        out_specs=(VMEM,) * 2,
        compiler_params=params(),
        cost_estimate=cost(3),
        name="intra",
    )(prompt_lengths, here, query_in, key_in, value_in, logd)

    given, intra, carried, crowded, queries, far_queries = lax.optimization_barrier(
        (given, intra, carried, crowded, queries, far_queries)
    )
    extra = lax.cond(
        crowded[0] > 0,
        lambda: more_tails(key_in, value_in, log_decay, prompt_lengths, me * BLOCK),
        lambda: jnp.zeros((LAST, QUART, HDIM), F32),
    )
    entry, own = pl.pallas_call(
        scan_kernel,
        out_shape=(shape(NDEV, QUART, HDIM), shape(PROMPTS, QUART, HDIM)),
        in_specs=[SMEM] + [VMEM] * 2,
        out_specs=(VMEM,) * 2,
        compiler_params=params(),
        cost_estimate=cost(2),
        name="scan",
    )(prompt_lengths, given, extra)
    slabs = [own] + [shift(own, "seq_1", NZ, 2 * d) for d in range(1, NQ)]
    entry, slabs, step_key = lax.optimization_barrier((entry, slabs, step_key))
    back = exchange(entry, SEQ)

    local_dec, scarried = pl.pallas_call(
        local_kernel,
        out_shape=(shape(n, width), shape(n, HEADS)),
        in_specs=[VMEM] * 4,
        out_specs=(VMEM,) * 2,
        compiler_params=params(),
        cost_estimate=cost(1),
        name="local",
    )(step_query, step_key, step_value, step_decay.transpose(0, 2, 1))

    products = pl.pallas_call(
        project_kernel,
        out_shape=(shape(2, NROW, HDIM),) * NX,
        in_specs=[SMEM] + [VMEM] * (NX + 1 + NQ),
        out_specs=(VMEM,) * NX,
        scratch_shapes=[pltpu.VMEM((PROMPTS * HDIM, HDIM), F32)],
        compiler_params=params(),
        cost_estimate=cost(2),
        name="project",
    )(here, *queries, far_queries, *slabs)
    products = [products[0]] + [shift(products[d], "seq_0", NX, -d) for d in range(1, NX)]
    far_products = over_pair(products)

    mixed, dec, sums_send = pl.pallas_call(
        mixed_kernel,
        out_shape=(shape(BLOCK, width), shape(n, width), shape(HEADS, 4, HDIM)),
        in_specs=[SMEM] + [VMEM] * (7 + NX),
        out_specs=(VMEM,) * 3,
        scratch_shapes=[pltpu.VMEM((HEADS, NROW, HDIM), F32)],
        compiler_params=params(),
        cost_estimate=cost(2),
        name="mixed",
    )(here, query_in, back, intra, carried, local_dec, scarried, *products, far_products)
    sums_all = exchange(sums_send, "head")

    return pl.pallas_call(
        final_kernel,
        out_shape=(shape(BLOCK, width, dtype=BF), shape(STEPS, ROWS_DEV, width, dtype=BF)),
        in_specs=[VMEM] * 4,
        out_specs=(VMEM,) * 2,
        compiler_params=params(),
        cost_estimate=cost(2),
        name="final",
    )(sums_all, mixed, dec, norm_gain.reshape(1, width))


def solution(mesh):
    split = Mesh(mesh.devices.reshape(NX, NZ, mesh.shape["head"]), ("seq_0", "seq_1", "head"))
    placed = (
        P(SEQ, "head"),
        P(SEQ, "head"),
        P(SEQ, "head"),
        P(SEQ, "head"),
        P("head"),
        P(),
        P(None, SEQ, "head"),
        P(None, SEQ, "head"),
        P(None, SEQ, "head"),
        P(None, SEQ, "head"),
        P(SEQ),
    )
    return jax.shard_map(
        local,
        mesh=split,
        in_specs=placed,
        out_specs=(P(SEQ, "head"), P(None, SEQ, "head")),
        check_vma=False,
    )
```

```python
import functools

import jax
import jax.numpy as jnp
from jax import lax
from jax.experimental import pallas as pl
from jax.experimental.pallas import tpu as pltpu
from jax.sharding import Mesh
from jax.sharding import PartitionSpec as P

HEAD_COUNT = 64
HDIM = 128
BLOCK = 256
PROMPTS = 4
STEPS = 4
SEQ = ("seq_0", "seq_1")
EPSILON = 1e-06

NX = 4
NZ = 8
HEADS = 8
NDEV = NX * NZ
NQ = NZ // 2
QUART = HDIM // NQ
ROWS_DEV = 16
NROW = STEPS * ROWS_DEV
LAST = PROMPTS - 1
ASK = NROW + 8

T0 = QUART
S0 = 2 * QUART
GIVE = S0 + 8

BF = jnp.bfloat16
F32 = jnp.float32
HI = lax.Precision.HIGHEST

SMEM = pl.BlockSpec(memory_space=pltpu.SMEM)
VMEM = pl.BlockSpec(memory_space=pltpu.VMEM)
PLACE = pl.BlockSpec(memory_space=pl.ANY)


def params(mib=12):
    return pltpu.CompilerParams(vmem_limit_bytes=mib << 20)


def cost(us):
    return pl.CostEstimate(flops=int(us * 1e9), bytes_accessed=int(us * 3e6), transcendentals=0)


def bounds(lens):
    ends = []
    total = lens[0]
    for p in range(PROMPTS):
        if p:
            total = total + lens[p]
        ends.append(total)
    return ends


def seg_of(pos, ends):
    out = (pos >= ends[0]).astype(jnp.int32)
    for p in range(1, PROMPTS):
        out = out + (pos >= ends[p]).astype(jnp.int32)
    return out


def entry_seg(first, ends):
    return jnp.where(first > 0, seg_of(first - 1, ends), -1)


def cum_columns(logd):
    t = lax.broadcasted_iota(jnp.int32, (BLOCK, BLOCK), 0)
    s = lax.broadcasted_iota(jnp.int32, (BLOCK, BLOCK), 1)
    return lax.dot_general(
        (s <= t).astype(F32), logd, (((1,), (1,)), ((), ())), precision=HI, preferred_element_type=F32
    )


def contract_rows(a, b):
    return lax.dot_general(a, b, (((0,), (0,)), ((), ())), preferred_element_type=F32)


def contract_cols(a, b):
    return lax.dot_general(a, b, (((1,), (1,)), ((), ())), preferred_element_type=F32)


def owner(head, quarter):
    return (head // 2) * NZ + 2 * quarter + head % 2


def send_kernel(
    lens, here, key_in, value_in, logd_ref, out_ref, flag_ref, key_ref, value_ref, cum_ref, sems
):
    moves = [
        pltpu.make_async_copy(key_in, key_ref, sems.at[0]),
        pltpu.make_async_copy(value_in, value_ref, sems.at[1]),
    ]
    for move in moves:
        move.start()
    first = here[0] * BLOCK
    ends = bounds(lens)
    front = entry_seg(first, ends)
    seg_last = seg_of(first + (BLOCK - 1), ends)
    cum = cum_columns(logd_ref[...])
    cum_ref[...] = cum
    tok = lax.broadcasted_iota(jnp.int32, (BLOCK, HEADS), 0)
    seg = seg_of(tok + first, ends)
    last = cum[BLOCK - 1 : BLOCK, :]
    keep = jnp.where(seg == seg_last, jnp.exp(last - cum), 0.0)
    factors = [jnp.exp(last) * (seg_last == front).astype(F32)]
    found = jnp.int32(-1)
    spot = jnp.int32(0)
    crowded = jnp.int32(0)
    for p in range(LAST):
        at = ends[p] - 1 - first
        inside = (at >= 0) & (at < BLOCK)
        reached = cum_ref[pl.ds(jnp.clip(at, 0, BLOCK - 1), 1), :]
        factors.append(jnp.exp(reached) * (inside & (front == p)).astype(F32))
        take = (at >= 0) & (at < BLOCK - 1) & (found < 0)
        found = jnp.where(take, p, found)
        spot = jnp.where(take, at, spot)
        if p:
            same = (ends[p] - 1) // BLOCK == (ends[p - 1] - 1) // BLOCK
            crowded = crowded | (same & (ends[p] % BLOCK != 0)).astype(jnp.int32)
    flag_ref[0] = crowded

    def emit(factor, row):
        for h in range(HEADS):
            cols = slice(h * HDIM, (h + 1) * HDIM)
            keyed = (key_ref[:, cols].astype(F32) * factor[:, h : h + 1]).astype(BF)
            total = contract_rows(keyed, value_ref[:, cols])
            for g in range(NQ):
                out_ref[owner(h, g), row : row + QUART, :] = total[g * QUART : (g + 1) * QUART, :]

    for move in moves:
        move.wait()
    emit(keep, 0)
    for h in range(HEADS):
        scal = jnp.concatenate(
            [jnp.broadcast_to(f[:, h : h + 1], (1, HDIM)) for f in factors]
            + [jnp.zeros((8 - len(factors), HDIM), F32)],
            axis=0,
        )
        for g in range(NQ):
            out_ref[owner(h, g), S0:GIVE, :] = scal

    @pl.when(found < 0)
    def _():
        out_ref[:, T0:S0, :] = jnp.zeros((NDEV, QUART, HDIM), F32)

    @pl.when(found >= 0)
    def _():
        reached = cum_ref[pl.ds(spot, 1), :]
        taken = (tok <= spot) & (seg == found)
        emit(jnp.where(taken, jnp.exp(jnp.where(taken, reached - cum, 0.0)), 0.0), T0)


def mate_head(here, dx, db):
    x = here[0] // NZ
    parity = lax.rem(here[0], 2)
    return 2 * lax.rem(x + dx, NX) + (1 - parity if db else parity)


def query_kernel(here, rows, query_ref, *out_refs):
    lane = lax.broadcasted_iota(jnp.int32, (8, HDIM), 1)
    ids = jnp.zeros((8, HDIM), F32)
    for k in range(ROWS_DEV):
        ids = jnp.where(lane == k, rows[k].astype(F32), ids)
    for dx, out_ref in enumerate(out_refs):
        for db in range(2):
            cols = pl.ds(pl.multiple_of(mate_head(here, dx, db) * HDIM, HDIM), HDIM)
            out_ref[db, :NROW, :] = query_ref[:, :, cols].astype(F32).reshape(NROW, HDIM)
            out_ref[db, NROW:, :] = ids


def intra_kernel(
    lens, here, query_ref, key_ref, value_ref, logd_ref, intra_ref, carried_ref
):
    first = here[0] * BLOCK
    ends = bounds(lens)
    front = entry_seg(first, ends)
    logd = logd_ref[...]
    t = lax.broadcasted_iota(jnp.int32, (BLOCK, BLOCK), 0)
    s = lax.broadcasted_iota(jnp.int32, (BLOCK, BLOCK), 1)
    cum = cum_columns(logd)
    cum_rows = jnp.dot(logd, (t <= s).astype(F32), precision=HI, preferred_element_type=F32)
    linked = (s <= t) & (seg_of(t + first, ends) == seg_of(s + first, ends))
    tok = lax.broadcasted_iota(jnp.int32, (BLOCK, HEADS), 0)
    carried_ref[...] = jnp.where(seg_of(tok + first, ends) == front, jnp.exp(cum), 0.0)
    for h in range(HEADS):
        cols = slice(h * HDIM, (h + 1) * HDIM)
        scores = contract_cols(query_ref[:, cols], key_ref[:, cols])
        spread = cum[:, h : h + 1] - cum_rows[h : h + 1, :]
        factor = jnp.exp(jnp.where(linked, spread, -1e30))
        weights = (scores * factor).astype(BF)
        intra_ref[:, cols] = jnp.dot(weights, value_ref[:, cols], preferred_element_type=F32)


def local_kernel(sq_ref, sk_ref, sv_ref, sd_ref, local_ref, scarried_ref):
    n = NROW
    a = lax.broadcasted_iota(jnp.int32, (n, n), 0)
    b = lax.broadcasted_iota(jnp.int32, (n, n), 1)
    same = (b <= a) & ((a - b) % ROWS_DEV == 0)
    total = sd_ref[0]
    pieces = [total]
    for step in range(1, STEPS):
        total = total + sd_ref[step]
        pieces.append(total)
    scum_rows = jnp.concatenate(pieces, axis=1)
    scum = lax.dot_general(
        (a == b).astype(F32), scum_rows, (((1,), (1,)), ((), ())), precision=HI,
        preferred_element_type=F32,
    )
    scarried_ref[...] = jnp.exp(scum)
    for h in range(HEADS):
        cols = slice(h * HDIM, (h + 1) * HDIM)
        q = sq_ref[:, :, cols].reshape(n, HDIM)
        k = sk_ref[:, :, cols].reshape(n, HDIM)
        v = sv_ref[:, :, cols].reshape(n, HDIM)
        spread = scum[:, h : h + 1] - scum_rows[h : h + 1, :]
        weights = contract_cols(q, k) * jnp.exp(jnp.where(same, spread, -1e30))
        high = weights.astype(BF)
        low = (weights - high.astype(F32)).astype(BF)
        local_ref[:, cols] = jnp.dot(high, v, preferred_element_type=F32) + jnp.dot(
            low, v, preferred_element_type=F32
        )


def scan_kernel(lens, give_ref, *refs):
    extra_ref = refs[0] if len(refs) == 3 else None
    entry_ref, slice_ref = refs[-2:]
    ends = bounds(lens)
    state = jnp.zeros((QUART, HDIM), F32)
    for k in range(NDEV):
        entry_ref[k] = state
        state = give_ref[k, S0 : S0 + 1, :] * state + give_ref[k, 0:T0, :]
    slice_ref[LAST] = state
    earlier = []
    for p in range(LAST):
        e = ends[p] - 1
        b = e // BLOCK
        slot = jnp.int32(0)
        for other in earlier:
            slot = slot + (other == b).astype(jnp.int32)
        earlier.append(b)
        whole = e % BLOCK == BLOCK - 1
        lead = give_ref[b, S0 + 1 + p : S0 + 2 + p, :]
        tail = give_ref[b, T0:S0, :]
        if extra_ref is not None:
            tail = jnp.where(slot == 0, tail, extra_ref[p])
        tail = jnp.where(whole, give_ref[b, 0:T0, :], tail)
        slice_ref[p] = lead * entry_ref[b] + tail


def project_kernel(here, *refs):
    near, far, slabs, outs, st_ref = refs[:NX], refs[NX], refs[NX + 1 : NX + 1 + NQ], refs[NX + 1 + NQ : -1], refs[-1]
    quarter = lax.rem(here[0], NZ) // 2
    for d, ref in enumerate(slabs):
        origin = lax.rem(quarter - d + NQ, NQ)
        for p in range(PROMPTS):
            at = pl.multiple_of(p * HDIM + origin * QUART, QUART)
            st_ref[pl.ds(at, QUART), :] = ref[p]
    st = st_ref[...]
    high = st.astype(BF)
    low = (st - high.astype(F32)).astype(BF)
    r = lax.broadcasted_iota(jnp.int32, (NROW, HDIM), 0) % ROWS_DEV
    c = lax.broadcasted_iota(jnp.int32, (NROW, HDIM), 1)
    rows = []
    for msg in [ref[0] for ref in near] + [far[dx] for dx in range(NX)]:
        q = msg[:NROW, :]
        ids = jnp.broadcast_to(msg[NROW : NROW + 1, :], (NROW, HDIM))
        prompt = jnp.sum(jnp.where(r == c, ids, 0.0), axis=1, keepdims=True)
        rows.append(
            jnp.concatenate(
                [jnp.where(prompt == float(p), q, 0.0).astype(BF) for p in range(PROMPTS)], axis=1
            )
        )
    wide = jnp.concatenate(rows, axis=0)
    res = jnp.dot(wide, high, preferred_element_type=F32) + jnp.dot(
        wide, low, preferred_element_type=F32
    )
    for dx, ref in enumerate(outs):
        for db in range(2):
            at = (db * NX + dx) * NROW
            ref[db] = res[at : at + NROW, :]


def mixed_kernel(here, query_ref, back_ref, intra_ref, carried_ref, local_ref, scarried_ref, *refs):
    near, far = refs[:NX], refs[NX]
    mixed_ref, dec_ref, send_ref, carry_ref = refs[NX + 1 :]
    for dx in range(NX):
        carry_ref[mate_head(here, dx, 0)] = near[dx][0]
        carry_ref[mate_head(here, dx, 1)] = far[dx]
    acc = jnp.zeros((NROW, HDIM), F32)
    for h in range(HEADS):
        cols = slice(h * HDIM, (h + 1) * HDIM)
        dec = local_ref[:, cols] + carry_ref[h] * scarried_ref[:, h : h + 1]
        dec_ref[:, cols] = dec
        acc = acc + dec * dec
    full = jnp.concatenate([acc, jnp.zeros((HDIM - NROW, HDIM), F32)], axis=0)
    dflat = jnp.sum(full.T, axis=0, keepdims=True)

    acc = jnp.zeros((BLOCK, HDIM), F32)
    for h in range(HEADS):
        cols = slice(h * HDIM, (h + 1) * HDIM)
        state = jnp.concatenate([back_ref[owner(h, g)] for g in range(NQ)], axis=0).astype(BF)
        outer = jnp.dot(query_ref[:, cols], state, preferred_element_type=F32)
        mixed = intra_ref[:, cols] + outer * carried_ref[:, h : h + 1]
        mixed_ref[:, cols] = mixed
        acc = acc + mixed * mixed
    flat = jnp.sum(acc.T, axis=0, keepdims=True)
    both = jnp.concatenate([flat[:, :HDIM], flat[:, HDIM:], dflat, dflat], axis=0)
    for k in range(HEADS):
        send_ref[k] = both


def final_kernel(sums_ref, mixed_ref, dec_ref, gain_ref, attn_ref, out_ref):
    total = sums_ref[0]
    for k in range(1, HEADS):
        total = total + sums_ref[k]
    scale = lax.rsqrt(total / (HEAD_COUNT * HDIM) + EPSILON)
    gain = gain_ref[...]

    def column(row):
        return jnp.broadcast_to(scale[row : row + 1, :], (HDIM, HDIM)).T

    for half in range(2):
        part = slice(half * HDIM, (half + 1) * HDIM)
        col = column(half)
        for h in range(HEADS):
            cols = slice(h * HDIM, (h + 1) * HDIM)
            attn_ref[part, cols] = (mixed_ref[part, cols] * col * gain[:, cols]).astype(BF)
    col = column(2)
    for h in range(HEADS):
        cols = slice(h * HDIM, (h + 1) * HDIM)
        res = (dec_ref[:, cols] * col[: STEPS * ROWS_DEV, :] * gain[:, cols]).astype(BF)
        for step in range(STEPS):
            out_ref[step, :, cols] = res[step * ROWS_DEV : (step + 1) * ROWS_DEV, :]


def shape(*dims, dtype=F32):
    return jax.ShapeDtypeStruct(dims, dtype)


def shift(x, axis, size, d):
    return lax.ppermute(x, axis, [(i, (i + d) % size) for i in range(size)])


def over_pair(pieces):
    both = jnp.stack([piece[1] for piece in pieces])
    return lax.ppermute(both, "seq_1", [(i, i ^ 1) for i in range(NZ)])


def exchange(x, axis):
    return lax.all_to_all(x, axis, split_axis=0, concat_axis=0, tiled=True)


def more_tails(key_in, value_in, log_decay, prompt_lengths, first):
    ends = jnp.cumsum(prompt_lengths)
    positions = first + jnp.arange(BLOCK, dtype=jnp.int32)
    segs = jnp.sum((positions[:, None] >= ends[None, :]).astype(jnp.int32), axis=1)
    cum = jnp.cumsum(log_decay, axis=0)
    keys = key_in.reshape(BLOCK, HEADS, HDIM)
    values = value_in.reshape(BLOCK, HEADS, HDIM)
    parts = []
    for p in (1, 2):
        local = ends[p] - 1 - first
        owned = (local >= 0) & (local < BLOCK) & (ends[p - 1] - 1 >= first)
        safe = jnp.clip(local, 0, BLOCK - 1)
        taken = (jnp.arange(BLOCK) <= safe) & (segs == p) & owned
        spread = jnp.where(taken[:, None], cum[safe][None, :] - cum, 0.0)
        keep = jnp.where(taken[:, None], jnp.exp(spread), 0.0)
        tailed = (keys.astype(F32) * keep[:, :, None]).astype(BF)
        part = jnp.einsum("shd,she->hde", tailed, values, preferred_element_type=F32)
        part = part.reshape(NX, 2, NQ, QUART, HDIM).transpose(0, 2, 1, 3, 4)
        parts.append(part.reshape(NDEV, QUART, HDIM))
    got = exchange(jnp.concatenate(parts, axis=1), SEQ)
    both = jnp.sum(got, axis=0)
    return jnp.stack([jnp.zeros((QUART, HDIM), F32), both[:QUART], both[QUART:]])


def local(
    query_in,
    key_in,
    value_in,
    log_decay,
    norm_gain,
    prompt_lengths,
    step_query,
    step_key,
    step_value,
    step_decay,
    row_prompt,
):
    me = lax.axis_index(SEQ).astype(jnp.int32)
    here = me[None]
    width = HEADS * HDIM
    n = STEPS * ROWS_DEV

    logd = log_decay.T
    give, crowded = pl.pallas_call(
        send_kernel,
        out_shape=(shape(NDEV, GIVE, HDIM), shape(1, dtype=jnp.int32)),
        in_specs=[SMEM] * 2 + [PLACE] * 2 + [VMEM],
        out_specs=(VMEM, SMEM),
        scratch_shapes=[
            pltpu.VMEM((BLOCK, width), BF),
            pltpu.VMEM((BLOCK, width), BF),
            pltpu.VMEM((BLOCK, HEADS), F32),
            pltpu.SemaphoreType.DMA((2,)),
        ],
        compiler_params=params(),
        cost_estimate=cost(3),
        name="send",
    )(prompt_lengths, here, key_in, value_in, logd)
    given = exchange(give, SEQ)

    queries = pl.pallas_call(
        query_kernel,
        out_shape=(shape(2, ASK, HDIM),) * NX,
        in_specs=[SMEM] * 2 + [VMEM],
        out_specs=(VMEM,) * NX,
        compiler_params=params(),
        cost_estimate=cost(1),
        name="query",
    )(here, row_prompt, step_query)
    queries = [queries[0]] + [shift(queries[d], "seq_0", NX, d) for d in range(1, NX)]
    far_queries = over_pair(queries)

    intra, carried = pl.pallas_call(
        intra_kernel,
        out_shape=(shape(BLOCK, width), shape(BLOCK, HEADS)),
        in_specs=[SMEM] * 2 + [VMEM] * 4,
        out_specs=(VMEM,) * 2,
        compiler_params=params(),
        cost_estimate=cost(3),
        name="intra",
    )(prompt_lengths, here, query_in, key_in, value_in, logd)

    given, intra, carried, crowded, queries, far_queries = lax.optimization_barrier(
        (given, intra, carried, crowded, queries, far_queries)
    )

    def scan(*extra):
        return pl.pallas_call(
            scan_kernel,
            out_shape=(shape(NDEV, QUART, HDIM), shape(PROMPTS, QUART, HDIM)),
            in_specs=[SMEM] + [VMEM] * (1 + len(extra)),
            out_specs=(VMEM,) * 2,
            compiler_params=params(),
            cost_estimate=cost(2),
            name="scan",
        )(prompt_lengths, given, *extra)

    entry, own = lax.cond(
        crowded[0] > 0,
        lambda: scan(more_tails(key_in, value_in, log_decay, prompt_lengths, me * BLOCK)),
        scan,
    )
    slabs = [own] + [shift(own, "seq_1", NZ, 2 * d) for d in range(1, NQ)]
    entry, slabs, step_key = lax.optimization_barrier((entry, slabs, step_key))
    back = exchange(entry, SEQ)

    local_dec, scarried = pl.pallas_call(
        local_kernel,
        out_shape=(shape(n, width), shape(n, HEADS)),
        in_specs=[VMEM] * 4,
        out_specs=(VMEM,) * 2,
        compiler_params=params(),
        cost_estimate=cost(1),
        name="local",
    )(step_query, step_key, step_value, step_decay.transpose(0, 2, 1))

    products = pl.pallas_call(
        project_kernel,
        out_shape=(shape(2, NROW, HDIM),) * NX,
        in_specs=[SMEM] + [VMEM] * (NX + 1 + NQ),
        out_specs=(VMEM,) * NX,
        scratch_shapes=[pltpu.VMEM((PROMPTS * HDIM, HDIM), F32)],
        compiler_params=params(),
        cost_estimate=cost(2),
        name="project",
    )(here, *queries, far_queries, *slabs)
    products = [products[0]] + [shift(products[d], "seq_0", NX, -d) for d in range(1, NX)]
    far_products = over_pair(products)

    mixed, dec, sums_send = pl.pallas_call(
        mixed_kernel,
        out_shape=(shape(BLOCK, width), shape(n, width), shape(HEADS, 4, HDIM)),
        in_specs=[SMEM] + [VMEM] * (7 + NX),
        out_specs=(VMEM,) * 3,
        scratch_shapes=[pltpu.VMEM((HEADS, NROW, HDIM), F32)],
        compiler_params=params(),
        cost_estimate=cost(2),
        name="mixed",
    )(here, query_in, back, intra, carried, local_dec, scarried, *products, far_products)
    sums_all = exchange(sums_send, "head")

    return pl.pallas_call(
        final_kernel,
        out_shape=(shape(BLOCK, width, dtype=BF), shape(STEPS, ROWS_DEV, width, dtype=BF)),
        in_specs=[VMEM] * 4,
        out_specs=(VMEM,) * 2,
        compiler_params=params(),
        cost_estimate=cost(2),
        name="final",
    )(sums_all, mixed, dec, norm_gain.reshape(1, width))


def solution(mesh):
    split = Mesh(mesh.devices.reshape(NX, NZ, mesh.shape["head"]), ("seq_0", "seq_1", "head"))
    placed = (
        P(SEQ, "head"),
        P(SEQ, "head"),
        P(SEQ, "head"),
        P(SEQ, "head"),
        P("head"),
        P(),
        P(None, SEQ, "head"),
        P(None, SEQ, "head"),
        P(None, SEQ, "head"),
        P(None, SEQ, "head"),
        P(SEQ),
    )
    return jax.shard_map(
        local,
        mesh=split,
        in_specs=placed,
        out_specs=(P(SEQ, "head"), P(None, SEQ, "head")),
        check_vma=False,
    )
```

```python
import functools

import jax
import jax.numpy as jnp
from jax import lax
from jax.experimental import pallas as pl
from jax.experimental.pallas import tpu as pltpu
from jax.sharding import Mesh
from jax.sharding import PartitionSpec as P

HEAD_COUNT = 64
HDIM = 128
BLOCK = 256
PROMPTS = 4
STEPS = 4
SEQ = ("seq_0", "seq_1")
EPSILON = 1e-06

NX = 4
NZ = 8
HEADS = 8
NDEV = NX * NZ
NQ = NZ // 2
QUART = HDIM // NQ
ROWS_DEV = 16
NROW = STEPS * ROWS_DEV
LAST = PROMPTS - 1
ASK = NROW + 8

T0 = QUART
S0 = 2 * QUART
GIVE = S0 + 8

BF = jnp.bfloat16
F32 = jnp.float32
HI = lax.Precision.HIGHEST

SMEM = pl.BlockSpec(memory_space=pltpu.SMEM)
VMEM = pl.BlockSpec(memory_space=pltpu.VMEM)


def params(mib=12):
    return pltpu.CompilerParams(vmem_limit_bytes=mib << 20)


def cost(us):
    return pl.CostEstimate(flops=int(us * 1e9), bytes_accessed=int(us * 3e6), transcendentals=0)


def bounds(lens):
    ends = []
    total = lens[0]
    for p in range(PROMPTS):
        if p:
            total = total + lens[p]
        ends.append(total)
    return ends


def seg_of(pos, ends):
    out = (pos >= ends[0]).astype(jnp.int32)
    for p in range(1, PROMPTS):
        out = out + (pos >= ends[p]).astype(jnp.int32)
    return out


def entry_seg(first, ends):
    return jnp.where(first > 0, seg_of(first - 1, ends), -1)


def cum_columns(logd):
    t = lax.broadcasted_iota(jnp.int32, (BLOCK, BLOCK), 0)
    s = lax.broadcasted_iota(jnp.int32, (BLOCK, BLOCK), 1)
    return lax.dot_general(
        (s <= t).astype(F32), logd, (((1,), (1,)), ((), ())), precision=HI, preferred_element_type=F32
    )


def contract_rows(a, b):
    return lax.dot_general(a, b, (((0,), (0,)), ((), ())), preferred_element_type=F32)


def contract_cols(a, b):
    return lax.dot_general(a, b, (((1,), (1,)), ((), ())), preferred_element_type=F32)


def owner(head, quarter):
    return (head // 2) * NZ + 2 * quarter + head % 2


def cum_rows_of(logd):
    s = lax.broadcasted_iota(jnp.int32, (BLOCK, BLOCK), 0)
    t = lax.broadcasted_iota(jnp.int32, (BLOCK, BLOCK), 1)
    tri = (s <= t).astype(BF)
    total = jnp.zeros((HEADS, BLOCK), F32)
    rest = logd
    for _ in range(3):
        term = rest.astype(BF)
        total = total + jnp.dot(term, tri, preferred_element_type=F32)
        rest = rest - term.astype(F32)
    return total


def send_kernel(lens, here, key_ref, value_ref, logd_ref, out_ref, flag_ref):
    first = here[0] * BLOCK
    ends = bounds(lens)
    front = entry_seg(first, ends)
    seg_last = seg_of(first + (BLOCK - 1), ends)
    cum = cum_rows_of(logd_ref[...])
    tok = lax.broadcasted_iota(jnp.int32, (HEADS, BLOCK), 1)
    seg = seg_of(tok + first, ends)

    def at_token(spot):
        return jnp.sum(jnp.where(tok == spot, cum, 0.0), axis=1, keepdims=True)

    last = cum[:, BLOCK - 1 : BLOCK]
    keep = jnp.where(seg == seg_last, jnp.exp(last - cum), 0.0)
    factors = [jnp.exp(last) * (seg_last == front).astype(F32)]
    found = jnp.int32(-1)
    spot = jnp.int32(0)
    crowded = jnp.int32(0)
    for p in range(LAST):
        at = ends[p] - 1 - first
        inside = (at >= 0) & (at < BLOCK)
        factors.append(jnp.exp(at_token(at)) * (inside & (front == p)).astype(F32))
        take = (at >= 0) & (at < BLOCK - 1) & (found < 0)
        found = jnp.where(take, p, found)
        spot = jnp.where(take, at, spot)
        if p:
            same = (ends[p] - 1) // BLOCK == (ends[p - 1] - 1) // BLOCK
            crowded = crowded | (same & (ends[p] % BLOCK != 0)).astype(jnp.int32)
    flag_ref[0] = crowded
    taken = (tok <= spot) & (seg == found)
    tail = jnp.where(taken, jnp.exp(jnp.where(taken, at_token(spot) - cum, 0.0)), 0.0)

    for h in range(HEADS):
        cols = slice(h * HDIM, (h + 1) * HDIM)
        keys = key_ref[:, cols].T.astype(F32)
        scaled = jnp.concatenate(
            [(keys * keep[h : h + 1, :]).astype(BF), (keys * tail[h : h + 1, :]).astype(BF)], axis=0
        )
        total = jnp.dot(scaled, value_ref[:, cols], preferred_element_type=F32)
        scal = jnp.concatenate(
            [jnp.broadcast_to(f[h : h + 1, :], (1, HDIM)) for f in factors]
            + [jnp.zeros((8 - len(factors), HDIM), F32)],
            axis=0,
        )
        for g in range(NQ):
            rows = slice(g * QUART, (g + 1) * QUART)
            out_ref[owner(h, g), 0:T0, :] = total[rows, :]
            out_ref[owner(h, g), T0:S0, :] = total[HDIM + g * QUART : HDIM + (g + 1) * QUART, :]
            out_ref[owner(h, g), S0:GIVE, :] = scal


def mate_head(here, dx, db):
    x = here[0] // NZ
    parity = lax.rem(here[0], 2)
    return 2 * lax.rem(x + dx, NX) + (1 - parity if db else parity)


def query_kernel(here, rows, query_ref, *out_refs):
    lane = lax.broadcasted_iota(jnp.int32, (8, HDIM), 1)
    ids = jnp.zeros((8, HDIM), F32)
    for k in range(ROWS_DEV):
        ids = jnp.where(lane == k, rows[k].astype(F32), ids)
    for dx, out_ref in enumerate(out_refs):
        for db in range(2):
            cols = pl.ds(pl.multiple_of(mate_head(here, dx, db) * HDIM, HDIM), HDIM)
            out_ref[db, :NROW, :] = query_ref[:, :, cols].astype(F32).reshape(NROW, HDIM)
            out_ref[db, NROW:, :] = ids


def intra_kernel(
    lens, here, query_ref, key_ref, value_ref, logd_ref, intra_ref, carried_ref
):
    first = here[0] * BLOCK
    ends = bounds(lens)
    front = entry_seg(first, ends)
    logd = logd_ref[...]
    t = lax.broadcasted_iota(jnp.int32, (BLOCK, BLOCK), 0)
    s = lax.broadcasted_iota(jnp.int32, (BLOCK, BLOCK), 1)
    cum = cum_columns(logd)
    cum_rows = jnp.dot(logd, (t <= s).astype(F32), precision=HI, preferred_element_type=F32)
    linked = (s <= t) & (seg_of(t + first, ends) == seg_of(s + first, ends))
    tok = lax.broadcasted_iota(jnp.int32, (BLOCK, HEADS), 0)
    carried_ref[...] = jnp.where(seg_of(tok + first, ends) == front, jnp.exp(cum), 0.0)
    for h in range(HEADS):
        cols = slice(h * HDIM, (h + 1) * HDIM)
        scores = contract_cols(query_ref[:, cols], key_ref[:, cols])
        spread = cum[:, h : h + 1] - cum_rows[h : h + 1, :]
        factor = jnp.exp(jnp.where(linked, spread, -1e30))
        weights = (scores * factor).astype(BF)
        intra_ref[:, cols] = jnp.dot(weights, value_ref[:, cols], preferred_element_type=F32)


def local_kernel(sq_ref, sk_ref, sv_ref, sd_ref, local_ref, scarried_ref):
    n = NROW
    a = lax.broadcasted_iota(jnp.int32, (n, n), 0)
    b = lax.broadcasted_iota(jnp.int32, (n, n), 1)
    same = (b <= a) & ((a - b) % ROWS_DEV == 0)
    total = sd_ref[0]
    pieces = [total]
    for step in range(1, STEPS):
        total = total + sd_ref[step]
        pieces.append(total)
    scum_rows = jnp.concatenate(pieces, axis=1)
    scum = lax.dot_general(
        (a == b).astype(F32), scum_rows, (((1,), (1,)), ((), ())), precision=HI,
        preferred_element_type=F32,
    )
    scarried_ref[...] = jnp.exp(scum)
    for h in range(HEADS):
        cols = slice(h * HDIM, (h + 1) * HDIM)
        q = sq_ref[:, :, cols].reshape(n, HDIM)
        k = sk_ref[:, :, cols].reshape(n, HDIM)
        v = sv_ref[:, :, cols].reshape(n, HDIM)
        spread = scum[:, h : h + 1] - scum_rows[h : h + 1, :]
        weights = contract_cols(q, k) * jnp.exp(jnp.where(same, spread, -1e30))
        high = weights.astype(BF)
        low = (weights - high.astype(F32)).astype(BF)
        local_ref[:, cols] = jnp.dot(high, v, preferred_element_type=F32) + jnp.dot(
            low, v, preferred_element_type=F32
        )


def scan_kernel(lens, give_ref, extra_ref, entry_ref, slice_ref):
    ends = bounds(lens)
    state = jnp.zeros((QUART, HDIM), F32)
    for k in range(NDEV):
        entry_ref[k] = state
        state = give_ref[k, S0 : S0 + 1, :] * state + give_ref[k, 0:T0, :]
    slice_ref[LAST] = state
    earlier = []
    for p in range(LAST):
        e = ends[p] - 1
        b = e // BLOCK
        slot = jnp.int32(0)
        for other in earlier:
            slot = slot + (other == b).astype(jnp.int32)
        earlier.append(b)
        whole = e % BLOCK == BLOCK - 1
        lead = give_ref[b, S0 + 1 + p : S0 + 2 + p, :]
        tail = jnp.where(slot == 0, give_ref[b, T0:S0, :], extra_ref[p])
        tail = jnp.where(whole, give_ref[b, 0:T0, :], tail)
        slice_ref[p] = lead * entry_ref[b] + tail


def project_kernel(here, *refs):
    near, far, slabs, outs, st_ref = refs[:NX], refs[NX], refs[NX + 1 : NX + 1 + NQ], refs[NX + 1 + NQ : -1], refs[-1]
    quarter = lax.rem(here[0], NZ) // 2
    for d, ref in enumerate(slabs):
        origin = lax.rem(quarter - d + NQ, NQ)
        for p in range(PROMPTS):
            at = pl.multiple_of(p * HDIM + origin * QUART, QUART)
            st_ref[pl.ds(at, QUART), :] = ref[p]
    st = st_ref[...]
    high = st.astype(BF)
    low = (st - high.astype(F32)).astype(BF)
    r = lax.broadcasted_iota(jnp.int32, (NROW, HDIM), 0) % ROWS_DEV
    c = lax.broadcasted_iota(jnp.int32, (NROW, HDIM), 1)
    rows = []
    for msg in [ref[0] for ref in near] + [far[dx] for dx in range(NX)]:
        q = msg[:NROW, :]
        ids = jnp.broadcast_to(msg[NROW : NROW + 1, :], (NROW, HDIM))
        prompt = jnp.sum(jnp.where(r == c, ids, 0.0), axis=1, keepdims=True)
        rows.append(
            jnp.concatenate(
                [jnp.where(prompt == float(p), q, 0.0).astype(BF) for p in range(PROMPTS)], axis=1
            )
        )
    wide = jnp.concatenate(rows, axis=0)
    res = jnp.dot(wide, high, preferred_element_type=F32) + jnp.dot(
        wide, low, preferred_element_type=F32
    )
    for dx, ref in enumerate(outs):
        for db in range(2):
            at = (db * NX + dx) * NROW
            ref[db] = res[at : at + NROW, :]


def mixed_kernel(here, query_ref, back_ref, intra_ref, carried_ref, local_ref, scarried_ref, *refs):
    near, far = refs[:NX], refs[NX]
    mixed_ref, dec_ref, send_ref, carry_ref = refs[NX + 1 :]
    for dx in range(NX):
        carry_ref[mate_head(here, dx, 0)] = near[dx][0]
        carry_ref[mate_head(here, dx, 1)] = far[dx]
    acc = jnp.zeros((NROW, HDIM), F32)
    for h in range(HEADS):
        cols = slice(h * HDIM, (h + 1) * HDIM)
        dec = local_ref[:, cols] + carry_ref[h] * scarried_ref[:, h : h + 1]
        dec_ref[:, cols] = dec
        acc = acc + dec * dec
    full = jnp.concatenate([acc, jnp.zeros((HDIM - NROW, HDIM), F32)], axis=0)
    dflat = jnp.sum(full.T, axis=0, keepdims=True)

    acc = jnp.zeros((BLOCK, HDIM), F32)
    for h in range(HEADS):
        cols = slice(h * HDIM, (h + 1) * HDIM)
        state = jnp.concatenate([back_ref[owner(h, g)] for g in range(NQ)], axis=0).astype(BF)
        outer = jnp.dot(query_ref[:, cols], state, preferred_element_type=F32)
        mixed = intra_ref[:, cols] + outer * carried_ref[:, h : h + 1]
        mixed_ref[:, cols] = mixed
        acc = acc + mixed * mixed
    flat = jnp.sum(acc.T, axis=0, keepdims=True)
    both = jnp.concatenate([flat[:, :HDIM], flat[:, HDIM:], dflat, dflat], axis=0)
    for k in range(HEADS):
        send_ref[k] = both


def final_kernel(sums_ref, mixed_ref, dec_ref, gain_ref, attn_ref, out_ref):
    total = sums_ref[0]
    for k in range(1, HEADS):
        total = total + sums_ref[k]
    scale = lax.rsqrt(total / (HEAD_COUNT * HDIM) + EPSILON)
    gain = gain_ref[...]

    def column(row):
        return jnp.broadcast_to(scale[row : row + 1, :], (HDIM, HDIM)).T

    for half in range(2):
        part = slice(half * HDIM, (half + 1) * HDIM)
        col = column(half)
        for h in range(HEADS):
            cols = slice(h * HDIM, (h + 1) * HDIM)
            attn_ref[part, cols] = (mixed_ref[part, cols] * col * gain[:, cols]).astype(BF)
    col = column(2)
    for h in range(HEADS):
        cols = slice(h * HDIM, (h + 1) * HDIM)
        res = (dec_ref[:, cols] * col[: STEPS * ROWS_DEV, :] * gain[:, cols]).astype(BF)
        for step in range(STEPS):
            out_ref[step, :, cols] = res[step * ROWS_DEV : (step + 1) * ROWS_DEV, :]


def shape(*dims, dtype=F32):
    return jax.ShapeDtypeStruct(dims, dtype)


def shift(x, axis, size, d):
    return lax.ppermute(x, axis, [(i, (i + d) % size) for i in range(size)])


def over_pair(pieces):
    both = jnp.stack([piece[1] for piece in pieces])
    return lax.ppermute(both, "seq_1", [(i, i ^ 1) for i in range(NZ)])


def exchange(x, axis):
    return lax.all_to_all(x, axis, split_axis=0, concat_axis=0, tiled=True)


def more_tails(key_in, value_in, log_decay, prompt_lengths, first):
    ends = jnp.cumsum(prompt_lengths)
    positions = first + jnp.arange(BLOCK, dtype=jnp.int32)
    segs = jnp.sum((positions[:, None] >= ends[None, :]).astype(jnp.int32), axis=1)
    cum = jnp.cumsum(log_decay, axis=0)
    keys = key_in.reshape(BLOCK, HEADS, HDIM)
    values = value_in.reshape(BLOCK, HEADS, HDIM)
    parts = []
    for p in (1, 2):
        local = ends[p] - 1 - first
        owned = (local >= 0) & (local < BLOCK) & (ends[p - 1] - 1 >= first)
        safe = jnp.clip(local, 0, BLOCK - 1)
        taken = (jnp.arange(BLOCK) <= safe) & (segs == p) & owned
        spread = jnp.where(taken[:, None], cum[safe][None, :] - cum, 0.0)
        keep = jnp.where(taken[:, None], jnp.exp(spread), 0.0)
        tailed = (keys.astype(F32) * keep[:, :, None]).astype(BF)
        part = jnp.einsum("shd,she->hde", tailed, values, preferred_element_type=F32)
        part = part.reshape(NX, 2, NQ, QUART, HDIM).transpose(0, 2, 1, 3, 4)
        parts.append(part.reshape(NDEV, QUART, HDIM))
    got = exchange(jnp.concatenate(parts, axis=1), SEQ)
    both = jnp.sum(got, axis=0)
    return jnp.stack([jnp.zeros((QUART, HDIM), F32), both[:QUART], both[QUART:]])


def local(
    query_in,
    key_in,
    value_in,
    log_decay,
    norm_gain,
    prompt_lengths,
    step_query,
    step_key,
    step_value,
    step_decay,
    row_prompt,
):
    me = lax.axis_index(SEQ).astype(jnp.int32)
    here = me[None]
    width = HEADS * HDIM
    n = STEPS * ROWS_DEV

    logd = log_decay.T
    give, crowded = pl.pallas_call(
        send_kernel,
        out_shape=(shape(NDEV, GIVE, HDIM), shape(1, dtype=jnp.int32)),
        in_specs=[SMEM] * 2 + [VMEM] * 3,
        out_specs=(VMEM, SMEM),
        compiler_params=params(),
        cost_estimate=cost(3),
        name="send",
    )(prompt_lengths, here, key_in, value_in, logd)
    given = exchange(give, SEQ)

    queries = pl.pallas_call(
        query_kernel,
        out_shape=(shape(2, ASK, HDIM),) * NX,
        in_specs=[SMEM] * 2 + [VMEM],
        out_specs=(VMEM,) * NX,
        compiler_params=params(),
        cost_estimate=cost(1),
        name="query",
    )(here, row_prompt, step_query)
    queries = [queries[0]] + [shift(queries[d], "seq_0", NX, d) for d in range(1, NX)]
    far_queries = over_pair(queries)

    intra, carried = pl.pallas_call(
        intra_kernel,
        out_shape=(shape(BLOCK, width), shape(BLOCK, HEADS)),
        in_specs=[SMEM] * 2 + [VMEM] * 4,
        out_specs=(VMEM,) * 2,
        compiler_params=params(),
        cost_estimate=cost(3),
        name="intra",
    )(prompt_lengths, here, query_in, key_in, value_in, logd)

    given, intra, carried, crowded, queries, far_queries = lax.optimization_barrier(
        (given, intra, carried, crowded, queries, far_queries)
    )
    extra = lax.cond(
        crowded[0] > 0,
        lambda: more_tails(key_in, value_in, log_decay, prompt_lengths, me * BLOCK),
        lambda: jnp.zeros((LAST, QUART, HDIM), F32),
    )
    entry, own = pl.pallas_call(
        scan_kernel,
        out_shape=(shape(NDEV, QUART, HDIM), shape(PROMPTS, QUART, HDIM)),
        in_specs=[SMEM] + [VMEM] * 2,
        out_specs=(VMEM,) * 2,
        compiler_params=params(),
        cost_estimate=cost(2),
        name="scan",
    )(prompt_lengths, given, extra)
    slabs = [own] + [shift(own, "seq_1", NZ, 2 * d) for d in range(1, NQ)]
    entry, slabs, step_key = lax.optimization_barrier((entry, slabs, step_key))
    back = exchange(entry, SEQ)

    local_dec, scarried = pl.pallas_call(
        local_kernel,
        out_shape=(shape(n, width), shape(n, HEADS)),
        in_specs=[VMEM] * 4,
        out_specs=(VMEM,) * 2,
        compiler_params=params(),
        cost_estimate=cost(1),
        name="local",
    )(step_query, step_key, step_value, step_decay.transpose(0, 2, 1))

    products = pl.pallas_call(
        project_kernel,
        out_shape=(shape(2, NROW, HDIM),) * NX,
        in_specs=[SMEM] + [VMEM] * (NX + 1 + NQ),
        out_specs=(VMEM,) * NX,
        scratch_shapes=[pltpu.VMEM((PROMPTS * HDIM, HDIM), F32)],
        compiler_params=params(),
        cost_estimate=cost(2),
        name="project",
    )(here, *queries, far_queries, *slabs)
    products = [products[0]] + [shift(products[d], "seq_0", NX, -d) for d in range(1, NX)]
    far_products = over_pair(products)

    mixed, dec, sums_send = pl.pallas_call(
        mixed_kernel,
        out_shape=(shape(BLOCK, width), shape(n, width), shape(HEADS, 4, HDIM)),
        in_specs=[SMEM] + [VMEM] * (7 + NX),
        out_specs=(VMEM,) * 3,
        scratch_shapes=[pltpu.VMEM((HEADS, NROW, HDIM), F32)],
        compiler_params=params(),
        cost_estimate=cost(2),
        name="mixed",
    )(here, query_in, back, intra, carried, local_dec, scarried, *products, far_products)
    sums_all = exchange(sums_send, "head")

    return pl.pallas_call(
        final_kernel,
        out_shape=(shape(BLOCK, width, dtype=BF), shape(STEPS, ROWS_DEV, width, dtype=BF)),
        in_specs=[VMEM] * 4,
        out_specs=(VMEM,) * 2,
        compiler_params=params(),
        cost_estimate=cost(2),
        name="final",
    )(sums_all, mixed, dec, norm_gain.reshape(1, width))


def solution(mesh):
    split = Mesh(mesh.devices.reshape(NX, NZ, mesh.shape["head"]), ("seq_0", "seq_1", "head"))
    placed = (
        P(SEQ, "head"),
        P(SEQ, "head"),
        P(SEQ, "head"),
        P(SEQ, "head"),
        P("head"),
        P(),
        P(None, SEQ, "head"),
        P(None, SEQ, "head"),
        P(None, SEQ, "head"),
        P(None, SEQ, "head"),
        P(SEQ),
    )
    return jax.shard_map(
        local,
        mesh=split,
        in_specs=placed,
        out_specs=(P(SEQ, "head"), P(None, SEQ, "head")),
        check_vma=False,
    )
```

```python
import functools

import jax
import jax.numpy as jnp
from jax import lax
from jax.experimental import pallas as pl
from jax.experimental.pallas import tpu as pltpu
from jax.sharding import Mesh
from jax.sharding import PartitionSpec as P

HEAD_COUNT = 64
HDIM = 128
BLOCK = 256
PROMPTS = 4
STEPS = 4
SEQ = ("seq_0", "seq_1")
EPSILON = 1e-06

NX = 4
NZ = 8
HEADS = 8
NDEV = NX * NZ
NQ = NZ // 2
QUART = HDIM // NQ
ROWS_DEV = 16
NROW = STEPS * ROWS_DEV
LAST = PROMPTS - 1
ASK = NROW + 8

T0 = QUART
S0 = 2 * QUART
GIVE = S0 + 8

BF = jnp.bfloat16
F32 = jnp.float32
HI = lax.Precision.HIGHEST

SMEM = pl.BlockSpec(memory_space=pltpu.SMEM)
VMEM = pl.BlockSpec(memory_space=pltpu.VMEM)


def params(mib=12):
    return pltpu.CompilerParams(vmem_limit_bytes=mib << 20)


def cost(us):
    return pl.CostEstimate(flops=int(us * 1e9), bytes_accessed=int(us * 3e6), transcendentals=0)


def bounds(lens):
    ends = []
    total = lens[0]
    for p in range(PROMPTS):
        if p:
            total = total + lens[p]
        ends.append(total)
    return ends


def seg_of(pos, ends):
    out = (pos >= ends[0]).astype(jnp.int32)
    for p in range(1, PROMPTS):
        out = out + (pos >= ends[p]).astype(jnp.int32)
    return out


def entry_seg(first, ends):
    return jnp.where(first > 0, seg_of(first - 1, ends), -1)


def cum_columns(logd):
    t = lax.broadcasted_iota(jnp.int32, (BLOCK, BLOCK), 0)
    s = lax.broadcasted_iota(jnp.int32, (BLOCK, BLOCK), 1)
    return lax.dot_general(
        (s <= t).astype(F32), logd, (((1,), (1,)), ((), ())), precision=HI, preferred_element_type=F32
    )


def contract_rows(a, b):
    return lax.dot_general(a, b, (((0,), (0,)), ((), ())), preferred_element_type=F32)


def contract_cols(a, b):
    return lax.dot_general(a, b, (((1,), (1,)), ((), ())), preferred_element_type=F32)


def owner(head, quarter):
    return (head // 2) * NZ + 2 * quarter + head % 2


def cum_rows_of(logd):
    s = lax.broadcasted_iota(jnp.int32, (BLOCK, BLOCK), 0)
    t = lax.broadcasted_iota(jnp.int32, (BLOCK, BLOCK), 1)
    tri = (s <= t).astype(BF)
    total = jnp.zeros((HEADS, BLOCK), F32)
    rest = logd
    for _ in range(3):
        term = rest.astype(BF)
        total = total + jnp.dot(term, tri, preferred_element_type=F32)
        rest = rest - term.astype(F32)
    return total


def send_kernel(lens, here, key_ref, value_ref, logd_ref, out_ref, flag_ref):
    first = here[0] * BLOCK
    ends = bounds(lens)
    front = entry_seg(first, ends)
    seg_last = seg_of(first + (BLOCK - 1), ends)
    cum = cum_rows_of(logd_ref[...])
    tok = lax.broadcasted_iota(jnp.int32, (HEADS, BLOCK), 1)
    seg = seg_of(tok + first, ends)

    def at_token(spot):
        return jnp.sum(jnp.where(tok == spot, cum, 0.0), axis=1, keepdims=True)

    last = cum[:, BLOCK - 1 : BLOCK]
    keep = jnp.where(seg == seg_last, jnp.exp(last - cum), 0.0)
    factors = [jnp.exp(last) * (seg_last == front).astype(F32)]
    found = jnp.int32(-1)
    spot = jnp.int32(0)
    crowded = jnp.int32(0)
    for p in range(LAST):
        at = ends[p] - 1 - first
        inside = (at >= 0) & (at < BLOCK)
        factors.append(jnp.exp(at_token(at)) * (inside & (front == p)).astype(F32))
        take = (at >= 0) & (at < BLOCK - 1) & (found < 0)
        found = jnp.where(take, p, found)
        spot = jnp.where(take, at, spot)
        if p:
            same = (ends[p] - 1) // BLOCK == (ends[p - 1] - 1) // BLOCK
            crowded = crowded | (same & (ends[p] % BLOCK != 0)).astype(jnp.int32)
    flag_ref[0] = crowded
    taken = (tok <= spot) & (seg == found)
    tail = jnp.where(taken, jnp.exp(jnp.where(taken, at_token(spot) - cum, 0.0)), 0.0)

    for h in range(HEADS):
        cols = slice(h * HDIM, (h + 1) * HDIM)
        keys = key_ref[:, cols].T.astype(F32)
        scaled = jnp.concatenate(
            [(keys * keep[h : h + 1, :]).astype(BF), (keys * tail[h : h + 1, :]).astype(BF)], axis=0
        )
        total = jnp.dot(scaled, value_ref[:, cols], preferred_element_type=F32)
        scal = jnp.concatenate(
            [jnp.broadcast_to(f[h : h + 1, :], (1, HDIM)) for f in factors]
            + [jnp.zeros((8 - len(factors), HDIM), F32)],
            axis=0,
        )
        for g in range(NQ):
            rows = slice(g * QUART, (g + 1) * QUART)
            out_ref[owner(h, g), 0:T0, :] = total[rows, :]
            out_ref[owner(h, g), T0:S0, :] = total[HDIM + g * QUART : HDIM + (g + 1) * QUART, :]
            out_ref[owner(h, g), S0:GIVE, :] = scal


def mate_head(here, dx, db):
    x = here[0] // NZ
    parity = lax.rem(here[0], 2)
    return 2 * lax.rem(x + dx, NX) + (1 - parity if db else parity)


def query_kernel(here, rows, query_ref, *out_refs):
    lane = lax.broadcasted_iota(jnp.int32, (8, HDIM), 1)
    ids = jnp.zeros((8, HDIM), F32)
    for k in range(ROWS_DEV):
        ids = jnp.where(lane == k, rows[k].astype(F32), ids)
    for dx, out_ref in enumerate(out_refs):
        for db in range(2):
            cols = pl.ds(pl.multiple_of(mate_head(here, dx, db) * HDIM, HDIM), HDIM)
            out_ref[db, :NROW, :] = query_ref[:, :, cols].astype(F32).reshape(NROW, HDIM)
            out_ref[db, NROW:, :] = ids


def intra_kernel(
    lens, here, query_ref, key_ref, value_ref, logd_ref, intra_ref, carried_ref
):
    first = here[0] * BLOCK
    ends = bounds(lens)
    front = entry_seg(first, ends)
    logd = logd_ref[...]
    t = lax.broadcasted_iota(jnp.int32, (BLOCK, BLOCK), 0)
    s = lax.broadcasted_iota(jnp.int32, (BLOCK, BLOCK), 1)
    cum = cum_columns(logd)
    cum_rows = jnp.dot(logd, (t <= s).astype(F32), precision=HI, preferred_element_type=F32)
    linked = (s <= t) & (seg_of(t + first, ends) == seg_of(s + first, ends))
    tok = lax.broadcasted_iota(jnp.int32, (BLOCK, HEADS), 0)
    carried_ref[...] = jnp.where(seg_of(tok + first, ends) == front, jnp.exp(cum), 0.0)
    for h in range(HEADS):
        cols = slice(h * HDIM, (h + 1) * HDIM)
        scores = contract_cols(query_ref[:, cols], key_ref[:, cols])
        spread = cum[:, h : h + 1] - cum_rows[h : h + 1, :]
        factor = jnp.exp(jnp.where(linked, spread, -1e30))
        weights = (scores * factor).astype(BF)
        intra_ref[:, cols] = jnp.dot(weights, value_ref[:, cols], preferred_element_type=F32)


def local_kernel(sq_ref, sk_ref, sv_ref, sd_ref, local_ref, scarried_ref):
    n = NROW
    a = lax.broadcasted_iota(jnp.int32, (n, n), 0)
    b = lax.broadcasted_iota(jnp.int32, (n, n), 1)
    same = (b <= a) & ((a - b) % ROWS_DEV == 0)
    total = sd_ref[0]
    pieces = [total]
    for step in range(1, STEPS):
        total = total + sd_ref[step]
        pieces.append(total)
    scum_rows = jnp.concatenate(pieces, axis=1)
    scum = lax.dot_general(
        (a == b).astype(F32), scum_rows, (((1,), (1,)), ((), ())), precision=HI,
        preferred_element_type=F32,
    )
    scarried_ref[...] = jnp.exp(scum)
    for h in range(HEADS):
        cols = slice(h * HDIM, (h + 1) * HDIM)
        q = sq_ref[:, :, cols].reshape(n, HDIM)
        k = sk_ref[:, :, cols].reshape(n, HDIM)
        v = sv_ref[:, :, cols].reshape(n, HDIM)
        spread = scum[:, h : h + 1] - scum_rows[h : h + 1, :]
        weights = contract_cols(q, k) * jnp.exp(jnp.where(same, spread, -1e30))
        high = weights.astype(BF)
        low = (weights - high.astype(F32)).astype(BF)
        local_ref[:, cols] = jnp.dot(high, v, preferred_element_type=F32) + jnp.dot(
            low, v, preferred_element_type=F32
        )


def slice_kernel(lens, give_ref, extra_ref, slice_ref, entry_ref):
    ends = bounds(lens)
    state = jnp.zeros((QUART, HDIM), F32)
    for k in range(NDEV):
        entry_ref[k] = state
        state = give_ref[k, S0 : S0 + 1, :] * state + give_ref[k, 0:T0, :]
    slice_ref[LAST] = state
    earlier = []
    for p in range(LAST):
        e = ends[p] - 1
        b = e // BLOCK
        slot = jnp.int32(0)
        for other in earlier:
            slot = slot + (other == b).astype(jnp.int32)
        earlier.append(b)
        whole = e % BLOCK == BLOCK - 1
        lead = give_ref[b, S0 + 1 + p : S0 + 2 + p, :]
        tail = jnp.where(slot == 0, give_ref[b, T0:S0, :], extra_ref[p])
        tail = jnp.where(whole, give_ref[b, 0:T0, :], tail)
        slice_ref[p] = lead * entry_ref[b] + tail


def entry_kernel(give_ref, entry_ref):
    state = jnp.zeros((QUART, HDIM), F32)
    for k in range(NDEV):
        entry_ref[k] = state
        state = give_ref[k, S0 : S0 + 1, :] * state + give_ref[k, 0:T0, :]


def project_kernel(here, *refs):
    near, far, slabs, outs, st_ref = refs[:NX], refs[NX], refs[NX + 1 : NX + 1 + NQ], refs[NX + 1 + NQ : -1], refs[-1]
    quarter = lax.rem(here[0], NZ) // 2
    for d, ref in enumerate(slabs):
        origin = lax.rem(quarter - d + NQ, NQ)
        for p in range(PROMPTS):
            at = pl.multiple_of(p * HDIM + origin * QUART, QUART)
            st_ref[pl.ds(at, QUART), :] = ref[p]
    st = st_ref[...]
    high = st.astype(BF)
    low = (st - high.astype(F32)).astype(BF)
    r = lax.broadcasted_iota(jnp.int32, (NROW, HDIM), 0) % ROWS_DEV
    c = lax.broadcasted_iota(jnp.int32, (NROW, HDIM), 1)
    rows = []
    for msg in [ref[0] for ref in near] + [far[dx] for dx in range(NX)]:
        q = msg[:NROW, :]
        ids = jnp.broadcast_to(msg[NROW : NROW + 1, :], (NROW, HDIM))
        prompt = jnp.sum(jnp.where(r == c, ids, 0.0), axis=1, keepdims=True)
        rows.append(
            jnp.concatenate(
                [jnp.where(prompt == float(p), q, 0.0).astype(BF) for p in range(PROMPTS)], axis=1
            )
        )
    wide = jnp.concatenate(rows, axis=0)
    res = jnp.dot(wide, high, preferred_element_type=F32) + jnp.dot(
        wide, low, preferred_element_type=F32
    )
    for dx, ref in enumerate(outs):
        for db in range(2):
            at = (db * NX + dx) * NROW
            ref[db] = res[at : at + NROW, :]


def mixed_kernel(query_ref, back_ref, intra_ref, carried_ref, mixed_ref, sums_ref):
    acc = jnp.zeros((BLOCK, HDIM), F32)
    for h in range(HEADS):
        cols = slice(h * HDIM, (h + 1) * HDIM)
        state = jnp.concatenate([back_ref[owner(h, g)] for g in range(NQ)], axis=0).astype(BF)
        outer = jnp.dot(query_ref[:, cols], state, preferred_element_type=F32)
        mixed = intra_ref[:, cols] + outer * carried_ref[:, h : h + 1]
        mixed_ref[:, cols] = mixed
        acc = acc + mixed * mixed
    flat = jnp.sum(acc.T, axis=0, keepdims=True)
    sums_ref[...] = jnp.concatenate(
        [flat[:, :HDIM], flat[:, HDIM:], jnp.zeros((6, HDIM), F32)], axis=0
    )


def decode_kernel(here, local_ref, scarried_ref, sums_ref, *refs):
    near, far = refs[:NX], refs[NX]
    dec_ref, send_ref, carry_ref = refs[NX + 1 :]
    for dx in range(NX):
        carry_ref[mate_head(here, dx, 0)] = near[dx][0]
        carry_ref[mate_head(here, dx, 1)] = far[dx]
    acc = jnp.zeros((NROW, HDIM), F32)
    for h in range(HEADS):
        cols = slice(h * HDIM, (h + 1) * HDIM)
        dec = local_ref[:, cols] + carry_ref[h] * scarried_ref[:, h : h + 1]
        dec_ref[:, cols] = dec
        acc = acc + dec * dec
    full = jnp.concatenate([acc, jnp.zeros((HDIM - NROW, HDIM), F32)], axis=0)
    dflat = jnp.sum(full.T, axis=0, keepdims=True)
    both = jnp.concatenate([sums_ref[0:2, :], dflat, dflat], axis=0)
    for k in range(HEADS):
        send_ref[k] = both


def final_kernel(sums_ref, mixed_ref, dec_ref, gain_ref, attn_ref, out_ref):
    total = sums_ref[0]
    for k in range(1, HEADS):
        total = total + sums_ref[k]
    scale = lax.rsqrt(total / (HEAD_COUNT * HDIM) + EPSILON)
    gain = gain_ref[...]

    def column(row):
        return jnp.broadcast_to(scale[row : row + 1, :], (HDIM, HDIM)).T

    for half in range(2):
        part = slice(half * HDIM, (half + 1) * HDIM)
        col = column(half)
        for h in range(HEADS):
            cols = slice(h * HDIM, (h + 1) * HDIM)
            attn_ref[part, cols] = (mixed_ref[part, cols] * col * gain[:, cols]).astype(BF)
    col = column(2)
    for h in range(HEADS):
        cols = slice(h * HDIM, (h + 1) * HDIM)
        res = (dec_ref[:, cols] * col[: STEPS * ROWS_DEV, :] * gain[:, cols]).astype(BF)
        for step in range(STEPS):
            out_ref[step, :, cols] = res[step * ROWS_DEV : (step + 1) * ROWS_DEV, :]


def shape(*dims, dtype=F32):
    return jax.ShapeDtypeStruct(dims, dtype)


def shift(x, axis, size, d):
    return lax.ppermute(x, axis, [(i, (i + d) % size) for i in range(size)])


def over_pair(pieces):
    both = jnp.stack([piece[1] for piece in pieces])
    return lax.ppermute(both, "seq_1", [(i, i ^ 1) for i in range(NZ)])


def exchange(x, axis):
    return lax.all_to_all(x, axis, split_axis=0, concat_axis=0, tiled=True)


def more_tails(key_in, value_in, log_decay, prompt_lengths, first):
    ends = jnp.cumsum(prompt_lengths)
    positions = first + jnp.arange(BLOCK, dtype=jnp.int32)
    segs = jnp.sum((positions[:, None] >= ends[None, :]).astype(jnp.int32), axis=1)
    cum = jnp.cumsum(log_decay, axis=0)
    keys = key_in.reshape(BLOCK, HEADS, HDIM)
    values = value_in.reshape(BLOCK, HEADS, HDIM)
    parts = []
    for p in (1, 2):
        local = ends[p] - 1 - first
        owned = (local >= 0) & (local < BLOCK) & (ends[p - 1] - 1 >= first)
        safe = jnp.clip(local, 0, BLOCK - 1)
        taken = (jnp.arange(BLOCK) <= safe) & (segs == p) & owned
        spread = jnp.where(taken[:, None], cum[safe][None, :] - cum, 0.0)
        keep = jnp.where(taken[:, None], jnp.exp(spread), 0.0)
        tailed = (keys.astype(F32) * keep[:, :, None]).astype(BF)
        part = jnp.einsum("shd,she->hde", tailed, values, preferred_element_type=F32)
        part = part.reshape(NX, 2, NQ, QUART, HDIM).transpose(0, 2, 1, 3, 4)
        parts.append(part.reshape(NDEV, QUART, HDIM))
    got = exchange(jnp.concatenate(parts, axis=1), SEQ)
    both = jnp.sum(got, axis=0)
    return jnp.stack([jnp.zeros((QUART, HDIM), F32), both[:QUART], both[QUART:]])


def local(
    query_in,
    key_in,
    value_in,
    log_decay,
    norm_gain,
    prompt_lengths,
    step_query,
    step_key,
    step_value,
    step_decay,
    row_prompt,
):
    me = lax.axis_index(SEQ).astype(jnp.int32)
    here = me[None]
    width = HEADS * HDIM
    n = STEPS * ROWS_DEV

    logd = log_decay.T
    give, crowded = pl.pallas_call(
        send_kernel,
        out_shape=(shape(NDEV, GIVE, HDIM), shape(1, dtype=jnp.int32)),
        in_specs=[SMEM] * 2 + [VMEM] * 3,
        out_specs=(VMEM, SMEM),
        compiler_params=params(),
        cost_estimate=cost(3),
        name="send",
    )(prompt_lengths, here, key_in, value_in, logd)
    given = exchange(give, SEQ)

    queries = pl.pallas_call(
        query_kernel,
        out_shape=(shape(2, ASK, HDIM),) * NX,
        in_specs=[SMEM] * 2 + [VMEM],
        out_specs=(VMEM,) * NX,
        compiler_params=params(),
        cost_estimate=cost(1),
        name="query",
    )(here, row_prompt, step_query)
    queries = [queries[0]] + [shift(queries[d], "seq_0", NX, d) for d in range(1, NX)]
    far_queries = over_pair(queries)

    intra, carried = pl.pallas_call(
        intra_kernel,
        out_shape=(shape(BLOCK, width), shape(BLOCK, HEADS)),
        in_specs=[SMEM] * 2 + [VMEM] * 4,
        out_specs=(VMEM,) * 2,
        compiler_params=params(),
        cost_estimate=cost(3),
        name="intra",
    )(prompt_lengths, here, query_in, key_in, value_in, logd)

    given, intra, carried, crowded, queries, far_queries = lax.optimization_barrier(
        (given, intra, carried, crowded, queries, far_queries)
    )
    extra = lax.cond(
        crowded[0] > 0,
        lambda: more_tails(key_in, value_in, log_decay, prompt_lengths, me * BLOCK),
        lambda: jnp.zeros((LAST, QUART, HDIM), F32),
    )
    own = pl.pallas_call(
        slice_kernel,
        out_shape=shape(PROMPTS, QUART, HDIM),
        in_specs=[SMEM] + [VMEM] * 2,
        out_specs=VMEM,
        scratch_shapes=[pltpu.VMEM((NDEV, QUART, HDIM), F32)],
        compiler_params=params(),
        cost_estimate=cost(1),
        name="slice",
    )(prompt_lengths, given, extra)
    given, own = lax.optimization_barrier((given, own))
    entry = pl.pallas_call(
        entry_kernel,
        out_shape=shape(NDEV, QUART, HDIM),
        in_specs=[VMEM],
        out_specs=VMEM,
        compiler_params=params(),
        cost_estimate=cost(2),
        name="entry",
    )(given)
    slabs = [own] + [shift(own, "seq_1", NZ, 2 * d) for d in range(1, NQ)]
    entry, slabs, step_key = lax.optimization_barrier((entry, slabs, step_key))
    back = exchange(entry, SEQ)

    local_dec, scarried = pl.pallas_call(
        local_kernel,
        out_shape=(shape(n, width), shape(n, HEADS)),
        in_specs=[VMEM] * 4,
        out_specs=(VMEM,) * 2,
        compiler_params=params(),
        cost_estimate=cost(1),
        name="local",
    )(step_query, step_key, step_value, step_decay.transpose(0, 2, 1))

    products = pl.pallas_call(
        project_kernel,
        out_shape=(shape(2, NROW, HDIM),) * NX,
        in_specs=[SMEM] + [VMEM] * (NX + 1 + NQ),
        out_specs=(VMEM,) * NX,
        scratch_shapes=[pltpu.VMEM((PROMPTS * HDIM, HDIM), F32)],
        compiler_params=params(),
        cost_estimate=cost(2),
        name="project",
    )(here, *queries, far_queries, *slabs)
    products = [products[0]] + [shift(products[d], "seq_0", NX, -d) for d in range(1, NX)]
    far_products = over_pair(products)

    mixed, sums = pl.pallas_call(
        mixed_kernel,
        out_shape=(shape(BLOCK, width), shape(8, HDIM)),
        in_specs=[VMEM] * 4,
        out_specs=(VMEM,) * 2,
        compiler_params=params(),
        cost_estimate=cost(1),
        name="mixed",
    )(query_in, back, intra, carried)
    dec, sums_send = pl.pallas_call(
        decode_kernel,
        out_shape=(shape(n, width), shape(HEADS, 4, HDIM)),
        in_specs=[SMEM] + [VMEM] * (4 + NX),
        out_specs=(VMEM,) * 2,
        scratch_shapes=[pltpu.VMEM((HEADS, NROW, HDIM), F32)],
        compiler_params=params(),
        cost_estimate=cost(1),
        name="decode",
    )(here, local_dec, scarried, sums, *products, far_products)
    sums_all = exchange(sums_send, "head")

    return pl.pallas_call(
        final_kernel,
        out_shape=(shape(BLOCK, width, dtype=BF), shape(STEPS, ROWS_DEV, width, dtype=BF)),
        in_specs=[VMEM] * 4,
        out_specs=(VMEM,) * 2,
        compiler_params=params(),
        cost_estimate=cost(2),
        name="final",
    )(sums_all, mixed, dec, norm_gain.reshape(1, width))


def solution(mesh):
    split = Mesh(mesh.devices.reshape(NX, NZ, mesh.shape["head"]), ("seq_0", "seq_1", "head"))
    placed = (
        P(SEQ, "head"),
        P(SEQ, "head"),
        P(SEQ, "head"),
        P(SEQ, "head"),
        P("head"),
        P(),
        P(None, SEQ, "head"),
        P(None, SEQ, "head"),
        P(None, SEQ, "head"),
        P(None, SEQ, "head"),
        P(SEQ),
    )
    return jax.shard_map(
        local,
        mesh=split,
        in_specs=placed,
        out_specs=(P(SEQ, "head"), P(None, SEQ, "head")),
        check_vma=False,
    )
```

```python
import functools

import jax
import jax.numpy as jnp
from jax import lax
from jax.experimental import pallas as pl
from jax.experimental.pallas import tpu as pltpu
from jax.sharding import Mesh
from jax.sharding import PartitionSpec as P

HEAD_COUNT = 64
HDIM = 128
BLOCK = 256
PROMPTS = 4
STEPS = 4
SEQ = ("seq_0", "seq_1")
EPSILON = 1e-06

NX = 4
NZ = 8
HEADS = 8
NDEV = NX * NZ
NQ = NZ // 2
QUART = HDIM // NQ
ROWS_DEV = 16
NROW = STEPS * ROWS_DEV
LAST = PROMPTS - 1
ORDER = (0, 2, 1, 3)
ASK = NROW + 8

T0 = QUART
S0 = 2 * QUART
GIVE = S0 + 8

BF = jnp.bfloat16
F32 = jnp.float32
HI = lax.Precision.HIGHEST

SMEM = pl.BlockSpec(memory_space=pltpu.SMEM)
VMEM = pl.BlockSpec(memory_space=pltpu.VMEM)


def params(mib=12):
    return pltpu.CompilerParams(vmem_limit_bytes=mib << 20)


def cost(us):
    return pl.CostEstimate(flops=int(us * 1e9), bytes_accessed=int(us * 3e6), transcendentals=0)


def bounds(lens):
    ends = []
    total = lens[0]
    for p in range(PROMPTS):
        if p:
            total = total + lens[p]
        ends.append(total)
    return ends


def seg_of(pos, ends):
    out = (pos >= ends[0]).astype(jnp.int32)
    for p in range(1, PROMPTS):
        out = out + (pos >= ends[p]).astype(jnp.int32)
    return out


def entry_seg(first, ends):
    return jnp.where(first > 0, seg_of(first - 1, ends), -1)


def cum_columns(logd):
    t = lax.broadcasted_iota(jnp.int32, (BLOCK, BLOCK), 0)
    s = lax.broadcasted_iota(jnp.int32, (BLOCK, BLOCK), 1)
    return lax.dot_general(
        (s <= t).astype(F32), logd, (((1,), (1,)), ((), ())), precision=HI, preferred_element_type=F32
    )


def contract_rows(a, b):
    return lax.dot_general(a, b, (((0,), (0,)), ((), ())), preferred_element_type=F32)


def contract_cols(a, b):
    return lax.dot_general(a, b, (((1,), (1,)), ((), ())), preferred_element_type=F32)


def owner(head, quarter):
    return (head // 2) * NZ + 2 * quarter + head % 2


def cum_rows_of(logd):
    s = lax.broadcasted_iota(jnp.int32, (BLOCK, BLOCK), 0)
    t = lax.broadcasted_iota(jnp.int32, (BLOCK, BLOCK), 1)
    tri = (s <= t).astype(BF)
    total = jnp.zeros((HEADS, BLOCK), F32)
    rest = logd
    for _ in range(3):
        term = rest.astype(BF)
        total = total + jnp.dot(term, tri, preferred_element_type=F32)
        rest = rest - term.astype(F32)
    return total


def send_kernel(lens, here, key_ref, value_ref, logd_ref, out_ref, flag_ref):
    first = here[0] * BLOCK
    ends = bounds(lens)
    front = entry_seg(first, ends)
    seg_last = seg_of(first + (BLOCK - 1), ends)
    cum = cum_rows_of(logd_ref[...])
    tok = lax.broadcasted_iota(jnp.int32, (HEADS, BLOCK), 1)
    seg = seg_of(tok + first, ends)

    def at_token(spot):
        return jnp.sum(jnp.where(tok == spot, cum, 0.0), axis=1, keepdims=True)

    last = cum[:, BLOCK - 1 : BLOCK]
    keep = jnp.where(seg == seg_last, jnp.exp(last - cum), 0.0)
    factors = [jnp.exp(last) * (seg_last == front).astype(F32)]
    found = jnp.int32(-1)
    spot = jnp.int32(0)
    crowded = jnp.int32(0)
    for p in range(LAST):
        at = ends[p] - 1 - first
        inside = (at >= 0) & (at < BLOCK)
        factors.append(jnp.exp(at_token(at)) * (inside & (front == p)).astype(F32))
        take = (at >= 0) & (at < BLOCK - 1) & (found < 0)
        found = jnp.where(take, p, found)
        spot = jnp.where(take, at, spot)
        if p:
            same = (ends[p] - 1) // BLOCK == (ends[p - 1] - 1) // BLOCK
            crowded = crowded | (same & (ends[p] % BLOCK != 0)).astype(jnp.int32)
    flag_ref[0] = crowded
    taken = (tok <= spot) & (seg == found)
    tail = jnp.where(taken, jnp.exp(jnp.where(taken, at_token(spot) - cum, 0.0)), 0.0)

    for h in range(HEADS):
        cols = slice(h * HDIM, (h + 1) * HDIM)
        keys = key_ref[:, cols].T.astype(F32)
        scaled = jnp.concatenate(
            [(keys * keep[h : h + 1, :]).astype(BF), (keys * tail[h : h + 1, :]).astype(BF)], axis=0
        )
        total = jnp.dot(scaled, value_ref[:, cols], preferred_element_type=F32)
        scal = jnp.concatenate(
            [jnp.broadcast_to(f[h : h + 1, :], (1, HDIM)) for f in factors]
            + [jnp.zeros((8 - len(factors), HDIM), F32)],
            axis=0,
        )
        for g in range(NQ):
            rows = slice(g * QUART, (g + 1) * QUART)
            out_ref[owner(h, g), 0:T0, :] = total[rows, :]
            out_ref[owner(h, g), T0:S0, :] = total[HDIM + g * QUART : HDIM + (g + 1) * QUART, :]
            out_ref[owner(h, g), S0:GIVE, :] = scal


def mate_head(here, dx, db):
    x = here[0] // NZ
    parity = lax.rem(here[0], 2)
    return 2 * lax.rem(x + dx, NX) + (1 - parity if db else parity)


def query_kernel(here, rows, query_ref, *out_refs):
    lane = lax.broadcasted_iota(jnp.int32, (8, HDIM), 1)
    ids = jnp.zeros((8, HDIM), F32)
    for k in range(ROWS_DEV):
        ids = jnp.where(lane == k, rows[k].astype(F32), ids)
    for dx, out_ref in zip(ORDER, out_refs):
        for db in range(2):
            cols = pl.ds(pl.multiple_of(mate_head(here, dx, db) * HDIM, HDIM), HDIM)
            out_ref[db, :NROW, :] = query_ref[:, :, cols].astype(F32).reshape(NROW, HDIM)
            out_ref[db, NROW:, :] = ids


def intra_kernel(
    lens, here, query_ref, key_ref, value_ref, logd_ref, intra_ref, carried_ref
):
    first = here[0] * BLOCK
    ends = bounds(lens)
    front = entry_seg(first, ends)
    logd = logd_ref[...]
    t = lax.broadcasted_iota(jnp.int32, (BLOCK, BLOCK), 0)
    s = lax.broadcasted_iota(jnp.int32, (BLOCK, BLOCK), 1)
    cum = cum_columns(logd)
    cum_rows = jnp.dot(logd, (t <= s).astype(F32), precision=HI, preferred_element_type=F32)
    linked = (s <= t) & (seg_of(t + first, ends) == seg_of(s + first, ends))
    tok = lax.broadcasted_iota(jnp.int32, (BLOCK, HEADS), 0)
    carried_ref[...] = jnp.where(seg_of(tok + first, ends) == front, jnp.exp(cum), 0.0)
    for h in range(HEADS):
        cols = slice(h * HDIM, (h + 1) * HDIM)
        scores = contract_cols(query_ref[:, cols], key_ref[:, cols])
        spread = cum[:, h : h + 1] - cum_rows[h : h + 1, :]
        factor = jnp.exp(jnp.where(linked, spread, -1e30))
        weights = (scores * factor).astype(BF)
        intra_ref[:, cols] = jnp.dot(weights, value_ref[:, cols], preferred_element_type=F32)


def local_kernel(sq_ref, sk_ref, sv_ref, sd_ref, local_ref, scarried_ref):
    n = NROW
    a = lax.broadcasted_iota(jnp.int32, (n, n), 0)
    b = lax.broadcasted_iota(jnp.int32, (n, n), 1)
    same = (b <= a) & ((a - b) % ROWS_DEV == 0)
    total = sd_ref[0]
    pieces = [total]
    for step in range(1, STEPS):
        total = total + sd_ref[step]
        pieces.append(total)
    scum_rows = jnp.concatenate(pieces, axis=1)
    scum = lax.dot_general(
        (a == b).astype(F32), scum_rows, (((1,), (1,)), ((), ())), precision=HI,
        preferred_element_type=F32,
    )
    scarried_ref[...] = jnp.exp(scum)
    for h in range(HEADS):
        cols = slice(h * HDIM, (h + 1) * HDIM)
        q = sq_ref[:, :, cols].reshape(n, HDIM)
        k = sk_ref[:, :, cols].reshape(n, HDIM)
        v = sv_ref[:, :, cols].reshape(n, HDIM)
        spread = scum[:, h : h + 1] - scum_rows[h : h + 1, :]
        weights = contract_cols(q, k) * jnp.exp(jnp.where(same, spread, -1e30))
        high = weights.astype(BF)
        low = (weights - high.astype(F32)).astype(BF)
        local_ref[:, cols] = jnp.dot(high, v, preferred_element_type=F32) + jnp.dot(
            low, v, preferred_element_type=F32
        )


def slice_kernel(lens, give_ref, extra_ref, slice_ref, entry_ref):
    ends = bounds(lens)
    state = jnp.zeros((QUART, HDIM), F32)
    for k in range(NDEV):
        entry_ref[k] = state
        state = give_ref[k, S0 : S0 + 1, :] * state + give_ref[k, 0:T0, :]
    slice_ref[LAST] = state
    earlier = []
    for p in range(LAST):
        e = ends[p] - 1
        b = e // BLOCK
        slot = jnp.int32(0)
        for other in earlier:
            slot = slot + (other == b).astype(jnp.int32)
        earlier.append(b)
        whole = e % BLOCK == BLOCK - 1
        lead = give_ref[b, S0 + 1 + p : S0 + 2 + p, :]
        tail = jnp.where(slot == 0, give_ref[b, T0:S0, :], extra_ref[p])
        tail = jnp.where(whole, give_ref[b, 0:T0, :], tail)
        slice_ref[p] = lead * entry_ref[b] + tail


def entry_kernel(give_ref, entry_ref):
    state = jnp.zeros((QUART, HDIM), F32)
    for k in range(NDEV):
        entry_ref[k] = state
        state = give_ref[k, S0 : S0 + 1, :] * state + give_ref[k, 0:T0, :]


def project_kernel(here, *refs):
    near, far, slabs, outs, st_ref = refs[:NX], refs[NX], refs[NX + 1 : NX + 1 + NQ], refs[NX + 1 + NQ : -1], refs[-1]
    quarter = lax.rem(here[0], NZ) // 2
    for d, ref in zip(ORDER, slabs):
        origin = lax.rem(quarter - d + NQ, NQ)
        for p in range(PROMPTS):
            at = pl.multiple_of(p * HDIM + origin * QUART, QUART)
            st_ref[pl.ds(at, QUART), :] = ref[p]
    st = st_ref[...]
    high = st.astype(BF)
    low = (st - high.astype(F32)).astype(BF)
    r = lax.broadcasted_iota(jnp.int32, (NROW, HDIM), 0) % ROWS_DEV
    c = lax.broadcasted_iota(jnp.int32, (NROW, HDIM), 1)
    rows = []
    for msg in [ref[0] for ref in near] + [far[dx] for dx in range(NX)]:
        q = msg[:NROW, :]
        ids = jnp.broadcast_to(msg[NROW : NROW + 1, :], (NROW, HDIM))
        prompt = jnp.sum(jnp.where(r == c, ids, 0.0), axis=1, keepdims=True)
        rows.append(
            jnp.concatenate(
                [jnp.where(prompt == float(p), q, 0.0).astype(BF) for p in range(PROMPTS)], axis=1
            )
        )
    wide = jnp.concatenate(rows, axis=0)
    res = jnp.dot(wide, high, preferred_element_type=F32) + jnp.dot(
        wide, low, preferred_element_type=F32
    )
    for dx, ref in enumerate(outs):
        for db in range(2):
            at = (db * NX + dx) * NROW
            ref[db] = res[at : at + NROW, :]


def mixed_kernel(query_ref, back_ref, intra_ref, carried_ref, mixed_ref, sums_ref):
    acc = jnp.zeros((BLOCK, HDIM), F32)
    for h in range(HEADS):
        cols = slice(h * HDIM, (h + 1) * HDIM)
        state = jnp.concatenate([back_ref[owner(h, g)] for g in range(NQ)], axis=0).astype(BF)
        outer = jnp.dot(query_ref[:, cols], state, preferred_element_type=F32)
        mixed = intra_ref[:, cols] + outer * carried_ref[:, h : h + 1]
        mixed_ref[:, cols] = mixed
        acc = acc + mixed * mixed
    flat = jnp.sum(acc.T, axis=0, keepdims=True)
    sums_ref[...] = jnp.concatenate(
        [flat[:, :HDIM], flat[:, HDIM:], jnp.zeros((6, HDIM), F32)], axis=0
    )


def decode_kernel(here, local_ref, scarried_ref, sums_ref, *refs):
    near, far = refs[:NX], refs[NX]
    dec_ref, send_ref, carry_ref = refs[NX + 1 :]
    for k, dx in enumerate(ORDER):
        carry_ref[mate_head(here, dx, 0)] = near[k][0]
        carry_ref[mate_head(here, dx, 1)] = far[k]
    acc = jnp.zeros((NROW, HDIM), F32)
    for h in range(HEADS):
        cols = slice(h * HDIM, (h + 1) * HDIM)
        dec = local_ref[:, cols] + carry_ref[h] * scarried_ref[:, h : h + 1]
        dec_ref[:, cols] = dec
        acc = acc + dec * dec
    full = jnp.concatenate([acc, jnp.zeros((HDIM - NROW, HDIM), F32)], axis=0)
    dflat = jnp.sum(full.T, axis=0, keepdims=True)
    both = jnp.concatenate([sums_ref[0:2, :], dflat, dflat], axis=0)
    for k in range(HEADS):
        send_ref[k] = both


def final_kernel(sums_ref, mixed_ref, dec_ref, gain_ref, attn_ref, out_ref):
    total = sums_ref[0]
    for k in range(1, HEADS):
        total = total + sums_ref[k]
    scale = lax.rsqrt(total / (HEAD_COUNT * HDIM) + EPSILON)
    gain = gain_ref[...]

    def column(row):
        return jnp.broadcast_to(scale[row : row + 1, :], (HDIM, HDIM)).T

    for half in range(2):
        part = slice(half * HDIM, (half + 1) * HDIM)
        col = column(half)
        for h in range(HEADS):
            cols = slice(h * HDIM, (h + 1) * HDIM)
            attn_ref[part, cols] = (mixed_ref[part, cols] * col * gain[:, cols]).astype(BF)
    col = column(2)
    for h in range(HEADS):
        cols = slice(h * HDIM, (h + 1) * HDIM)
        res = (dec_ref[:, cols] * col[: STEPS * ROWS_DEV, :] * gain[:, cols]).astype(BF)
        for step in range(STEPS):
            out_ref[step, :, cols] = res[step * ROWS_DEV : (step + 1) * ROWS_DEV, :]


def shape(*dims, dtype=F32):
    return jax.ShapeDtypeStruct(dims, dtype)


def shift(x, axis, size, d):
    return lax.ppermute(x, axis, [(i, (i + d) % size) for i in range(size)])


def over_pair(pieces):
    both = jnp.stack([piece[1] for piece in pieces])
    return lax.ppermute(both, "seq_1", [(i, i ^ 1) for i in range(NZ)])


def spread(pieces, axis, size, step):
    return [shift(x, axis, size, step * d) if d else x for x, d in zip(pieces, ORDER)]


def exchange(x, axis):
    return lax.all_to_all(x, axis, split_axis=0, concat_axis=0, tiled=True)


def more_tails(key_in, value_in, log_decay, prompt_lengths, first):
    ends = jnp.cumsum(prompt_lengths)
    positions = first + jnp.arange(BLOCK, dtype=jnp.int32)
    segs = jnp.sum((positions[:, None] >= ends[None, :]).astype(jnp.int32), axis=1)
    cum = jnp.cumsum(log_decay, axis=0)
    keys = key_in.reshape(BLOCK, HEADS, HDIM)
    values = value_in.reshape(BLOCK, HEADS, HDIM)
    parts = []
    for p in (1, 2):
        local = ends[p] - 1 - first
        owned = (local >= 0) & (local < BLOCK) & (ends[p - 1] - 1 >= first)
        safe = jnp.clip(local, 0, BLOCK - 1)
        taken = (jnp.arange(BLOCK) <= safe) & (segs == p) & owned
        spread = jnp.where(taken[:, None], cum[safe][None, :] - cum, 0.0)
        keep = jnp.where(taken[:, None], jnp.exp(spread), 0.0)
        tailed = (keys.astype(F32) * keep[:, :, None]).astype(BF)
        part = jnp.einsum("shd,she->hde", tailed, values, preferred_element_type=F32)
        part = part.reshape(NX, 2, NQ, QUART, HDIM).transpose(0, 2, 1, 3, 4)
        parts.append(part.reshape(NDEV, QUART, HDIM))
    got = exchange(jnp.concatenate(parts, axis=1), SEQ)
    both = jnp.sum(got, axis=0)
    return jnp.stack([jnp.zeros((QUART, HDIM), F32), both[:QUART], both[QUART:]])


def local(
    query_in,
    key_in,
    value_in,
    log_decay,
    norm_gain,
    prompt_lengths,
    step_query,
    step_key,
    step_value,
    step_decay,
    row_prompt,
):
    me = lax.axis_index(SEQ).astype(jnp.int32)
    here = me[None]
    width = HEADS * HDIM
    n = STEPS * ROWS_DEV

    logd = log_decay.T
    give, crowded = pl.pallas_call(
        send_kernel,
        out_shape=(shape(NDEV, GIVE, HDIM), shape(1, dtype=jnp.int32)),
        in_specs=[SMEM] * 2 + [VMEM] * 3,
        out_specs=(VMEM, SMEM),
        compiler_params=params(),
        cost_estimate=cost(3),
        name="send",
    )(prompt_lengths, here, key_in, value_in, logd)
    given = exchange(give, SEQ)

    queries = pl.pallas_call(
        query_kernel,
        out_shape=(shape(2, ASK, HDIM),) * NX,
        in_specs=[SMEM] * 2 + [VMEM],
        out_specs=(VMEM,) * NX,
        compiler_params=params(),
        cost_estimate=cost(1),
        name="query",
    )(here, row_prompt, step_query)
    queries = spread(queries, "seq_0", NX, 1)
    far_queries = over_pair(queries)

    intra, carried = pl.pallas_call(
        intra_kernel,
        out_shape=(shape(BLOCK, width), shape(BLOCK, HEADS)),
        in_specs=[SMEM] * 2 + [VMEM] * 4,
        out_specs=(VMEM,) * 2,
        compiler_params=params(),
        cost_estimate=cost(3),
        name="intra",
    )(prompt_lengths, here, query_in, key_in, value_in, logd)

    given, intra, carried, crowded, queries, far_queries = lax.optimization_barrier(
        (given, intra, carried, crowded, queries, far_queries)
    )
    extra = lax.cond(
        crowded[0] > 0,
        lambda: more_tails(key_in, value_in, log_decay, prompt_lengths, me * BLOCK),
        lambda: jnp.zeros((LAST, QUART, HDIM), F32),
    )
    own = pl.pallas_call(
        slice_kernel,
        out_shape=shape(PROMPTS, QUART, HDIM),
        in_specs=[SMEM] + [VMEM] * 2,
        out_specs=VMEM,
        scratch_shapes=[pltpu.VMEM((NDEV, QUART, HDIM), F32)],
        compiler_params=params(),
        cost_estimate=cost(1),
        name="slice",
    )(prompt_lengths, given, extra)
    given, own = lax.optimization_barrier((given, own))
    entry = pl.pallas_call(
        entry_kernel,
        out_shape=shape(NDEV, QUART, HDIM),
        in_specs=[VMEM],
        out_specs=VMEM,
        compiler_params=params(),
        cost_estimate=cost(2),
        name="entry",
    )(given)
    slabs = spread([own] * NQ, "seq_1", NZ, 2)
    entry, slabs, step_key = lax.optimization_barrier((entry, slabs, step_key))
    back = exchange(entry, SEQ)

    local_dec, scarried = pl.pallas_call(
        local_kernel,
        out_shape=(shape(n, width), shape(n, HEADS)),
        in_specs=[VMEM] * 4,
        out_specs=(VMEM,) * 2,
        compiler_params=params(),
        cost_estimate=cost(1),
        name="local",
    )(step_query, step_key, step_value, step_decay.transpose(0, 2, 1))

    products = pl.pallas_call(
        project_kernel,
        out_shape=(shape(2, NROW, HDIM),) * NX,
        in_specs=[SMEM] + [VMEM] * (NX + 1 + NQ),
        out_specs=(VMEM,) * NX,
        scratch_shapes=[pltpu.VMEM((PROMPTS * HDIM, HDIM), F32)],
        compiler_params=params(),
        cost_estimate=cost(2),
        name="project",
    )(here, *queries, far_queries, *slabs)
    products = spread(products, "seq_0", NX, -1)
    far_products = over_pair(products)

    mixed, sums = pl.pallas_call(
        mixed_kernel,
        out_shape=(shape(BLOCK, width), shape(8, HDIM)),
        in_specs=[VMEM] * 4,
        out_specs=(VMEM,) * 2,
        compiler_params=params(),
        cost_estimate=cost(1),
        name="mixed",
    )(query_in, back, intra, carried)
    dec, sums_send = pl.pallas_call(
        decode_kernel,
        out_shape=(shape(n, width), shape(HEADS, 4, HDIM)),
        in_specs=[SMEM] + [VMEM] * (4 + NX),
        out_specs=(VMEM,) * 2,
        scratch_shapes=[pltpu.VMEM((HEADS, NROW, HDIM), F32)],
        compiler_params=params(),
        cost_estimate=cost(1),
        name="decode",
    )(here, local_dec, scarried, sums, *products, far_products)
    sums_all = exchange(sums_send, "head")

    return pl.pallas_call(
        final_kernel,
        out_shape=(shape(BLOCK, width, dtype=BF), shape(STEPS, ROWS_DEV, width, dtype=BF)),
        in_specs=[VMEM] * 4,
        out_specs=(VMEM,) * 2,
        compiler_params=params(),
        cost_estimate=cost(2),
        name="final",
    )(sums_all, mixed, dec, norm_gain.reshape(1, width))


def solution(mesh):
    split = Mesh(mesh.devices.reshape(NX, NZ, mesh.shape["head"]), ("seq_0", "seq_1", "head"))
    placed = (
        P(SEQ, "head"),
        P(SEQ, "head"),
        P(SEQ, "head"),
        P(SEQ, "head"),
        P("head"),
        P(),
        P(None, SEQ, "head"),
        P(None, SEQ, "head"),
        P(None, SEQ, "head"),
        P(None, SEQ, "head"),
        P(SEQ),
    )
    return jax.shard_map(
        local,
        mesh=split,
        in_specs=placed,
        out_specs=(P(SEQ, "head"), P(None, SEQ, "head")),
        check_vma=False,
    )
```

```python
import functools

import jax
import jax.numpy as jnp
from jax import lax
from jax.experimental import pallas as pl
from jax.experimental.pallas import tpu as pltpu
from jax.sharding import Mesh
from jax.sharding import PartitionSpec as P

HEAD_COUNT = 64
HDIM = 128
BLOCK = 256
PROMPTS = 4
STEPS = 4
SEQ = ("seq_0", "seq_1")
EPSILON = 1e-06

NX = 4
NZ = 8
HEADS = 8
NDEV = NX * NZ
NQ = NZ // 2
QUART = HDIM // NQ
ROWS_DEV = 16
NROW = STEPS * ROWS_DEV
LAST = PROMPTS - 1
ASK = NROW + 8

T0 = QUART
S0 = 2 * QUART
GIVE = S0 + 8

BF = jnp.bfloat16
F32 = jnp.float32
HI = lax.Precision.HIGHEST

SMEM = pl.BlockSpec(memory_space=pltpu.SMEM)
VMEM = pl.BlockSpec(memory_space=pltpu.VMEM)


def params(mib=12):
    return pltpu.CompilerParams(vmem_limit_bytes=mib << 20)


def cost(us):
    return pl.CostEstimate(flops=int(us * 1e9), bytes_accessed=int(us * 3e6), transcendentals=0)


def bounds(lens):
    ends = []
    total = lens[0]
    for p in range(PROMPTS):
        if p:
            total = total + lens[p]
        ends.append(total)
    return ends


def seg_of(pos, ends):
    out = (pos >= ends[0]).astype(jnp.int32)
    for p in range(1, PROMPTS):
        out = out + (pos >= ends[p]).astype(jnp.int32)
    return out


def entry_seg(first, ends):
    return jnp.where(first > 0, seg_of(first - 1, ends), -1)


def cum_columns(logd):
    t = lax.broadcasted_iota(jnp.int32, (BLOCK, BLOCK), 0)
    s = lax.broadcasted_iota(jnp.int32, (BLOCK, BLOCK), 1)
    return lax.dot_general(
        (s <= t).astype(F32), logd, (((1,), (1,)), ((), ())), precision=HI, preferred_element_type=F32
    )


def contract_rows(a, b):
    return lax.dot_general(a, b, (((0,), (0,)), ((), ())), preferred_element_type=F32)


def contract_cols(a, b):
    return lax.dot_general(a, b, (((1,), (1,)), ((), ())), preferred_element_type=F32)


def owner(head, quarter):
    return (head // 2) * NZ + 2 * quarter + head % 2


def cum_rows_of(logd):
    s = lax.broadcasted_iota(jnp.int32, (BLOCK, BLOCK), 0)
    t = lax.broadcasted_iota(jnp.int32, (BLOCK, BLOCK), 1)
    tri = (s <= t).astype(BF)
    total = jnp.zeros((HEADS, BLOCK), F32)
    rest = logd
    for _ in range(3):
        term = rest.astype(BF)
        total = total + jnp.dot(term, tri, preferred_element_type=F32)
        rest = rest - term.astype(F32)
    return total


def send_kernel(lens, here, key_ref, value_ref, logd_ref, out_ref, flag_ref):
    first = here[0] * BLOCK
    ends = bounds(lens)
    front = entry_seg(first, ends)
    seg_last = seg_of(first + (BLOCK - 1), ends)
    cum = cum_rows_of(logd_ref[...])
    tok = lax.broadcasted_iota(jnp.int32, (HEADS, BLOCK), 1)
    seg = seg_of(tok + first, ends)

    def at_token(spot):
        return jnp.sum(jnp.where(tok == spot, cum, 0.0), axis=1, keepdims=True)

    last = cum[:, BLOCK - 1 : BLOCK]
    keep = jnp.where(seg == seg_last, jnp.exp(last - cum), 0.0)
    factors = [jnp.exp(last) * (seg_last == front).astype(F32)]
    found = jnp.int32(-1)
    spot = jnp.int32(0)
    crowded = jnp.int32(0)
    for p in range(LAST):
        at = ends[p] - 1 - first
        inside = (at >= 0) & (at < BLOCK)
        factors.append(jnp.exp(at_token(at)) * (inside & (front == p)).astype(F32))
        take = (at >= 0) & (at < BLOCK - 1) & (found < 0)
        found = jnp.where(take, p, found)
        spot = jnp.where(take, at, spot)
        if p:
            same = (ends[p] - 1) // BLOCK == (ends[p - 1] - 1) // BLOCK
            crowded = crowded | (same & (ends[p] % BLOCK != 0)).astype(jnp.int32)
    flag_ref[0] = crowded
    taken = (tok <= spot) & (seg == found)
    tail = jnp.where(taken, jnp.exp(jnp.where(taken, at_token(spot) - cum, 0.0)), 0.0)

    for h in range(HEADS):
        cols = slice(h * HDIM, (h + 1) * HDIM)
        keys = key_ref[:, cols].T.astype(F32)
        scaled = jnp.concatenate(
            [(keys * keep[h : h + 1, :]).astype(BF), (keys * tail[h : h + 1, :]).astype(BF)], axis=0
        )
        total = jnp.dot(scaled, value_ref[:, cols], preferred_element_type=F32)
        scal = jnp.concatenate(
            [jnp.broadcast_to(f[h : h + 1, :], (1, HDIM)) for f in factors]
            + [jnp.zeros((8 - len(factors), HDIM), F32)],
            axis=0,
        )
        for g in range(NQ):
            rows = slice(g * QUART, (g + 1) * QUART)
            out_ref[owner(h, g), 0:T0, :] = total[rows, :]
            out_ref[owner(h, g), T0:S0, :] = total[HDIM + g * QUART : HDIM + (g + 1) * QUART, :]
            out_ref[owner(h, g), S0:GIVE, :] = scal


def mate_head(here, dx, db):
    x = here[0] // NZ
    parity = lax.rem(here[0], 2)
    return 2 * lax.rem(x + dx, NX) + (1 - parity if db else parity)


def query_kernel(here, rows, query_ref, *out_refs):
    lane = lax.broadcasted_iota(jnp.int32, (8, HDIM), 1)
    ids = jnp.zeros((8, HDIM), F32)
    for k in range(ROWS_DEV):
        ids = jnp.where(lane == k, rows[k].astype(F32), ids)
    for dx, out_ref in enumerate(out_refs):
        for db in range(2):
            cols = pl.ds(pl.multiple_of(mate_head(here, dx, db) * HDIM, HDIM), HDIM)
            out_ref[db, :NROW, :] = query_ref[:, :, cols].astype(F32).reshape(NROW, HDIM)
            out_ref[db, NROW:, :] = ids


def intra_kernel(
    lens, here, query_ref, key_ref, value_ref, logd_ref, intra_ref, carried_ref
):
    first = here[0] * BLOCK
    ends = bounds(lens)
    front = entry_seg(first, ends)
    logd = logd_ref[...]
    t = lax.broadcasted_iota(jnp.int32, (BLOCK, BLOCK), 0)
    s = lax.broadcasted_iota(jnp.int32, (BLOCK, BLOCK), 1)
    cum = cum_columns(logd)
    cum_rows = jnp.dot(logd, (t <= s).astype(F32), precision=HI, preferred_element_type=F32)
    linked = (s <= t) & (seg_of(t + first, ends) == seg_of(s + first, ends))
    tok = lax.broadcasted_iota(jnp.int32, (BLOCK, HEADS), 0)
    carried_ref[...] = jnp.where(seg_of(tok + first, ends) == front, jnp.exp(cum), 0.0)
    for h in range(HEADS):
        cols = slice(h * HDIM, (h + 1) * HDIM)
        scores = contract_cols(query_ref[:, cols], key_ref[:, cols])
        spread = cum[:, h : h + 1] - cum_rows[h : h + 1, :]
        factor = jnp.exp(jnp.where(linked, spread, -1e30))
        weights = (scores * factor).astype(BF)
        intra_ref[:, cols] = jnp.dot(weights, value_ref[:, cols], preferred_element_type=F32)


def local_kernel(sq_ref, sk_ref, sv_ref, sd_ref, local_ref, scarried_ref):
    n = NROW
    a = lax.broadcasted_iota(jnp.int32, (n, n), 0)
    b = lax.broadcasted_iota(jnp.int32, (n, n), 1)
    same = (b <= a) & ((a - b) % ROWS_DEV == 0)
    total = sd_ref[0]
    pieces = [total]
    for step in range(1, STEPS):
        total = total + sd_ref[step]
        pieces.append(total)
    scum_rows = jnp.concatenate(pieces, axis=1)
    scum = lax.dot_general(
        (a == b).astype(F32), scum_rows, (((1,), (1,)), ((), ())), precision=HI,
        preferred_element_type=F32,
    )
    scarried_ref[...] = jnp.exp(scum)
    for h in range(HEADS):
        cols = slice(h * HDIM, (h + 1) * HDIM)
        q = sq_ref[:, :, cols].reshape(n, HDIM)
        k = sk_ref[:, :, cols].reshape(n, HDIM)
        v = sv_ref[:, :, cols].reshape(n, HDIM)
        spread = scum[:, h : h + 1] - scum_rows[h : h + 1, :]
        weights = contract_cols(q, k) * jnp.exp(jnp.where(same, spread, -1e30))
        high = weights.astype(BF)
        low = (weights - high.astype(F32)).astype(BF)
        local_ref[:, cols] = jnp.dot(high, v, preferred_element_type=F32) + jnp.dot(
            low, v, preferred_element_type=F32
        )


def slice_kernel(lens, give_ref, extra_ref, slice_ref, entry_ref):
    ends = bounds(lens)
    state = jnp.zeros((QUART, HDIM), F32)
    for k in range(NDEV):
        entry_ref[k] = state
        state = give_ref[k, S0 : S0 + 1, :] * state + give_ref[k, 0:T0, :]
    slice_ref[LAST] = state
    earlier = []
    for p in range(LAST):
        e = ends[p] - 1
        b = e // BLOCK
        slot = jnp.int32(0)
        for other in earlier:
            slot = slot + (other == b).astype(jnp.int32)
        earlier.append(b)
        whole = e % BLOCK == BLOCK - 1
        lead = give_ref[b, S0 + 1 + p : S0 + 2 + p, :]
        tail = jnp.where(slot == 0, give_ref[b, T0:S0, :], extra_ref[p])
        tail = jnp.where(whole, give_ref[b, 0:T0, :], tail)
        slice_ref[p] = lead * entry_ref[b] + tail


def entry_kernel(give_ref, entry_ref):
    state = jnp.zeros((QUART, HDIM), F32)
    for k in range(NDEV):
        entry_ref[k] = state
        state = give_ref[k, S0 : S0 + 1, :] * state + give_ref[k, 0:T0, :]


def project_kernel(here, *refs):
    near, far, slabs, outs, st_ref = refs[:NX], refs[NX], refs[NX + 1 : NX + 1 + NQ], refs[NX + 1 + NQ : -1], refs[-1]
    quarter = lax.rem(here[0], NZ) // 2
    for d, ref in enumerate(slabs):
        origin = lax.rem(quarter - d + NQ, NQ)
        for p in range(PROMPTS):
            at = pl.multiple_of(p * HDIM + origin * QUART, QUART)
            st_ref[pl.ds(at, QUART), :] = ref[p]
    st = st_ref[...]
    high = st.astype(BF)
    low = (st - high.astype(F32)).astype(BF)
    r = lax.broadcasted_iota(jnp.int32, (NROW, HDIM), 0) % ROWS_DEV
    c = lax.broadcasted_iota(jnp.int32, (NROW, HDIM), 1)
    rows = []
    for msg in [ref[0] for ref in near] + [far[dx] for dx in range(NX)]:
        q = msg[:NROW, :]
        ids = jnp.broadcast_to(msg[NROW : NROW + 1, :], (NROW, HDIM))
        prompt = jnp.sum(jnp.where(r == c, ids, 0.0), axis=1, keepdims=True)
        rows.append(
            jnp.concatenate(
                [jnp.where(prompt == float(p), q, 0.0).astype(BF) for p in range(PROMPTS)], axis=1
            )
        )
    wide = jnp.concatenate(rows, axis=0)
    res = jnp.dot(wide, high, preferred_element_type=F32) + jnp.dot(
        wide, low, preferred_element_type=F32
    )
    for dx, ref in enumerate(outs):
        for db in range(2):
            at = (db * NX + dx) * NROW
            ref[db] = res[at : at + NROW, :]


def mixed_kernel(query_ref, back_ref, intra_ref, carried_ref, mixed_ref, sums_ref):
    acc = jnp.zeros((BLOCK, HDIM), F32)
    for h in range(HEADS):
        cols = slice(h * HDIM, (h + 1) * HDIM)
        state = jnp.concatenate([back_ref[owner(h, g)] for g in range(NQ)], axis=0).astype(BF)
        outer = jnp.dot(query_ref[:, cols], state, preferred_element_type=F32)
        mixed = intra_ref[:, cols] + outer * carried_ref[:, h : h + 1]
        mixed_ref[:, cols] = mixed
        acc = acc + mixed * mixed
    flat = jnp.sum(acc.T, axis=0, keepdims=True)
    sums_ref[...] = jnp.concatenate(
        [flat[:, :HDIM], flat[:, HDIM:], jnp.zeros((6, HDIM), F32)], axis=0
    )


def decode_kernel(here, local_ref, scarried_ref, sums_ref, *refs):
    near, far = refs[:NX], refs[NX]
    dec_ref, send_ref, carry_ref = refs[NX + 1 :]
    for dx in range(NX):
        carry_ref[mate_head(here, dx, 0)] = near[dx][0]
        carry_ref[mate_head(here, dx, 1)] = far[dx]
    acc = jnp.zeros((NROW, HDIM), F32)
    for h in range(HEADS):
        cols = slice(h * HDIM, (h + 1) * HDIM)
        dec = local_ref[:, cols] + carry_ref[h] * scarried_ref[:, h : h + 1]
        dec_ref[:, cols] = dec
        acc = acc + dec * dec
    full = jnp.concatenate([acc, jnp.zeros((HDIM - NROW, HDIM), F32)], axis=0)
    dflat = jnp.sum(full.T, axis=0, keepdims=True)
    both = jnp.concatenate([sums_ref[0:2, :], dflat, dflat], axis=0)
    for k in range(HEADS):
        send_ref[k] = both


def final_kernel(sums_ref, mixed_ref, dec_ref, gain_ref, attn_ref, out_ref):
    total = sums_ref[0]
    for k in range(1, HEADS):
        total = total + sums_ref[k]
    scale = lax.rsqrt(total / (HEAD_COUNT * HDIM) + EPSILON)
    gain = gain_ref[...]

    def column(row):
        return jnp.broadcast_to(scale[row : row + 1, :], (HDIM, HDIM)).T

    for half in range(2):
        part = slice(half * HDIM, (half + 1) * HDIM)
        col = column(half)
        for h in range(HEADS):
            cols = slice(h * HDIM, (h + 1) * HDIM)
            attn_ref[part, cols] = (mixed_ref[part, cols] * col * gain[:, cols]).astype(BF)
    col = column(2)
    for h in range(HEADS):
        cols = slice(h * HDIM, (h + 1) * HDIM)
        res = (dec_ref[:, cols] * col[: STEPS * ROWS_DEV, :] * gain[:, cols]).astype(BF)
        for step in range(STEPS):
            out_ref[step, :, cols] = res[step * ROWS_DEV : (step + 1) * ROWS_DEV, :]


def shape(*dims, dtype=F32):
    return jax.ShapeDtypeStruct(dims, dtype)


def shift(x, axis, size, d):
    return lax.ppermute(x, axis, [(i, (i + d) % size) for i in range(size)])


def over_pair(pieces):
    both = jnp.stack([piece[1] for piece in pieces])
    return lax.ppermute(both, "seq_1", [(i, i ^ 1) for i in range(NZ)])


def exchange(x, axis):
    return lax.all_to_all(x, axis, split_axis=0, concat_axis=0, tiled=True)


def more_tails(key_in, value_in, log_decay, prompt_lengths, first):
    ends = jnp.cumsum(prompt_lengths)
    positions = first + jnp.arange(BLOCK, dtype=jnp.int32)
    segs = jnp.sum((positions[:, None] >= ends[None, :]).astype(jnp.int32), axis=1)
    cum = jnp.cumsum(log_decay, axis=0)
    keys = key_in.reshape(BLOCK, HEADS, HDIM)
    values = value_in.reshape(BLOCK, HEADS, HDIM)
    parts = []
    for p in (1, 2):
        local = ends[p] - 1 - first
        owned = (local >= 0) & (local < BLOCK) & (ends[p - 1] - 1 >= first)
        safe = jnp.clip(local, 0, BLOCK - 1)
        taken = (jnp.arange(BLOCK) <= safe) & (segs == p) & owned
        spread = jnp.where(taken[:, None], cum[safe][None, :] - cum, 0.0)
        keep = jnp.where(taken[:, None], jnp.exp(spread), 0.0)
        tailed = (keys.astype(F32) * keep[:, :, None]).astype(BF)
        part = jnp.einsum("shd,she->hde", tailed, values, preferred_element_type=F32)
        part = part.reshape(NX, 2, NQ, QUART, HDIM).transpose(0, 2, 1, 3, 4)
        parts.append(part.reshape(NDEV, QUART, HDIM))
    got = exchange(jnp.concatenate(parts, axis=1), SEQ)
    both = jnp.sum(got, axis=0)
    return jnp.stack([jnp.zeros((QUART, HDIM), F32), both[:QUART], both[QUART:]])


def local(
    query_in,
    key_in,
    value_in,
    log_decay,
    norm_gain,
    prompt_lengths,
    step_query,
    step_key,
    step_value,
    step_decay,
    row_prompt,
):
    me = lax.axis_index(SEQ).astype(jnp.int32)
    here = me[None]
    width = HEADS * HDIM
    n = STEPS * ROWS_DEV

    logd = log_decay.T
    give, crowded = pl.pallas_call(
        send_kernel,
        out_shape=(shape(NDEV, GIVE, HDIM), shape(1, dtype=jnp.int32)),
        in_specs=[SMEM] * 2 + [VMEM] * 3,
        out_specs=(VMEM, SMEM),
        compiler_params=params(),
        cost_estimate=cost(3),
        name="send",
    )(prompt_lengths, here, key_in, value_in, logd)
    given = exchange(give, SEQ)

    queries = pl.pallas_call(
        query_kernel,
        out_shape=(shape(2, ASK, HDIM),) * NX,
        in_specs=[SMEM] * 2 + [VMEM],
        out_specs=(VMEM,) * NX,
        compiler_params=params(),
        cost_estimate=cost(1),
        name="query",
    )(here, row_prompt, step_query)
    queries = [queries[0]] + [shift(queries[d], "seq_0", NX, d) for d in range(1, NX)]
    far_queries = over_pair(queries)

    intra, carried = pl.pallas_call(
        intra_kernel,
        out_shape=(shape(BLOCK, width), shape(BLOCK, HEADS)),
        in_specs=[SMEM] * 2 + [VMEM] * 4,
        out_specs=(VMEM,) * 2,
        compiler_params=params(),
        cost_estimate=cost(3),
        name="intra",
    )(prompt_lengths, here, query_in, key_in, value_in, logd)

    given, intra, carried, crowded, queries = lax.optimization_barrier(
        (given, intra, carried, crowded, queries)
    )
    extra = lax.cond(
        crowded[0] > 0,
        lambda: more_tails(key_in, value_in, log_decay, prompt_lengths, me * BLOCK),
        lambda: jnp.zeros((LAST, QUART, HDIM), F32),
    )
    own = pl.pallas_call(
        slice_kernel,
        out_shape=shape(PROMPTS, QUART, HDIM),
        in_specs=[SMEM] + [VMEM] * 2,
        out_specs=VMEM,
        scratch_shapes=[pltpu.VMEM((NDEV, QUART, HDIM), F32)],
        compiler_params=params(),
        cost_estimate=cost(1),
        name="slice",
    )(prompt_lengths, given, extra)
    given, own = lax.optimization_barrier((given, own))
    entry = pl.pallas_call(
        entry_kernel,
        out_shape=shape(NDEV, QUART, HDIM),
        in_specs=[VMEM],
        out_specs=VMEM,
        compiler_params=params(),
        cost_estimate=cost(2),
        name="entry",
    )(given)
    slabs = [own] + [shift(own, "seq_1", NZ, 2 * d) for d in range(1, NQ)]
    entry, slabs, step_key, far_queries = lax.optimization_barrier(
        (entry, slabs, step_key, far_queries)
    )
    back = exchange(entry, SEQ)

    local_dec, scarried = pl.pallas_call(
        local_kernel,
        out_shape=(shape(n, width), shape(n, HEADS)),
        in_specs=[VMEM] * 4,
        out_specs=(VMEM,) * 2,
        compiler_params=params(),
        cost_estimate=cost(1),
        name="local",
    )(step_query, step_key, step_value, step_decay.transpose(0, 2, 1))

    products = pl.pallas_call(
        project_kernel,
        out_shape=(shape(2, NROW, HDIM),) * NX,
        in_specs=[SMEM] + [VMEM] * (NX + 1 + NQ),
        out_specs=(VMEM,) * NX,
        scratch_shapes=[pltpu.VMEM((PROMPTS * HDIM, HDIM), F32)],
        compiler_params=params(),
        cost_estimate=cost(2),
        name="project",
    )(here, *queries, far_queries, *slabs)
    products = [products[0]] + [shift(products[d], "seq_0", NX, -d) for d in range(1, NX)]
    far_products = over_pair(products)

    mixed, sums = pl.pallas_call(
        mixed_kernel,
        out_shape=(shape(BLOCK, width), shape(8, HDIM)),
        in_specs=[VMEM] * 4,
        out_specs=(VMEM,) * 2,
        compiler_params=params(),
        cost_estimate=cost(1),
        name="mixed",
    )(query_in, back, intra, carried)
    dec, sums_send = pl.pallas_call(
        decode_kernel,
        out_shape=(shape(n, width), shape(HEADS, 4, HDIM)),
        in_specs=[SMEM] + [VMEM] * (4 + NX),
        out_specs=(VMEM,) * 2,
        scratch_shapes=[pltpu.VMEM((HEADS, NROW, HDIM), F32)],
        compiler_params=params(),
        cost_estimate=cost(1),
        name="decode",
    )(here, local_dec, scarried, sums, *products, far_products)
    sums_all = exchange(sums_send, "head")

    return pl.pallas_call(
        final_kernel,
        out_shape=(shape(BLOCK, width, dtype=BF), shape(STEPS, ROWS_DEV, width, dtype=BF)),
        in_specs=[VMEM] * 4,
        out_specs=(VMEM,) * 2,
        compiler_params=params(),
        cost_estimate=cost(2),
        name="final",
    )(sums_all, mixed, dec, norm_gain.reshape(1, width))


def solution(mesh):
    split = Mesh(mesh.devices.reshape(NX, NZ, mesh.shape["head"]), ("seq_0", "seq_1", "head"))
    placed = (
        P(SEQ, "head"),
        P(SEQ, "head"),
        P(SEQ, "head"),
        P(SEQ, "head"),
        P("head"),
        P(),
        P(None, SEQ, "head"),
        P(None, SEQ, "head"),
        P(None, SEQ, "head"),
        P(None, SEQ, "head"),
        P(SEQ),
    )
    return jax.shard_map(
        local,
        mesh=split,
        in_specs=placed,
        out_specs=(P(SEQ, "head"), P(None, SEQ, "head")),
        check_vma=False,
    )
```

```python
import functools

import jax
import jax.numpy as jnp
from jax import lax
from jax.experimental import pallas as pl
from jax.experimental.pallas import tpu as pltpu
from jax.sharding import Mesh
from jax.sharding import PartitionSpec as P

HEAD_COUNT = 64
HDIM = 128
BLOCK = 256
PROMPTS = 4
STEPS = 4
SEQ = ("seq_0", "seq_1")
EPSILON = 1e-06

NX = 4
NZ = 8
HEADS = 8
NDEV = NX * NZ
NQ = NZ // 2
QUART = HDIM // NQ
ROWS_DEV = 16
NROW = STEPS * ROWS_DEV
LAST = PROMPTS - 1
ASK = NROW + 8

T0 = QUART
S0 = 2 * QUART
GIVE = S0 + 8

BF = jnp.bfloat16
F32 = jnp.float32
HI = lax.Precision.HIGHEST

SMEM = pl.BlockSpec(memory_space=pltpu.SMEM)
VMEM = pl.BlockSpec(memory_space=pltpu.VMEM)


def params(mib=12):
    return pltpu.CompilerParams(vmem_limit_bytes=mib << 20)


def cost(us):
    return pl.CostEstimate(flops=int(us * 1e9), bytes_accessed=int(us * 3e6), transcendentals=0)


def bounds(lens):
    ends = []
    total = lens[0]
    for p in range(PROMPTS):
        if p:
            total = total + lens[p]
        ends.append(total)
    return ends


def seg_of(pos, ends):
    out = (pos >= ends[0]).astype(jnp.int32)
    for p in range(1, PROMPTS):
        out = out + (pos >= ends[p]).astype(jnp.int32)
    return out


def entry_seg(first, ends):
    return jnp.where(first > 0, seg_of(first - 1, ends), -1)


def cum_columns(logd):
    t = lax.broadcasted_iota(jnp.int32, (BLOCK, BLOCK), 0)
    s = lax.broadcasted_iota(jnp.int32, (BLOCK, BLOCK), 1)
    return lax.dot_general(
        (s <= t).astype(F32), logd, (((1,), (1,)), ((), ())), precision=HI, preferred_element_type=F32
    )


def contract_rows(a, b):
    return lax.dot_general(a, b, (((0,), (0,)), ((), ())), preferred_element_type=F32)


def contract_cols(a, b):
    return lax.dot_general(a, b, (((1,), (1,)), ((), ())), preferred_element_type=F32)


def owner(head, quarter):
    return (head // 2) * NZ + 2 * quarter + head % 2


def cum_rows_of(logd):
    s = lax.broadcasted_iota(jnp.int32, (BLOCK, BLOCK), 0)
    t = lax.broadcasted_iota(jnp.int32, (BLOCK, BLOCK), 1)
    tri = (s <= t).astype(BF)
    total = jnp.zeros((HEADS, BLOCK), F32)
    rest = logd
    for _ in range(3):
        term = rest.astype(BF)
        total = total + jnp.dot(term, tri, preferred_element_type=F32)
        rest = rest - term.astype(F32)
    return total


def send_kernel(lens, here, key_ref, value_ref, logd_ref, out_ref, flag_ref):
    first = here[0] * BLOCK
    ends = bounds(lens)
    front = entry_seg(first, ends)
    seg_last = seg_of(first + (BLOCK - 1), ends)
    cum = cum_rows_of(logd_ref[...])
    tok = lax.broadcasted_iota(jnp.int32, (HEADS, BLOCK), 1)
    seg = seg_of(tok + first, ends)

    def at_token(spot):
        return jnp.sum(jnp.where(tok == spot, cum, 0.0), axis=1, keepdims=True)

    last = cum[:, BLOCK - 1 : BLOCK]
    keep = jnp.where(seg == seg_last, jnp.exp(last - cum), 0.0)
    factors = [jnp.exp(last) * (seg_last == front).astype(F32)]
    found = jnp.int32(-1)
    spot = jnp.int32(0)
    crowded = jnp.int32(0)
    for p in range(LAST):
        at = ends[p] - 1 - first
        inside = (at >= 0) & (at < BLOCK)
        factors.append(jnp.exp(at_token(at)) * (inside & (front == p)).astype(F32))
        take = (at >= 0) & (at < BLOCK - 1) & (found < 0)
        found = jnp.where(take, p, found)
        spot = jnp.where(take, at, spot)
        if p:
            same = (ends[p] - 1) // BLOCK == (ends[p - 1] - 1) // BLOCK
            crowded = crowded | (same & (ends[p] % BLOCK != 0)).astype(jnp.int32)
    flag_ref[0] = crowded
    taken = (tok <= spot) & (seg == found)
    tail = jnp.where(taken, jnp.exp(jnp.where(taken, at_token(spot) - cum, 0.0)), 0.0)

    for h in range(HEADS):
        cols = slice(h * HDIM, (h + 1) * HDIM)
        keys = key_ref[:, cols].T.astype(F32)
        scaled = jnp.concatenate(
            [(keys * keep[h : h + 1, :]).astype(BF), (keys * tail[h : h + 1, :]).astype(BF)], axis=0
        )
        total = jnp.dot(scaled, value_ref[:, cols], preferred_element_type=F32)
        scal = jnp.concatenate(
            [jnp.broadcast_to(f[h : h + 1, :], (1, HDIM)) for f in factors]
            + [jnp.zeros((8 - len(factors), HDIM), F32)],
            axis=0,
        )
        for g in range(NQ):
            rows = slice(g * QUART, (g + 1) * QUART)
            out_ref[owner(h, g), 0:T0, :] = total[rows, :]
            out_ref[owner(h, g), T0:S0, :] = total[HDIM + g * QUART : HDIM + (g + 1) * QUART, :]
            out_ref[owner(h, g), S0:GIVE, :] = scal


def mate_head(here, dx, db):
    x = here[0] // NZ
    parity = lax.rem(here[0], 2)
    return 2 * lax.rem(x + dx, NX) + (1 - parity if db else parity)


def query_kernel(here, rows, query_ref, *out_refs):
    lane = lax.broadcasted_iota(jnp.int32, (8, HDIM), 1)
    ids = jnp.zeros((8, HDIM), F32)
    for k in range(ROWS_DEV):
        ids = jnp.where(lane == k, rows[k].astype(F32), ids)
    for dx, out_ref in enumerate(out_refs):
        for db in range(2):
            cols = pl.ds(pl.multiple_of(mate_head(here, dx, db) * HDIM, HDIM), HDIM)
            out_ref[db, :NROW, :] = query_ref[:, :, cols].astype(F32).reshape(NROW, HDIM)
            out_ref[db, NROW:, :] = ids


def intra_kernel(
    lens, here, query_ref, key_ref, value_ref, logd_ref, intra_ref, carried_ref
):
    first = here[0] * BLOCK
    ends = bounds(lens)
    front = entry_seg(first, ends)
    logd = logd_ref[...]
    t = lax.broadcasted_iota(jnp.int32, (BLOCK, BLOCK), 0)
    s = lax.broadcasted_iota(jnp.int32, (BLOCK, BLOCK), 1)
    cum = cum_columns(logd)
    cum_rows = jnp.dot(logd, (t <= s).astype(F32), precision=HI, preferred_element_type=F32)
    linked = (s <= t) & (seg_of(t + first, ends) == seg_of(s + first, ends))
    tok = lax.broadcasted_iota(jnp.int32, (BLOCK, HEADS), 0)
    carried_ref[...] = jnp.where(seg_of(tok + first, ends) == front, jnp.exp(cum), 0.0)
    for h in range(HEADS):
        cols = slice(h * HDIM, (h + 1) * HDIM)
        scores = contract_cols(query_ref[:, cols], key_ref[:, cols])
        spread = cum[:, h : h + 1] - cum_rows[h : h + 1, :]
        factor = jnp.exp(jnp.where(linked, spread, -1e30))
        weights = (scores * factor).astype(BF)
        intra_ref[:, cols] = jnp.dot(weights, value_ref[:, cols], preferred_element_type=F32)


def local_kernel(sq_ref, sk_ref, sv_ref, sd_ref, local_ref, scarried_ref):
    n = NROW
    a = lax.broadcasted_iota(jnp.int32, (n, n), 0)
    b = lax.broadcasted_iota(jnp.int32, (n, n), 1)
    same = (b <= a) & ((a - b) % ROWS_DEV == 0)
    total = sd_ref[0]
    pieces = [total]
    for step in range(1, STEPS):
        total = total + sd_ref[step]
        pieces.append(total)
    scum_rows = jnp.concatenate(pieces, axis=1)
    scum = lax.dot_general(
        (a == b).astype(F32), scum_rows, (((1,), (1,)), ((), ())), precision=HI,
        preferred_element_type=F32,
    )
    scarried_ref[...] = jnp.exp(scum)
    for h in range(HEADS):
        cols = slice(h * HDIM, (h + 1) * HDIM)
        q = sq_ref[:, :, cols].reshape(n, HDIM)
        k = sk_ref[:, :, cols].reshape(n, HDIM)
        v = sv_ref[:, :, cols].reshape(n, HDIM)
        spread = scum[:, h : h + 1] - scum_rows[h : h + 1, :]
        weights = contract_cols(q, k) * jnp.exp(jnp.where(same, spread, -1e30))
        high = weights.astype(BF)
        low = (weights - high.astype(F32)).astype(BF)
        local_ref[:, cols] = jnp.dot(high, v, preferred_element_type=F32) + jnp.dot(
            low, v, preferred_element_type=F32
        )


def slice_kernel(lens, give_ref, extra_ref, slice_ref, entry_ref):
    ends = bounds(lens)
    state = jnp.zeros((QUART, HDIM), F32)
    for k in range(NDEV):
        entry_ref[k] = state
        state = give_ref[k, S0 : S0 + 1, :] * state + give_ref[k, 0:T0, :]
    slice_ref[LAST] = state
    earlier = []
    for p in range(LAST):
        e = ends[p] - 1
        b = e // BLOCK
        slot = jnp.int32(0)
        for other in earlier:
            slot = slot + (other == b).astype(jnp.int32)
        earlier.append(b)
        whole = e % BLOCK == BLOCK - 1
        lead = give_ref[b, S0 + 1 + p : S0 + 2 + p, :]
        tail = jnp.where(slot == 0, give_ref[b, T0:S0, :], extra_ref[p])
        tail = jnp.where(whole, give_ref[b, 0:T0, :], tail)
        slice_ref[p] = lead * entry_ref[b] + tail


def entry_kernel(give_ref, entry_ref):
    state = jnp.zeros((QUART, HDIM), F32)
    for k in range(NDEV):
        entry_ref[k] = state
        state = give_ref[k, S0 : S0 + 1, :] * state + give_ref[k, 0:T0, :]


def stack_kernel(*refs):
    for k in range(NX):
        refs[NX][k] = refs[k][1]


def project_kernel(here, *refs):
    near, far, slabs, outs, st_ref = refs[:NX], refs[NX], refs[NX + 1 : NX + 1 + NQ], refs[NX + 1 + NQ : -1], refs[-1]
    quarter = lax.rem(here[0], NZ) // 2
    for d, ref in enumerate(slabs):
        origin = lax.rem(quarter - d + NQ, NQ)
        for p in range(PROMPTS):
            at = pl.multiple_of(p * HDIM + origin * QUART, QUART)
            st_ref[pl.ds(at, QUART), :] = ref[p]
    st = st_ref[...]
    high = st.astype(BF)
    low = (st - high.astype(F32)).astype(BF)
    r = lax.broadcasted_iota(jnp.int32, (NROW, HDIM), 0) % ROWS_DEV
    c = lax.broadcasted_iota(jnp.int32, (NROW, HDIM), 1)
    rows = []
    for msg in [ref[0] for ref in near] + [far[dx] for dx in range(NX)]:
        q = msg[:NROW, :]
        ids = jnp.broadcast_to(msg[NROW : NROW + 1, :], (NROW, HDIM))
        prompt = jnp.sum(jnp.where(r == c, ids, 0.0), axis=1, keepdims=True)
        rows.append(
            jnp.concatenate(
                [jnp.where(prompt == float(p), q, 0.0).astype(BF) for p in range(PROMPTS)], axis=1
            )
        )
    wide = jnp.concatenate(rows, axis=0)
    res = jnp.dot(wide, high, preferred_element_type=F32) + jnp.dot(
        wide, low, preferred_element_type=F32
    )
    for dx, ref in enumerate(outs):
        for db in range(2):
            at = (db * NX + dx) * NROW
            ref[db] = res[at : at + NROW, :]


def mixed_kernel(query_ref, back_ref, intra_ref, carried_ref, mixed_ref, sums_ref):
    acc = jnp.zeros((BLOCK, HDIM), F32)
    for h in range(HEADS):
        cols = slice(h * HDIM, (h + 1) * HDIM)
        state = jnp.concatenate([back_ref[owner(h, g)] for g in range(NQ)], axis=0).astype(BF)
        outer = jnp.dot(query_ref[:, cols], state, preferred_element_type=F32)
        mixed = intra_ref[:, cols] + outer * carried_ref[:, h : h + 1]
        mixed_ref[:, cols] = mixed
        acc = acc + mixed * mixed
    flat = jnp.sum(acc.T, axis=0, keepdims=True)
    sums_ref[...] = jnp.concatenate(
        [flat[:, :HDIM], flat[:, HDIM:], jnp.zeros((6, HDIM), F32)], axis=0
    )


def decode_kernel(here, local_ref, scarried_ref, sums_ref, *refs):
    near, far = refs[:NX], refs[NX]
    dec_ref, send_ref, carry_ref = refs[NX + 1 :]
    for dx in range(NX):
        carry_ref[mate_head(here, dx, 0)] = near[dx][0]
        carry_ref[mate_head(here, dx, 1)] = far[dx]
    acc = jnp.zeros((NROW, HDIM), F32)
    for h in range(HEADS):
        cols = slice(h * HDIM, (h + 1) * HDIM)
        dec = local_ref[:, cols] + carry_ref[h] * scarried_ref[:, h : h + 1]
        dec_ref[:, cols] = dec
        acc = acc + dec * dec
    full = jnp.concatenate([acc, jnp.zeros((HDIM - NROW, HDIM), F32)], axis=0)
    dflat = jnp.sum(full.T, axis=0, keepdims=True)
    both = jnp.concatenate([sums_ref[0:2, :], dflat, dflat], axis=0)
    for k in range(HEADS):
        send_ref[k] = both


def final_kernel(sums_ref, mixed_ref, dec_ref, gain_ref, attn_ref, out_ref):
    total = sums_ref[0]
    for k in range(1, HEADS):
        total = total + sums_ref[k]
    scale = lax.rsqrt(total / (HEAD_COUNT * HDIM) + EPSILON)
    gain = gain_ref[...]

    def column(row):
        return jnp.broadcast_to(scale[row : row + 1, :], (HDIM, HDIM)).T

    for half in range(2):
        part = slice(half * HDIM, (half + 1) * HDIM)
        col = column(half)
        for h in range(HEADS):
            cols = slice(h * HDIM, (h + 1) * HDIM)
            attn_ref[part, cols] = (mixed_ref[part, cols] * col * gain[:, cols]).astype(BF)
    col = column(2)
    for h in range(HEADS):
        cols = slice(h * HDIM, (h + 1) * HDIM)
        res = (dec_ref[:, cols] * col[: STEPS * ROWS_DEV, :] * gain[:, cols]).astype(BF)
        for step in range(STEPS):
            out_ref[step, :, cols] = res[step * ROWS_DEV : (step + 1) * ROWS_DEV, :]


def shape(*dims, dtype=F32):
    return jax.ShapeDtypeStruct(dims, dtype)


def shift(x, axis, size, d):
    return lax.ppermute(x, axis, [(i, (i + d) % size) for i in range(size)])


def over_pair(pieces):
    rows = pieces[0].shape[1]
    both = pl.pallas_call(
        stack_kernel,
        out_shape=shape(NX, rows, HDIM),
        in_specs=[VMEM] * NX,
        out_specs=VMEM,
        compiler_params=params(),
        cost_estimate=cost(1),
        name="stack",
    )(*pieces)
    return lax.ppermute(both, "seq_1", [(i, i ^ 1) for i in range(NZ)])


def exchange(x, axis):
    return lax.all_to_all(x, axis, split_axis=0, concat_axis=0, tiled=True)


def more_tails(key_in, value_in, log_decay, prompt_lengths, first):
    ends = jnp.cumsum(prompt_lengths)
    positions = first + jnp.arange(BLOCK, dtype=jnp.int32)
    segs = jnp.sum((positions[:, None] >= ends[None, :]).astype(jnp.int32), axis=1)
    cum = jnp.cumsum(log_decay, axis=0)
    keys = key_in.reshape(BLOCK, HEADS, HDIM)
    values = value_in.reshape(BLOCK, HEADS, HDIM)
    parts = []
    for p in (1, 2):
        local = ends[p] - 1 - first
        owned = (local >= 0) & (local < BLOCK) & (ends[p - 1] - 1 >= first)
        safe = jnp.clip(local, 0, BLOCK - 1)
        taken = (jnp.arange(BLOCK) <= safe) & (segs == p) & owned
        spread = jnp.where(taken[:, None], cum[safe][None, :] - cum, 0.0)
        keep = jnp.where(taken[:, None], jnp.exp(spread), 0.0)
        tailed = (keys.astype(F32) * keep[:, :, None]).astype(BF)
        part = jnp.einsum("shd,she->hde", tailed, values, preferred_element_type=F32)
        part = part.reshape(NX, 2, NQ, QUART, HDIM).transpose(0, 2, 1, 3, 4)
        parts.append(part.reshape(NDEV, QUART, HDIM))
    got = exchange(jnp.concatenate(parts, axis=1), SEQ)
    both = jnp.sum(got, axis=0)
    return jnp.stack([jnp.zeros((QUART, HDIM), F32), both[:QUART], both[QUART:]])


def local(
    query_in,
    key_in,
    value_in,
    log_decay,
    norm_gain,
    prompt_lengths,
    step_query,
    step_key,
    step_value,
    step_decay,
    row_prompt,
):
    me = lax.axis_index(SEQ).astype(jnp.int32)
    here = me[None]
    width = HEADS * HDIM
    n = STEPS * ROWS_DEV

    logd = log_decay.T
    give, crowded = pl.pallas_call(
        send_kernel,
        out_shape=(shape(NDEV, GIVE, HDIM), shape(1, dtype=jnp.int32)),
        in_specs=[SMEM] * 2 + [VMEM] * 3,
        out_specs=(VMEM, SMEM),
        compiler_params=params(),
        cost_estimate=cost(3),
        name="send",
    )(prompt_lengths, here, key_in, value_in, logd)
    given = exchange(give, SEQ)

    queries = pl.pallas_call(
        query_kernel,
        out_shape=(shape(2, ASK, HDIM),) * NX,
        in_specs=[SMEM] * 2 + [VMEM],
        out_specs=(VMEM,) * NX,
        compiler_params=params(),
        cost_estimate=cost(1),
        name="query",
    )(here, row_prompt, step_query)
    queries = [queries[0]] + [shift(queries[d], "seq_0", NX, d) for d in range(1, NX)]
    far_queries = over_pair(queries)

    intra, carried = pl.pallas_call(
        intra_kernel,
        out_shape=(shape(BLOCK, width), shape(BLOCK, HEADS)),
        in_specs=[SMEM] * 2 + [VMEM] * 4,
        out_specs=(VMEM,) * 2,
        compiler_params=params(),
        cost_estimate=cost(3),
        name="intra",
    )(prompt_lengths, here, query_in, key_in, value_in, logd)

    given, intra, carried, crowded, queries = lax.optimization_barrier(
        (given, intra, carried, crowded, queries)
    )
    extra = lax.cond(
        crowded[0] > 0,
        lambda: more_tails(key_in, value_in, log_decay, prompt_lengths, me * BLOCK),
        lambda: jnp.zeros((LAST, QUART, HDIM), F32),
    )
    own = pl.pallas_call(
        slice_kernel,
        out_shape=shape(PROMPTS, QUART, HDIM),
        in_specs=[SMEM] + [VMEM] * 2,
        out_specs=VMEM,
        scratch_shapes=[pltpu.VMEM((NDEV, QUART, HDIM), F32)],
        compiler_params=params(),
        cost_estimate=cost(1),
        name="slice",
    )(prompt_lengths, given, extra)
    given, own = lax.optimization_barrier((given, own))
    entry = pl.pallas_call(
        entry_kernel,
        out_shape=shape(NDEV, QUART, HDIM),
        in_specs=[VMEM],
        out_specs=VMEM,
        compiler_params=params(),
        cost_estimate=cost(2),
        name="entry",
    )(given)
    slabs = [own] + [shift(own, "seq_1", NZ, 2 * d) for d in range(1, NQ)]
    entry, slabs, step_key, far_queries = lax.optimization_barrier(
        (entry, slabs, step_key, far_queries)
    )
    back = exchange(entry, SEQ)

    local_dec, scarried = pl.pallas_call(
        local_kernel,
        out_shape=(shape(n, width), shape(n, HEADS)),
        in_specs=[VMEM] * 4,
        out_specs=(VMEM,) * 2,
        compiler_params=params(),
        cost_estimate=cost(1),
        name="local",
    )(step_query, step_key, step_value, step_decay.transpose(0, 2, 1))

    products = pl.pallas_call(
        project_kernel,
        out_shape=(shape(2, NROW, HDIM),) * NX,
        in_specs=[SMEM] + [VMEM] * (NX + 1 + NQ),
        out_specs=(VMEM,) * NX,
        scratch_shapes=[pltpu.VMEM((PROMPTS * HDIM, HDIM), F32)],
        compiler_params=params(),
        cost_estimate=cost(2),
        name="project",
    )(here, *queries, far_queries, *slabs)
    products = [products[0]] + [shift(products[d], "seq_0", NX, -d) for d in range(1, NX)]
    far_products = over_pair(products)

    mixed, sums = pl.pallas_call(
        mixed_kernel,
        out_shape=(shape(BLOCK, width), shape(8, HDIM)),
        in_specs=[VMEM] * 4,
        out_specs=(VMEM,) * 2,
        compiler_params=params(),
        cost_estimate=cost(1),
        name="mixed",
    )(query_in, back, intra, carried)
    dec, sums_send = pl.pallas_call(
        decode_kernel,
        out_shape=(shape(n, width), shape(HEADS, 4, HDIM)),
        in_specs=[SMEM] + [VMEM] * (4 + NX),
        out_specs=(VMEM,) * 2,
        scratch_shapes=[pltpu.VMEM((HEADS, NROW, HDIM), F32)],
        compiler_params=params(),
        cost_estimate=cost(1),
        name="decode",
    )(here, local_dec, scarried, sums, *products, far_products)
    sums_all = exchange(sums_send, "head")

    return pl.pallas_call(
        final_kernel,
        out_shape=(shape(BLOCK, width, dtype=BF), shape(STEPS, ROWS_DEV, width, dtype=BF)),
        in_specs=[VMEM] * 4,
        out_specs=(VMEM,) * 2,
        compiler_params=params(),
        cost_estimate=cost(2),
        name="final",
    )(sums_all, mixed, dec, norm_gain.reshape(1, width))


def solution(mesh):
    split = Mesh(mesh.devices.reshape(NX, NZ, mesh.shape["head"]), ("seq_0", "seq_1", "head"))
    placed = (
        P(SEQ, "head"),
        P(SEQ, "head"),
        P(SEQ, "head"),
        P(SEQ, "head"),
        P("head"),
        P(),
        P(None, SEQ, "head"),
        P(None, SEQ, "head"),
        P(None, SEQ, "head"),
        P(None, SEQ, "head"),
        P(SEQ),
    )
    return jax.shard_map(
        local,
        mesh=split,
        in_specs=placed,
        out_specs=(P(SEQ, "head"), P(None, SEQ, "head")),
        check_vma=False,
    )
```
